32 devices in a mesh: dp: 8 (over z, y), fsdp: 4 (over x, core).
Axes of the slice: x: 2, y: 2, z: 4, core: 2. Of those that a mesh axis runs over, the one named last changes fastest.
Arguments:
- tokens: bfloat16 [8192, 2048], P(('dp', 'fsdp')), may hold values from -6 to 6
- cotangent: bfloat16 [8192, 2048], P(('dp', 'fsdp')), may hold values from -6 to 6
- seq_lengths: int32 [8, 4], P('dp'), may hold values from 1 to 512, as said below
- deal_order: int32 [8, 4], P('dp'), may hold values from 0 to 3, as said below
- attn_gain: bfloat16 [2048], P(('dp', 'fsdp')), may hold values from 0.099609375 to 1.8984375
- w_query: bfloat16 [2048, 1536], P(('dp', 'fsdp')), may hold values from -0.125 to 0.125
- w_key: bfloat16 [2048, 384], P(('dp', 'fsdp')), may hold values from -0.125 to 0.125
- w_value: bfloat16 [2048, 384], P(('dp', 'fsdp')), may hold values from -0.125 to 0.125
- q_gain: bfloat16 [64], replicated, may hold values from 0.796875 to 1.796875
- k_gain: bfloat16 [64], replicated, may hold values from 0.796875 to 1.796875
- w_out: bfloat16 [1536, 2048], P(('dp', 'fsdp')), may hold values from -1.25 to 1.25
- ffn_gain: bfloat16 [2048], P(('dp', 'fsdp')), may hold values from 0.099609375 to 1.8984375
- w_gate: bfloat16 [2048, 4864], P(('dp', 'fsdp')), may hold values from -0.125 to 0.125
- w_up: bfloat16 [2048, 4864], P(('dp', 'fsdp')), may hold values from -0.125 to 0.125
- w_down: bfloat16 [4864, 2048], P(('dp', 'fsdp')), may hold values from -0.078125 to 0.078125
Outputs:
- output: bfloat16 [8192, 2048], P(('dp', 'fsdp'))
- input_grad: bfloat16 [8192, 2048], P(('dp', 'fsdp'))
- attn_gain_grad: float32 [2048], P(('dp', 'fsdp'))
- w_query_grad: float32 [2048, 1536], P(('dp', 'fsdp'))
- w_key_grad: float32 [2048, 384], P(('dp', 'fsdp'))
- w_value_grad: float32 [2048, 384], P(('dp', 'fsdp'))
- q_gain_grad: float32 [64], replicated
- k_gain_grad: float32 [64], replicated
- w_out_grad: float32 [1536, 2048], P(('dp', 'fsdp'))
- ffn_gain_grad: float32 [2048], P(('dp', 'fsdp'))
- w_gate_grad: float32 [2048, 4864], P(('dp', 'fsdp'))
- w_up_grad: float32 [2048, 4864], P(('dp', 'fsdp'))
- w_down_grad: float32 [4864, 2048], P(('dp', 'fsdp'))
The draws below stay inside these ranges and needn't reach their ends.
Inputs may be any that keep to these rules, and one draw needn't show every extreme that they name: `seq_lengths`: in each group, laid out in the order that deal_order gives, the 4 sequences fill two micro-batch buffers of 512 tokens each exactly; one sequence of each group has 512 tokens. `deal_order`: each group's row is a permutation of 0 to 3.
All inputs are finite; a program needn't handle non-finite values.
Results may differ from the reference program's by a relative error of at most 0.017.
Values may be sent and summed in bfloat16 or wider, within the bound.
No kernel may reach another device: no remote copies, remote signals or barrier semaphores. Data moves between devices by JAX's collectives and lax.ppermute only.
A program may use at most 320 MiB of HBM per device.

```python
import math
import jax
import jax.numpy as jnp
from jax import lax

D = 2048
HEADS = 24
KV_HEADS = 6
HD = 64
FF = 4864
TOK_DEV = 128
MB = 2
SEQ_GROUP = 4
GROUP = 512
GROUPS = 8
TOKENS = 8192


def deal_plan(key):
    base_key = jax.random.fold_in(key, 11)
    group_keys = jax.random.split(base_key, GROUPS)

    def one_group(group_key):
        first_key, short_key, roll_key, order_key = jax.random.split(group_key, 4)
        full_first = jax.random.randint(first_key, (), 0, 2)
        shorts = jax.random.randint(short_key, (2,), 1, TOK_DEV // 2)
        middle = GROUP - shorts[0] - shorts[1]
        three = jnp.stack([shorts[0], middle, shorts[1]]).astype(jnp.int32)
        shift = jax.random.randint(roll_key, (), 0, 3)
        rolled = three[(jnp.arange(3) + shift) % 3]
        whole = jnp.full((1,), GROUP, jnp.int32)
        dealt = jnp.where(full_first == 1, jnp.concatenate([whole, rolled]), jnp.concatenate([rolled, whole]))
        slots = jax.random.permutation(order_key, SEQ_GROUP).astype(jnp.int32)
        given = jnp.sum(jnp.where(slots[:, None] == jnp.arange(SEQ_GROUP)[None, :], dealt[:, None], 0), axis=0)
        return (given.astype(jnp.int32), slots)
    return jax.vmap(one_group)(group_keys)


def draw_seq_lengths(key, part):
    return deal_plan(key)[0]


def draw_deal_order(key, part):
    return deal_plan(key)[1]


def with_spikes(result, key, source, target, shards_of, factor):
    def block_of(axis_at):
        return (jnp.arange(result.shape[axis_at]) // (result.shape[axis_at] // shards_of)).reshape((-1,) + (1,) * (result.ndim - 1 - axis_at))

    near = jax.random.permutation(key, shards_of)[block_of(target)]
    other_side = (block_of(target) + shards_of // 2) % shards_of
    return jnp.where((block_of(source) == near) | (block_of(source) == other_side), factor * result, result)


def shard_levels(rng, dims, cuts, low, top_value):
    def one(position, parts):
        heights = jax.random.uniform(jax.random.fold_in(jax.random.fold_in(rng, 6), position), (parts,), jnp.float32, low / len(cuts), top_value / len(cuts))
        return jnp.repeat(jnp.exp(heights), dims[position] // parts).reshape((-1,) + (1,) * (len(dims) - position - 1))

    factor_of = one(*cuts[0])
    for cut in cuts[1:]:
        factor_of = factor_of * one(*cut)
    return factor_of


def scatter_about(key, extent, deviation, reach, cuts=(), kind=jnp.bfloat16):
    loudness = shard_levels(key, extent, cuts, -0.22, 0.18) if cuts else 1.0
    drawn = jax.random.normal(key, extent, jnp.float32) * deviation * loudness
    return jnp.minimum(jnp.maximum(drawn, -reach), reach).astype(kind)


def heavy_noise(stream_key, extent, spread, reach, cuts, heavy, kind=jnp.bfloat16):
    array = spread * jax.random.normal(stream_key, extent, jnp.float32)
    if cuts:
        array = array * shard_levels(stream_key, extent, cuts, -0.22, 0.18)
    return jnp.clip(with_spikes(array, jax.random.fold_in(stream_key, 3), *heavy), -reach, reach).astype(kind)


def setup_inputs(seed: int = 0) -> dict:
    streams_of = jax.random.split(jax.random.key(seed), 16)
    tokens = heavy_noise(streams_of[0], (TOKENS, D), 1.0, 6.0, ((0, 32),), (0, 1, 32, 2.75))
    cotangent = scatter_about(streams_of[1], (TOKENS, D), 1.0, 6.0, ((0, 32),))
    seq_lengths = draw_seq_lengths(jax.random.fold_in(streams_of[15], 71), 0)
    deal_order = draw_deal_order(jax.random.fold_in(streams_of[15], 71), 0)
    attn_gain = jnp.clip(1.0 + 0.18 * jax.random.normal(streams_of[4], (D,), jnp.float32), 0.099609375, 1.8984375).astype(jnp.bfloat16)
    w_query = scatter_about(streams_of[5], (D, HEADS * HD), D ** -0.5, 0.125, ((0, 32),))
    w_key = scatter_about(streams_of[6], (D, KV_HEADS * HD), D ** -0.5, 0.125, ((0, 32),))
    w_value = scatter_about(streams_of[7], (D, KV_HEADS * HD), D ** -0.5, 0.125, ((0, 32),))
    q_gain = jnp.clip(jax.random.uniform(streams_of[8], (HD,), jnp.float32, 0.796875, 1.796875), 0.796875, 1.796875).astype(jnp.bfloat16)
    k_gain = jnp.clip(jax.random.uniform(streams_of[9], (HD,), jnp.float32, 0.796875, 1.796875), 0.796875, 1.796875).astype(jnp.bfloat16)
    w_out = scatter_about(streams_of[10], (HEADS * HD, D), (HEADS * HD // 64) ** -0.5, 1.25, ((0, 32),))
    ffn_gain = jnp.clip(1.0 + 0.18 * jax.random.normal(streams_of[11], (D,), jnp.float32), 0.099609375, 1.8984375).astype(jnp.bfloat16)
    w_gate = scatter_about(streams_of[12], (D, FF), D ** -0.5, 0.125, ((0, 32),))
    w_up = scatter_about(streams_of[13], (D, FF), D ** -0.5, 0.125, ((0, 32),))
    w_down = scatter_about(streams_of[14], (FF, D), FF ** -0.5, 0.078125, ((0, 32),))
    return dict(tokens=tokens, cotangent=cotangent, seq_lengths=seq_lengths, deal_order=deal_order, attn_gain=attn_gain, w_query=w_query, w_key=w_key, w_value=w_value, q_gain=q_gain, k_gain=k_gain, w_out=w_out, ffn_gain=ffn_gain, w_gate=w_gate, w_up=w_up, w_down=w_down)


EPSILON = 1e-06
MASKED = -1e+30
PRECISE = lax.Precision.HIGHEST

@jax.custom_vjp
def low(v):
    return lax.optimization_barrier(v.astype(jnp.bfloat16)).astype(jnp.float32)

@jax.custom_vjp
def low_back(v):
    return v

def low_keep(v):
    return (low(v), None)

def low_pass(kept, grad):
    return (grad,)

def back_keep(v):
    return (v, None)

def back_low(kept, grad):
    return (low(grad),)
low.defvjp(low_keep, low_pass)
low_back.defvjp(back_keep, back_low)

def rms_scale(values, gain_row):
    inverse = lax.rsqrt(lax.optimization_barrier(jnp.mean(values * values, axis=-1, keepdims=True)) + EPSILON)
    return values * inverse * gain_row

def rotary(places, head_size):
    halfway = head_size // 2
    frequency = 10000.0 ** (-2.0 * jnp.arange(halfway, dtype=jnp.float32) / head_size)
    angles = places.astype(jnp.float32)[:, None] * frequency[None, :]
    return (jnp.cos(angles), jnp.sin(angles))

def head_part(pre_values, gain_row, cosine, sine_table, head_count):
    row_count = pre_values.shape[0]
    split_heads = pre_values.reshape(row_count, head_count, -1)
    scaled = split_heads * lax.rsqrt(lax.optimization_barrier(jnp.mean(split_heads * split_heads, axis=-1, keepdims=True)) + EPSILON) * gain_row
    halfway = scaled.shape[-1] // 2
    leading = scaled[..., :halfway]
    trailing = scaled[..., halfway:]
    cos_rows = cosine[:, None, :]
    sin_rows = sine_table[:, None, :]
    turned = jnp.concatenate([leading * cos_rows - trailing * sin_rows, trailing * cos_rows + leading * sin_rows], axis=-1)
    return turned.reshape(row_count, -1)

def dense(left, right):
    return jnp.dot(left, right, precision=PRECISE)

def block(inputs, segments, places, weight_set):
    attn_gain, w_query, w_key, w_value, q_gain, k_gain, w_out, ffn_gain, w_gate, w_up, w_down = weight_set
    row_count = inputs.shape[0]
    repeat = HEADS // KV_HEADS
    normed = low(rms_scale(inputs, attn_gain))
    query_pre = low_back(dense(normed, w_query))
    key_pre = low_back(dense(normed, w_key))
    value_low = low(low_back(dense(normed, w_value)))
    cosine, sine_table = rotary(places, HD)
    queries = low(head_part(query_pre, q_gain, cosine, sine_table, HEADS)).reshape(row_count, KV_HEADS, repeat, HD)
    keys_low = low(head_part(key_pre, k_gain, cosine, sine_table, KV_HEADS)).reshape(row_count, KV_HEADS, HD)
    value_heads = value_low.reshape(row_count, KV_HEADS, HD)
    raw_scores = jnp.einsum('tkrd,skd->krts', queries, keys_low, precision=PRECISE) * (1.0 / math.sqrt(HD))
    scores = low_back(raw_scores)
    allowed = (segments[:, None] == segments[None, :]) & (places[None, :] <= places[:, None])
    scores = jnp.where(allowed, scores, MASKED)
    highest = lax.optimization_barrier(jnp.max(scores, axis=-1, keepdims=True))
    log_total = highest + jnp.log(lax.optimization_barrier(jnp.sum(jnp.exp(scores - highest), axis=-1, keepdims=True)))
    attn_low = low(jnp.exp(scores - log_total))
    mixed = jnp.einsum('krts,skd->tkrd', attn_low, value_heads, precision=PRECISE).reshape(row_count, HEADS * HD)
    mixed = low(low_back(mixed))
    hidden = inputs + low_back(dense(mixed, w_out))
    ffn_low = low(rms_scale(hidden, ffn_gain))
    gate_values = low_back(dense(ffn_low, w_gate))
    up_values = low_back(dense(ffn_low, w_up))
    act_low = low(jax.nn.silu(gate_values) * up_values)
    return hidden + low_back(dense(act_low, w_down))

def plan(seq_lengths, deal_order):
    slot_ids = jnp.arange(SEQ_GROUP, dtype=jnp.int32)
    picked = deal_order[:, :, None] == slot_ids[None, None, :]
    dealt_len = lax.optimization_barrier(jnp.sum(jnp.where(picked, seq_lengths[:, None, :], 0), axis=2)).astype(jnp.int32)
    given_start = (jnp.cumsum(seq_lengths, axis=1) - seq_lengths).astype(jnp.int32)
    dealt_start = (jnp.cumsum(dealt_len, axis=1) - dealt_len).astype(jnp.int32)
    source_start = jnp.take_along_axis(given_start, deal_order, axis=1)
    wanted = jnp.arange(MB * GROUP, dtype=jnp.int32)
    sequence = (lax.optimization_barrier(jnp.sum((dealt_start[:, None, :] <= wanted[None, :, None]).astype(jnp.int32), axis=2)) - 1).astype(jnp.int32)
    places = (wanted[None, :] - jnp.take_along_axis(dealt_start, sequence, axis=1)).astype(jnp.int32)
    group_base = (jnp.arange(GROUPS, dtype=jnp.int32) * (MB * GROUP))[:, None]
    sources = (jnp.take_along_axis(source_start, sequence, axis=1) + places + group_base).astype(jnp.int32)
    return (sources, sequence, places)

def reference(tokens, cotangent, seq_lengths, deal_order, attn_gain, w_query, w_key, w_value, q_gain, k_gain, w_out, ffn_gain, w_gate, w_up, w_down):
    sources, sequence, places = plan(seq_lengths, deal_order)
    flat_sources = sources.reshape(-1)
    dealt_inputs = jnp.take(tokens.astype(jnp.float32), flat_sources, axis=0).reshape(GROUPS * MB, GROUP, D)
    dealt_upstream = jnp.take(cotangent.astype(jnp.float32), flat_sources, axis=0).reshape(GROUPS * MB, GROUP, D)
    seg_blocks = sequence.reshape(GROUPS * MB, GROUP)
    place_blocks = places.reshape(GROUPS * MB, GROUP)
    weight_set = tuple((weight_arg.astype(jnp.float32) for weight_arg in (attn_gain, w_query, w_key, w_value, q_gain, k_gain, w_out, ffn_gain, w_gate, w_up, w_down)))

    def forward(inputs, weights_now):

        def one_buffer(operands):
            return jax.checkpoint(block)(operands[0], operands[1], operands[2], weights_now)
        return lax.map(one_buffer, (inputs, seg_blocks, place_blocks))
    outputs, pullback = jax.vjp(forward, dealt_inputs, weight_set)
    input_grads, grads = pullback(dealt_upstream)
    output = jnp.zeros((TOKENS, D), jnp.float32).at[flat_sources].set(outputs.reshape(-1, D)).astype(jnp.bfloat16)
    input_grad = jnp.zeros((TOKENS, D), jnp.float32).at[flat_sources].set(input_grads.reshape(-1, D)).astype(jnp.bfloat16)
    return (output, input_grad, grads[0], grads[1], grads[2], grads[3], grads[4], grads[5], grads[6], grads[7], grads[8], grads[9], grads[10])
```

```python
import functools
import math

import jax
import jax.numpy as jnp
from jax import lax
from jax.experimental import pallas as pl
from jax.experimental.pallas import tpu as pltpu
from jax.sharding import PartitionSpec as P

HEADS = 24
KV_HEADS = 6
HD = 64
EPSILON = 1e-06
MASKED = -1e30
LANES = 128
BOTH = ("dp", "fsdp")
F32 = jnp.float32
BF16 = jnp.bfloat16
VMEM_LIMIT = 48 * 1024 * 1024


def product(left, right):
    return jnp.dot(left, right, preferred_element_type=F32)


def right_transposed(left, right):
    return lax.dot_general(left, right, (((1,), (1,)), ((), ())), preferred_element_type=F32)


def left_transposed(left, right):
    return lax.dot_general(left, right, (((0,), (0,)), ((), ())), preferred_element_type=F32)


def half_sums(values):
    rows = lax.broadcasted_iota(jnp.int32, (LANES, LANES), 0) // HD
    cols = lax.broadcasted_iota(jnp.int32, (LANES, LANES), 1) // HD
    same = (rows == cols).astype(F32)
    return jnp.dot(values, same, precision=lax.Precision.HIGHEST, preferred_element_type=F32)


def swapped_halves(values):
    lane = lax.broadcasted_iota(jnp.int32, values.shape, 1) % HD
    return jnp.where(
        lane < HD // 2, pltpu.roll(values, LANES - HD // 2, 1), pltpu.roll(values, HD // 2, 1)
    )


def head_prep_kernel(pre_ref, cos_ref, sin_ref, gain_ref, q_ref, kv_ref):
    q_blocks = HEADS * HD // LANES
    k_blocks = KV_HEADS * HD // LANES
    cosine, sine = cos_ref[...], sin_ref[...]
    for block in range(q_blocks + k_blocks):
        at = pl.ds(block * LANES, LANES)
        u = pre_ref[:, at]
        n = u * lax.rsqrt(half_sums(u * u) / HD + EPSILON) * gain_ref[:1, at]
        turned = n * cosine + swapped_halves(n) * sine
        if block < q_blocks:
            q_ref[:, at] = turned.astype(BF16)
        else:
            kv_ref[0, :, pl.ds((block - q_blocks) * LANES, LANES)] = turned.astype(BF16)
    v_at = (q_blocks + k_blocks) * LANES
    kv_ref[1] = pre_ref[:, v_at : v_at + k_blocks * LANES].astype(BF16)


def head_prep(pre, cosine, sine, gains):
    rows = pre.shape[0]
    return pl.pallas_call(
        head_prep_kernel,
        out_shape=(
            jax.ShapeDtypeStruct((rows, HEADS * HD), BF16),
            jax.ShapeDtypeStruct((2, rows, KV_HEADS * HD), BF16),
        ),
        compiler_params=pltpu.CompilerParams(vmem_limit_bytes=VMEM_LIMIT),
        name="head_prep",
    )(pre, cosine, sine, gains)


def head_back_kernel(
    gq_ref, gkv_ref, one_ref, two_ref, pre_ref, cos_ref, sin_ref, gain_ref, out_ref, sums_ref
):
    q_blocks = HEADS * HD // LANES
    k_blocks = KV_HEADS * HD // LANES
    cosine, sine = cos_ref[...], sin_ref[...]
    sums_ref[...] = jnp.zeros_like(sums_ref)
    for block in range(q_blocks + k_blocks):
        at = pl.ds(block * LANES, LANES)
        if block < q_blocks:
            g = gq_ref[:, at]
        else:
            k_at = pl.ds((block - q_blocks) * LANES, LANES)
            g = gkv_ref[0, :, k_at] + one_ref[0, :, k_at].astype(F32) + two_ref[0, :, k_at].astype(F32)
        g = g * cosine - swapped_halves(g) * sine
        u = pre_ref[:, at]
        inverse = lax.rsqrt(half_sums(u * u) / HD + EPSILON)
        unit = u * inverse
        row = 0 if block < q_blocks else 1
        sums_ref[row : row + 1, :] += jnp.sum(unit * g, axis=0, keepdims=True)
        e = g * gain_ref[:1, at]
        out_ref[:, at] = (inverse * (e - unit * (half_sums(e * unit) / HD))).astype(BF16)
    v_at = (q_blocks + k_blocks) * LANES
    width = k_blocks * LANES
    out_ref[:, v_at : v_at + width] = (
        gkv_ref[1] + one_ref[1].astype(F32) + two_ref[1].astype(F32)
    ).astype(BF16)
    tail = out_ref.shape[1] - v_at - width
    out_ref[:, v_at + width :] = jnp.zeros((out_ref.shape[0], tail), BF16)


def head_back(gq, gkv, one, two, pre, cosine, sine, gains):
    rows, width = pre.shape
    return pl.pallas_call(
        head_back_kernel,
        out_shape=(
            jax.ShapeDtypeStruct((rows, width), BF16),
            jax.ShapeDtypeStruct((8, LANES), F32),
        ),
        compiler_params=pltpu.CompilerParams(vmem_limit_bytes=VMEM_LIMIT),
        name="head_back",
    )(gq, gkv, one, two, pre, cosine, sine, gains)


def stacked_heads(ref, pair, repeat):
    return jnp.concatenate(
        [ref[:, pl.ds((pair * repeat + h) * HD, HD)] for h in range(repeat)], axis=0
    )


def window_probs(q4, keys, rel, repeat):
    rows, span = rel.shape[0], keys.shape[0]
    scores = right_transposed(q4, keys).reshape(repeat, rows, span)
    key_at = lax.broadcasted_iota(jnp.int32, (rows, span), 1) - (span - rows)
    row_at = lax.broadcasted_iota(jnp.int32, (rows, span), 0)
    allowed = (key_at <= row_at) & (key_at >= rel)
    scores = jnp.where(allowed[None], scores, MASKED)
    top = jnp.max(scores, axis=-1, keepdims=True)
    raised = jnp.exp(scores - top)
    return raised * (1.0 / jnp.sum(raised, axis=-1, keepdims=True))


def attend_kernel(q_ref, two_ref, one_ref, kv_ref, rel_ref, out_ref):
    repeat = HEADS // KV_HEADS
    rows = q_ref.shape[0]
    rel = rel_ref[:, :1]
    keys = jnp.concatenate([two_ref[0], one_ref[0], kv_ref[0]], axis=0)
    vals = jnp.concatenate([two_ref[1], one_ref[1], kv_ref[1]], axis=0)
    for pair in range(2):
        part = slice(pair * HD, (pair + 1) * HD)
        q4 = stacked_heads(q_ref, pair, repeat)
        probs = window_probs(q4, keys[:, part], rel, repeat)
        low = probs.astype(BF16).reshape(repeat * rows, -1)
        mixed = product(low, vals[:, part])
        for h in range(repeat):
            out_ref[:, pl.ds((pair * repeat + h) * HD, HD)] = mixed[
                h * rows : (h + 1) * rows
            ].astype(BF16)


def attend_specs(rows):
    q_spec = pl.BlockSpec((rows, HEADS * HD // 3), lambda g: (0, g))
    kv_spec = pl.BlockSpec((2, rows, LANES), lambda g: (0, 0, g))
    rel_spec = pl.BlockSpec((rows, LANES), lambda g: (0, 0))
    return q_spec, kv_spec, rel_spec


def attend(q, two, one, kv, rel):
    rows = q.shape[0]
    q_spec, kv_spec, rel_spec = attend_specs(rows)
    return pl.pallas_call(
        attend_kernel,
        grid=(3,),
        in_specs=[q_spec, kv_spec, kv_spec, kv_spec, rel_spec],
        out_specs=q_spec,
        out_shape=jax.ShapeDtypeStruct((rows, HEADS * HD), BF16),
        compiler_params=pltpu.CompilerParams(vmem_limit_bytes=VMEM_LIMIT),
        name="attend",
    )(q, two, one, kv, rel)


def attend_back_kernel(
    q_ref, two_ref, one_ref, kv_ref, rel_ref, gm_ref, gq_ref, gtwo_ref, gone_ref, gkv_ref
):
    repeat = HEADS // KV_HEADS
    rows = q_ref.shape[0]
    rel = rel_ref[:, :1]
    keys = jnp.concatenate([two_ref[0], one_ref[0], kv_ref[0]], axis=0)
    vals = jnp.concatenate([two_ref[1], one_ref[1], kv_ref[1]], axis=0)
    key_grads, val_grads = [], []
    for pair in range(2):
        part = slice(pair * HD, (pair + 1) * HD)
        q4 = stacked_heads(q_ref, pair, repeat)
        gm4 = stacked_heads(gm_ref, pair, repeat)
        probs = window_probs(q4, keys[:, part], rel, repeat)
        grad_probs = right_transposed(gm4, vals[:, part]).reshape(probs.shape)
        weighted = jnp.sum(probs * grad_probs, axis=-1, keepdims=True)
        span = probs.shape[-1]
        gs = (probs * (grad_probs - weighted)).astype(BF16).reshape(repeat * rows, span)
        low = probs.astype(BF16).reshape(repeat * rows, span)
        gq = product(gs, keys[:, part]) * (1.0 / math.sqrt(HD))
        for h in range(repeat):
            gq_ref[:, pl.ds((pair * repeat + h) * HD, HD)] = gq[h * rows : (h + 1) * rows]
        key_grads.append(product(q4.T, gs).T)
        val_grads.append(product(gm4.T, low).T)
    for at, parts in ((0, key_grads), (1, val_grads)):
        both = jnp.concatenate(parts, axis=1)
        gtwo_ref[at] = both[:rows].astype(gtwo_ref.dtype)
        gone_ref[at] = both[rows : 2 * rows].astype(gone_ref.dtype)
        gkv_ref[at] = both[2 * rows :]


def attend_back(q, two, one, kv, rel, gm):
    rows = q.shape[0]
    q_spec, kv_spec, rel_spec = attend_specs(rows)
    return pl.pallas_call(
        attend_back_kernel,
        grid=(3,),
        in_specs=[q_spec, kv_spec, kv_spec, kv_spec, rel_spec, q_spec],
        out_specs=(q_spec, kv_spec, kv_spec, kv_spec),
        out_shape=(
            jax.ShapeDtypeStruct((rows, HEADS * HD), F32),
            jax.ShapeDtypeStruct((2, rows, KV_HEADS * HD), BF16),
            jax.ShapeDtypeStruct((2, rows, KV_HEADS * HD), BF16),
            jax.ShapeDtypeStruct((2, rows, KV_HEADS * HD), F32),
        ),
        compiler_params=pltpu.CompilerParams(vmem_limit_bytes=VMEM_LIMIT),
        name="attend_back",
    )(q, two, one, kv, rel, gm)


class Ring:
    def __init__(self, depth):
        self.depth = depth
        self.arrived = []

    def send(self, value, axis, pairs):
        if len(self.arrived) >= self.depth:
            value, _ = lax.optimization_barrier((value, self.arrived[-self.depth]))
        out = lax.ppermute(value, axis, pairs)
        self.arrived.append(out)
        return out


def swap_pairs(size, bit):
    return [(i, i ^ bit) for i in range(size)]


def far_pairs(size, shift):
    far = size // 2
    return [(i, (i // 2 + shift) % far * 2 + i % 2) for i in range(size)]


def far_order(far):
    order = []
    for step in range(1, far // 2 + 1):
        order.append(step)
        if far - step != step:
            order.append(far - step)
    return order


def gather_dp(piece, size, ring):
    mine = lax.axis_index("dp")
    far, near = mine // 2, mine % 2
    held = [(0, piece)]
    for shift in far_order(size // 2):
        held.append((shift, ring.send(piece, "dp", far_pairs(size, shift))))
    out = jnp.zeros((size,) + piece.shape, piece.dtype)
    zero = jnp.int32(0)
    for shift, value in held:
        other = lax.ppermute(value, "dp", swap_pairs(size, 1))
        base = (far + size // 2 - shift) % (size // 2) * 2
        out = lax.dynamic_update_slice(out, value[None], (base + near, zero, zero))
        out = lax.dynamic_update_slice(out, other[None], (base + 1 - near, zero, zero))
    return out


def scatter_dp(terms, size, ring):
    mine = lax.axis_index("dp")
    far, near = mine // 2, mine % 2
    total = None
    for shift in far_order(size // 2) + [0]:
        base = (far + shift) % (size // 2) * 2
        other = lax.dynamic_index_in_dim(terms, base + 1 - near, 0, keepdims=False)
        own = lax.dynamic_index_in_dim(terms, base + near, 0, keepdims=False)
        got = lax.ppermute(other, "dp", swap_pairs(size, 1))
        pair = own.astype(F32) + got.astype(F32)
        if shift:
            pair = ring.send(pair.astype(BF16), "dp", far_pairs(size, shift)).astype(F32)
        total = pair if total is None else total + pair
    return total


def gather_rows(rows):
    core, chip = swap_pairs(4, 1), swap_pairs(4, 2)
    near = lax.ppermute(rows, "fsdp", core)
    far = lax.ppermute(rows, "fsdp", chip)
    both = lax.ppermute(far, "fsdp", core)
    return jnp.concatenate([rows, near, far, both], axis=0)


def scatter_rows(partial):
    rows = partial.shape[0] // 4
    core, chip = swap_pairs(4, 1), swap_pairs(4, 2)
    parts = partial.reshape(4, rows, -1)
    far = lax.ppermute(parts[3].astype(BF16), "fsdp", core)
    far = parts[2] + far.astype(F32)
    far = lax.ppermute(far.astype(BF16), "fsdp", chip)
    near = lax.ppermute(parts[1].astype(BF16), "fsdp", core)
    return parts[0] + near.astype(F32) + far.astype(F32)


def sum_all(value, dp_size):
    for axis, size in (("fsdp", 4), ("dp", dp_size)):
        bit = 1
        while bit < size:
            value = value + lax.ppermute(value, axis, swap_pairs(size, bit))
            bit *= 2
    return value


def local(
    tokens,
    cotangent,
    seq_lengths,
    deal_order,
    attn_gain,
    w_query,
    w_key,
    w_value,
    q_gain,
    k_gain,
    w_out,
    ffn_gain,
    w_gate,
    w_up,
    w_down,
):
    rows, width = tokens.shape
    dp_size = lax.axis_size("dp")
    shard = w_gate.shape[0]
    ff_rows = w_down.shape[0]
    member = lax.axis_index("fsdp")

    lengths = seq_lengths[0]
    slots = jnp.arange(lengths.shape[0], dtype=jnp.int32)
    starts = jnp.sum(jnp.where(slots[None, :] < slots[:, None], lengths[None, :], 0), axis=1)
    row_ids = member * rows + jnp.arange(rows, dtype=jnp.int32)
    begun = starts[None, :] <= row_ids[:, None]
    row_start = jnp.max(jnp.where(begun, starts[None, :], 0), axis=1)
    place = row_ids - row_start
    rel = jnp.broadcast_to((row_start - member * rows)[:, None], (rows, LANES))
    frequency = 10000.0 ** (-2.0 * jnp.arange(HD // 2, dtype=F32) / HD)
    angles = place.astype(F32)[:, None] * frequency[None, :]
    cosine, sine = jnp.cos(angles), jnp.sin(angles)
    cosine = jnp.concatenate([cosine] * 4, axis=1)
    sine = jnp.concatenate([-sine, sine, -sine, sine], axis=1)
    head_gains = jnp.concatenate([jnp.tile(q_gain, HEADS), jnp.tile(k_gain, KV_HEADS)])
    head_gains = jnp.broadcast_to(head_gains.astype(F32)[None, :], (8, head_gains.shape[0]))

    gain_columns = jnp.pad(
        jnp.stack([attn_gain, ffn_gain], axis=1), ((0, 0), (0, LANES - 2))
    )
    w_qkv = jnp.concatenate([w_query, w_key, w_value, gain_columns], axis=1)
    full_qkv = lax.all_gather(w_qkv, BOTH, axis=0, tiled=True)
    full_out = lax.all_gather(w_out, BOTH, axis=0, tiled=True)

    def quarters(weight):
        split = weight.reshape(shard, dp_size, 4, ff_rows)
        return jnp.moveaxis(split, 2, 0).reshape(4, shard, dp_size * ff_rows)

    ring = Ring(2)
    gate_piece = lax.all_to_all(quarters(w_gate), "fsdp", 0, 0, tiled=True)
    up_piece = lax.all_to_all(quarters(w_up), "fsdp", 0, 0, tiled=True)
    ff_width = dp_size * ff_rows
    my_gate = gather_dp(gate_piece.reshape(4 * shard, ff_width), dp_size, ring)
    my_up = gather_dp(up_piece.reshape(4 * shard, ff_width), dp_size, ring)
    my_down = gather_dp(w_down, dp_size, ring)
    my_gate = my_gate.reshape(width, ff_width)
    my_up = my_up.reshape(width, ff_width)
    my_down = my_down.reshape(ff_width, width)

    gain_table = full_qkv[:, full_qkv.shape[1] - LANES :]
    pick = (
        lax.broadcasted_iota(jnp.int32, (8, LANES), 0)
        == lax.broadcasted_iota(jnp.int32, (8, LANES), 1)
    ).astype(BF16)
    gain_rows = right_transposed(pick, gain_table)
    attn_row, ffn_row = gain_rows[0:1], gain_rows[1:2]
    x = tokens.astype(F32)
    x_inverse = lax.rsqrt(jnp.mean(x * x, axis=-1, keepdims=True) + EPSILON)
    normed = (x * x_inverse * attn_row).astype(BF16)
    pre = product(normed, full_qkv)
    queries, kv = head_prep(pre, cosine, sine, head_gains)
    queries = queries * jnp.bfloat16(1.0 / math.sqrt(HD))
    ahead_one = [(i, i + 1) for i in range(3)]
    ahead_two = [(i, i + 2) for i in range(2)]
    kv_one = lax.ppermute(kv, "fsdp", ahead_one)
    kv_two = lax.ppermute(kv, "fsdp", ahead_two)
    mixed = attend(queries, kv_two, kv_one, kv, rel)
    hidden = x + product(mixed, full_out)
    h_inverse = lax.rsqrt(jnp.mean(hidden * hidden, axis=-1, keepdims=True) + EPSILON)
    ffn_mine = (hidden * h_inverse * ffn_row).astype(BF16)

    upstream = gather_rows(cotangent)
    ffn_low = gather_rows(ffn_mine)
    gate = product(ffn_low, my_gate)
    up = product(ffn_low, my_up)
    sig = 1.0 / (1.0 + jnp.exp(-gate))
    silu = gate * sig
    act_low = (silu * up).astype(BF16)
    back = Ring(2)
    term_down = left_transposed(act_low, upstream).astype(BF16)
    down_grad = scatter_dp(term_down.reshape(dp_size, ff_rows, width), dp_size, back)
    grad_act = right_transposed(upstream, my_down)
    grad_gate = (grad_act * up * sig * (1.0 + gate * (1.0 - sig))).astype(BF16)
    grad_up = (grad_act * silu).astype(BF16)
    grad_ffn = scatter_rows(right_transposed(grad_gate, my_gate) + right_transposed(grad_up, my_up))
    term_gate = left_transposed(ffn_low, grad_gate).astype(BF16)
    term_up = left_transposed(ffn_low, grad_up).astype(BF16)
    gate_sum = scatter_dp(term_gate.reshape(dp_size, 4 * shard, ff_width), dp_size, back)
    up_sum = scatter_dp(term_up.reshape(dp_size, 4 * shard, ff_width), dp_size, back)
    output = (hidden + scatter_rows(product(act_low, my_down))).astype(BF16)

    def whole_rows(total):
        sent = total.astype(BF16).reshape(4, shard, ff_width)
        got = lax.all_to_all(sent, "fsdp", 0, 0, tiled=True)
        split = jnp.moveaxis(got.reshape(4, shard, dp_size, ff_rows), 0, 2)
        return split.reshape(shard, 4 * ff_width).astype(F32)

    gate_grad = whole_rows(gate_sum)
    up_grad = whole_rows(up_sum)

    e = grad_ffn * ffn_row
    slope = jnp.mean(hidden * e, axis=-1, keepdims=True)
    grad_hidden = cotangent.astype(F32) + h_inverse * e - hidden * (h_inverse**3 * slope)
    ffn_gain_term = jnp.sum(grad_ffn * hidden * h_inverse, axis=0)
    grad_hidden_low = grad_hidden.astype(BF16)
    grad_mixed = right_transposed(grad_hidden_low, full_out).astype(BF16)
    term_out = left_transposed(mixed, grad_hidden_low).astype(BF16)
    out_grad = lax.psum_scatter(term_out, BOTH, scatter_dimension=0, tiled=True).astype(F32)
    gq, gkv_two, gkv_one, gkv = attend_back(queries, kv_two, kv_one, kv, rel, grad_mixed)
    got_one = lax.ppermute(gkv_one, "fsdp", [(b, a) for a, b in ahead_one])
    got_two = lax.ppermute(gkv_two, "fsdp", [(b, a) for a, b in ahead_two])
    grad_pre, head_sums = head_back(gq, gkv, got_one, got_two, pre, cosine, sine, head_gains)
    term_qkv = left_transposed(normed, grad_pre).astype(BF16)
    qkv_grad = lax.psum_scatter(term_qkv, BOTH, scatter_dimension=0, tiled=True).astype(F32)
    grad_normed = right_transposed(grad_pre, full_qkv)
    e = grad_normed * attn_row
    slope = jnp.mean(x * e, axis=-1, keepdims=True)
    input_grad = grad_hidden + x_inverse * e - x * (x_inverse**3 * slope)
    attn_gain_term = jnp.sum(grad_normed * x * x_inverse, axis=0)

    small = jnp.concatenate([attn_gain_term, ffn_gain_term, head_sums.reshape(-1)])
    small = sum_all(small.reshape(-1, LANES), dp_size).reshape(-1)
    mine = (lax.axis_index("dp") * 4 + member) * shard
    attn_gain_grad = lax.dynamic_slice(small, (mine,), (shard,))
    ffn_gain_grad = lax.dynamic_slice(small, (width + mine,), (shard,))
    head_total = small[2 * width : 2 * width + 2 * LANES].reshape(2, 2, HD).sum(axis=1)

    q_end = HEADS * HD
    k_end = q_end + KV_HEADS * HD
    v_end = k_end + KV_HEADS * HD
    return (
        output,
        input_grad.astype(BF16),
        attn_gain_grad,
        qkv_grad[:, :q_end],
        qkv_grad[:, q_end:k_end],
        qkv_grad[:, k_end:v_end],
        head_total[0],
        head_total[1],
        out_grad,
        ffn_gain_grad,
        gate_grad,
        up_grad,
        down_grad,
    )


def solution(mesh):
    rows = P(BOTH, None)
    vector = P(BOTH)
    in_specs = (
        rows,
        rows,
        P("dp", None),
        P("dp", None),
        vector,
        rows,
        rows,
        rows,
        P(),
        P(),
        rows,
        vector,
        rows,
        rows,
        rows,
    )
    out_specs = (rows, rows, vector, rows, rows, rows, P(), P(), rows, vector, rows, rows, rows)
    return jax.shard_map(local, mesh=mesh, in_specs=in_specs, out_specs=out_specs, check_vma=False)
```

```python
import functools
import math

import jax
import jax.numpy as jnp
from jax import lax
from jax.experimental import pallas as pl
from jax.experimental.pallas import tpu as pltpu
from jax.sharding import PartitionSpec as P

HEADS = 24
KV_HEADS = 6
HD = 64
EPSILON = 1e-06
MASKED = -1e30
LANES = 128
BOTH = ("dp", "fsdp")
F32 = jnp.float32
BF16 = jnp.bfloat16
VMEM_LIMIT = 48 * 1024 * 1024


def product(left, right):
    return jnp.dot(left, right, preferred_element_type=F32)


def right_transposed(left, right):
    return lax.dot_general(left, right, (((1,), (1,)), ((), ())), preferred_element_type=F32)


def left_transposed(left, right):
    return lax.dot_general(left, right, (((0,), (0,)), ((), ())), preferred_element_type=F32)


def half_sums(values):
    rows = lax.broadcasted_iota(jnp.int32, (LANES, LANES), 0) // HD
    cols = lax.broadcasted_iota(jnp.int32, (LANES, LANES), 1) // HD
    same = (rows == cols).astype(F32)
    return jnp.dot(values, same, precision=lax.Precision.HIGHEST, preferred_element_type=F32)


def swapped_halves(values):
    lane = lax.broadcasted_iota(jnp.int32, values.shape, 1) % HD
    return jnp.where(
        lane < HD // 2, pltpu.roll(values, LANES - HD // 2, 1), pltpu.roll(values, HD // 2, 1)
    )


def head_prep_kernel(pre_ref, cos_ref, sin_ref, gain_ref, q_ref, kv_ref):
    q_blocks = HEADS * HD // LANES
    k_blocks = KV_HEADS * HD // LANES
    cosine, sine = cos_ref[...], sin_ref[...]
    for block in range(q_blocks + k_blocks):
        at = pl.ds(block * LANES, LANES)
        u = pre_ref[:, at]
        n = u * lax.rsqrt(half_sums(u * u) / HD + EPSILON) * gain_ref[:1, at]
        turned = n * cosine + swapped_halves(n) * sine
        if block < q_blocks:
            q_ref[:, at] = (turned.astype(BF16).astype(F32) * (1.0 / math.sqrt(HD))).astype(BF16)
        else:
            kv_ref[0, :, pl.ds((block - q_blocks) * LANES, LANES)] = turned.astype(BF16)
    v_at = (q_blocks + k_blocks) * LANES
    kv_ref[1] = pre_ref[:, v_at : v_at + k_blocks * LANES].astype(BF16)


def head_prep(pre, cosine, sine, gains):
    rows = pre.shape[0]
    return pl.pallas_call(
        head_prep_kernel,
        out_shape=(
            jax.ShapeDtypeStruct((rows, HEADS * HD), BF16),
            jax.ShapeDtypeStruct((2, rows, KV_HEADS * HD), BF16),
        ),
        compiler_params=pltpu.CompilerParams(vmem_limit_bytes=VMEM_LIMIT),
        name="head_prep",
    )(pre, cosine, sine, gains)


def head_back_kernel(
    gq_ref, gkv_ref, one_ref, two_ref, pre_ref, cos_ref, sin_ref, gain_ref, out_ref, sums_ref
):
    q_blocks = HEADS * HD // LANES
    k_blocks = KV_HEADS * HD // LANES
    cosine, sine = cos_ref[...], sin_ref[...]
    sums_ref[...] = jnp.zeros_like(sums_ref)
    for block in range(q_blocks + k_blocks):
        at = pl.ds(block * LANES, LANES)
        if block < q_blocks:
            g = gq_ref[:, at]
        else:
            k_at = pl.ds((block - q_blocks) * LANES, LANES)
            g = gkv_ref[0, :, k_at] + one_ref[0, :, k_at].astype(F32) + two_ref[0, :, k_at].astype(F32)
        g = g * cosine - swapped_halves(g) * sine
        u = pre_ref[:, at]
        inverse = lax.rsqrt(half_sums(u * u) / HD + EPSILON)
        unit = u * inverse
        row = 0 if block < q_blocks else 1
        sums_ref[row : row + 1, :] += jnp.sum(unit * g, axis=0, keepdims=True)
        e = g * gain_ref[:1, at]
        out_ref[:, at] = (inverse * (e - unit * (half_sums(e * unit) / HD))).astype(BF16)
    v_at = (q_blocks + k_blocks) * LANES
    width = k_blocks * LANES
    out_ref[:, v_at : v_at + width] = (
        gkv_ref[1] + one_ref[1].astype(F32) + two_ref[1].astype(F32)
    ).astype(BF16)
    tail = out_ref.shape[1] - v_at - width
    out_ref[:, v_at + width :] = jnp.zeros((out_ref.shape[0], tail), BF16)


def head_back(gq, gkv, one, two, pre, cosine, sine, gains):
    rows, width = pre.shape
    return pl.pallas_call(
        head_back_kernel,
        out_shape=(
            jax.ShapeDtypeStruct((rows, width), BF16),
            jax.ShapeDtypeStruct((8, LANES), F32),
        ),
        compiler_params=pltpu.CompilerParams(vmem_limit_bytes=VMEM_LIMIT),
        name="head_back",
    )(gq, gkv, one, two, pre, cosine, sine, gains)


def stacked_heads(ref, pair, repeat):
    return jnp.concatenate(
        [ref[:, pl.ds((pair * repeat + h) * HD, HD)] for h in range(repeat)], axis=0
    )


def window_probs(q4, keys, rel, repeat):
    rows, span = rel.shape[0], keys.shape[0]
    scores = right_transposed(q4, keys).reshape(repeat, rows, span)
    key_at = lax.broadcasted_iota(jnp.int32, (rows, span), 1) - (span - rows)
    row_at = lax.broadcasted_iota(jnp.int32, (rows, span), 0)
    allowed = (key_at <= row_at) & (key_at >= rel)
    scores = jnp.where(allowed[None], scores, MASKED)
    top = jnp.max(scores, axis=-1, keepdims=True)
    raised = jnp.exp(scores - top)
    return raised * (1.0 / jnp.sum(raised, axis=-1, keepdims=True))


def attend_kernel(q_ref, two_ref, one_ref, kv_ref, rel_ref, out_ref):
    repeat = HEADS // KV_HEADS
    rows = q_ref.shape[0]
    rel = rel_ref[:, :1]
    keys = jnp.concatenate([two_ref[0], one_ref[0], kv_ref[0]], axis=0)
    vals = jnp.concatenate([two_ref[1], one_ref[1], kv_ref[1]], axis=0)
    for pair in range(2):
        part = slice(pair * HD, (pair + 1) * HD)
        q4 = stacked_heads(q_ref, pair, repeat)
        probs = window_probs(q4, keys[:, part], rel, repeat)
        low = probs.astype(BF16).reshape(repeat * rows, -1)
        mixed = product(low, vals[:, part])
        for h in range(repeat):
            out_ref[:, pl.ds((pair * repeat + h) * HD, HD)] = mixed[
                h * rows : (h + 1) * rows
            ].astype(BF16)


def attend_specs(rows):
    q_spec = pl.BlockSpec((rows, HEADS * HD // 3), lambda g: (0, g))
    kv_spec = pl.BlockSpec((2, rows, LANES), lambda g: (0, 0, g))
    rel_spec = pl.BlockSpec((rows, LANES), lambda g: (0, 0))
    return q_spec, kv_spec, rel_spec


def attend(q, two, one, kv, rel):
    rows = q.shape[0]
    q_spec, kv_spec, rel_spec = attend_specs(rows)
    return pl.pallas_call(
        attend_kernel,
        grid=(3,),
        in_specs=[q_spec, kv_spec, kv_spec, kv_spec, rel_spec],
        out_specs=q_spec,
        out_shape=jax.ShapeDtypeStruct((rows, HEADS * HD), BF16),
        compiler_params=pltpu.CompilerParams(vmem_limit_bytes=VMEM_LIMIT),
        name="attend",
    )(q, two, one, kv, rel)


def attend_back_kernel(
    q_ref, two_ref, one_ref, kv_ref, rel_ref, gm_ref, gq_ref, gtwo_ref, gone_ref, gkv_ref
):
    repeat = HEADS // KV_HEADS
    rows = q_ref.shape[0]
    rel = rel_ref[:, :1]
    keys = jnp.concatenate([two_ref[0], one_ref[0], kv_ref[0]], axis=0)
    vals = jnp.concatenate([two_ref[1], one_ref[1], kv_ref[1]], axis=0)
    key_grads, val_grads = [], []
    for pair in range(2):
        part = slice(pair * HD, (pair + 1) * HD)
        q4 = stacked_heads(q_ref, pair, repeat)
        gm4 = stacked_heads(gm_ref, pair, repeat)
        probs = window_probs(q4, keys[:, part], rel, repeat)
        grad_probs = right_transposed(gm4, vals[:, part]).reshape(probs.shape)
        weighted = jnp.sum(probs * grad_probs, axis=-1, keepdims=True)
        span = probs.shape[-1]
        gs = (probs * (grad_probs - weighted)).astype(BF16).reshape(repeat * rows, span)
        low = probs.astype(BF16).reshape(repeat * rows, span)
        gq = product(gs, keys[:, part]) * (1.0 / math.sqrt(HD))
        for h in range(repeat):
            gq_ref[:, pl.ds((pair * repeat + h) * HD, HD)] = gq[h * rows : (h + 1) * rows]
        key_grads.append(product(q4.T, gs).T)
        val_grads.append(product(gm4.T, low).T)
    for at, parts in ((0, key_grads), (1, val_grads)):
        both = jnp.concatenate(parts, axis=1)
        gtwo_ref[at] = both[:rows].astype(gtwo_ref.dtype)
        gone_ref[at] = both[rows : 2 * rows].astype(gone_ref.dtype)
        gkv_ref[at] = both[2 * rows :]


def attend_back(q, two, one, kv, rel, gm):
    rows = q.shape[0]
    q_spec, kv_spec, rel_spec = attend_specs(rows)
    return pl.pallas_call(
        attend_back_kernel,
        grid=(3,),
        in_specs=[q_spec, kv_spec, kv_spec, kv_spec, rel_spec, q_spec],
        out_specs=(q_spec, kv_spec, kv_spec, kv_spec),
        out_shape=(
            jax.ShapeDtypeStruct((rows, HEADS * HD), F32),
            jax.ShapeDtypeStruct((2, rows, KV_HEADS * HD), BF16),
            jax.ShapeDtypeStruct((2, rows, KV_HEADS * HD), BF16),
            jax.ShapeDtypeStruct((2, rows, KV_HEADS * HD), F32),
        ),
        compiler_params=pltpu.CompilerParams(vmem_limit_bytes=VMEM_LIMIT),
        name="attend_back",
    )(q, two, one, kv, rel, gm)


def feed_kernel(x_ref, gate_ref, up_ref, act_ref, gate_slope_ref, up_slope_ref):
    x = x_ref[...]
    gate, up = product(x, gate_ref[...]), product(x, up_ref[...])
    sig = 1.0 / (1.0 + jnp.exp(-gate))
    silu = gate * sig
    act_ref[...] = (silu * up).astype(BF16)
    gate_slope_ref[...] = (up * sig * (1.0 + gate * (1.0 - sig))).astype(BF16)
    up_slope_ref[...] = silu.astype(BF16)


def feed(x, both):
    rows, width = x.shape
    units = both.shape[1] // 2
    tile = 2 * LANES
    steps = units // tile
    out = pl.BlockSpec((rows, tile), lambda j: (0, j))
    return pl.pallas_call(
        feed_kernel,
        grid=(steps,),
        in_specs=[
            pl.BlockSpec((rows, width), lambda j: (0, 0)),
            pl.BlockSpec((width, tile), lambda j: (0, j)),
            pl.BlockSpec((width, tile), lambda j: (0, j + steps)),
        ],
        out_specs=[out] * 3,
        out_shape=[jax.ShapeDtypeStruct((rows, units), BF16)] * 3,
        compiler_params=pltpu.CompilerParams(vmem_limit_bytes=VMEM_LIMIT),
        cost_estimate=pl.CostEstimate(
            flops=4 * rows * width * units,
            transcendentals=rows * units,
            bytes_accessed=2 * (rows * width + 2 * width * units + 3 * rows * units),
        ),
        name="feed",
    )(x, both, both)


def feed_slopes_kernel(x_ref, down_ref, gs_ref, us_ref, gg_ref, gu_ref):
    grad_act = right_transposed(x_ref[...], down_ref[...])
    gg_ref[...] = (grad_act * gs_ref[...].astype(F32)).astype(BF16)
    gu_ref[...] = (grad_act * us_ref[...].astype(F32)).astype(BF16)


def feed_slopes(upstream, down, gate_slope, up_slope):
    rows, width = upstream.shape
    units = down.shape[0]
    tile = 2 * LANES
    columns = pl.BlockSpec((rows, tile), lambda j: (0, j))
    return pl.pallas_call(
        feed_slopes_kernel,
        grid=(units // tile,),
        in_specs=[
            pl.BlockSpec((rows, width), lambda j: (0, 0)),
            pl.BlockSpec((tile, width), lambda j: (j, 0)),
            columns,
            columns,
        ],
        out_specs=[columns, columns],
        out_shape=[jax.ShapeDtypeStruct((rows, units), BF16)] * 2,
        compiler_params=pltpu.CompilerParams(vmem_limit_bytes=VMEM_LIMIT),
        cost_estimate=pl.CostEstimate(
            flops=2 * rows * width * units,
            transcendentals=0,
            bytes_accessed=2 * (rows * width + width * units + 4 * rows * units),
        ),
        name="feed_slopes",
    )(upstream, down, gate_slope, up_slope)


def feed_back_kernel(gg_ref, gu_ref, both_ref, own_ref, other_ref):
    units = gg_ref.shape[1]
    lot = own_ref.shape[1]
    total = right_transposed(gg_ref[...], both_ref[:, :units]) + right_transposed(
        gu_ref[...], both_ref[:, units:]
    )
    for half in range(2):
        own_ref[half] = total[2 * half * lot : (2 * half + 1) * lot]
        other_ref[half] = total[(2 * half + 1) * lot : (2 * half + 2) * lot].astype(BF16)


def feed_back(grad_gate, grad_up, both):
    rows, units = grad_gate.shape
    width = both.shape[0]
    lot = rows // 4
    tile = 2 * LANES
    out = pl.BlockSpec((2, lot, tile), lambda j: (0, 0, j))
    return pl.pallas_call(
        feed_back_kernel,
        grid=(width // tile,),
        in_specs=[
            pl.BlockSpec((rows, units), lambda j: (0, 0)),
            pl.BlockSpec((rows, units), lambda j: (0, 0)),
            pl.BlockSpec((tile, 2 * units), lambda j: (j, 0)),
        ],
        out_specs=[out, out],
        out_shape=[
            jax.ShapeDtypeStruct((2, lot, width), F32),
            jax.ShapeDtypeStruct((2, lot, width), BF16),
        ],
        compiler_params=pltpu.CompilerParams(vmem_limit_bytes=VMEM_LIMIT),
        cost_estimate=pl.CostEstimate(
            flops=4 * rows * width * units,
            transcendentals=0,
            bytes_accessed=2 * (2 * rows * units + 2 * width * units + 2 * rows * width),
        ),
        name="feed_back",
    )(grad_gate, grad_up, both)


def lane_window(read, tiles, start):
    tile, shift = start // LANES, start % LANES
    first = read(min(max(tile, 0), tiles - 1))
    if shift == 0:
        return first
    second = read(min(max(tile + 1, 0), tiles - 1))
    lane = lax.broadcasted_iota(jnp.int32, first.shape, 1)
    return jnp.where(
        lane < LANES - shift,
        pltpu.roll(first, LANES - shift, 1),
        pltpu.roll(second, LANES - shift, 1),
    )


def lane_runs(target, runs, source_of):
    total = None
    for first, length, source in runs:
        low, high = max(first, target), min(first + length, target + LANES)
        if low >= high:
            continue
        window = source_of(source, target - first)
        lane = lax.broadcasted_iota(jnp.int32, window.shape, 1) + target
        kept = jnp.where((lane >= low) & (lane < high), window, 0.0)
        total = kept if total is None else total + kept
    return total


def quarters_kernel(dp_size, unit, block, gate_ref, up_ref, out_ref):
    units = dp_size * block
    tiles = -(-gate_ref.shape[1] // LANES)
    for at, ref in ((0, gate_ref), (units, up_ref)):
        for member in range(4):
            runs = [(d * block, unit, (4 * d + member) * unit) for d in range(dp_size)]

            def source_of(source, offset):
                read = lambda t: ref[:, t * LANES : (t + 1) * LANES].astype(F32)
                return lane_window(read, tiles, source + offset)

            for target in range(0, units, LANES):
                value = lane_runs(target, runs, source_of)
                out_ref[member, :, at + target : at + target + LANES] = value.astype(BF16)


def quarters_of(gate, up, dp_size, unit, block):
    return pl.pallas_call(
        functools.partial(quarters_kernel, dp_size, unit, block),
        out_shape=jax.ShapeDtypeStruct((4, gate.shape[0], 2 * dp_size * block), BF16),
        compiler_params=pltpu.CompilerParams(vmem_limit_bytes=VMEM_LIMIT),
        name="quarters",
    )(gate, up)


def columns_kernel(dp_size, unit, block, got_ref, out_ref):
    tiles = got_ref.shape[2] // LANES
    runs = [
        ((4 * d + member) * unit, unit, (member, d * block))
        for d in range(dp_size)
        for member in range(4)
    ]

    def source_of(source, offset):
        read = lambda t: got_ref[source[0], :, t * LANES : (t + 1) * LANES].astype(F32)
        return lane_window(read, tiles, source[1] + offset)

    for target in range(0, out_ref.shape[1], LANES):
        out_ref[:, target : target + LANES] = lane_runs(target, runs, source_of)


def columns_of(got, dp_size, unit, block):
    return pl.pallas_call(
        functools.partial(columns_kernel, dp_size, unit, block),
        out_shape=jax.ShapeDtypeStruct((got.shape[1], 4 * dp_size * unit), F32),
        compiler_params=pltpu.CompilerParams(vmem_limit_bytes=VMEM_LIMIT),
        name="columns",
    )(got)


def swap_pairs(size, bit):
    return [(i, i ^ bit) for i in range(size)]


def far_pairs(size, shift):
    far = size // 2
    return [(i, (i // 2 + shift) % far * 2 + i % 2) for i in range(size)]


def far_order(far):
    order = []
    for step in range(1, far // 2 + 1):
        order.append(step)
        if far - step != step:
            order.append(far - step)
    return order


def place_kernel(counts, slots, *refs):
    pieces, out, held, come, gone = refs[: len(counts)], *refs[len(counts) :]
    arrivals, departures = [], []
    for piece, count in zip(pieces, counts):
        for k in range(count):
            at = len(arrivals)
            arrivals.append(pltpu.make_async_copy(piece.at[k], held.at[at], come.at[at]))
            departures.append(pltpu.make_async_copy(held.at[at], out.at[slots[at]], gone.at[at]))
    for copy in arrivals:
        copy.start()
    for arrival, departure in zip(arrivals, departures):
        arrival.wait()
        departure.start()
    for copy in departures:
        copy.wait()


def place(pieces, slots):
    counts = [piece.shape[0] for piece in pieces]
    total = sum(counts)
    shape = (total,) + pieces[0].shape[1:]
    moved = 2 * math.prod(shape) * pieces[0].dtype.itemsize
    return pl.pallas_call(
        functools.partial(place_kernel, counts),
        in_specs=[pl.BlockSpec(memory_space=pltpu.SMEM)]
        + [pl.BlockSpec(memory_space=pl.ANY)] * len(pieces),
        out_specs=pl.BlockSpec(memory_space=pl.ANY),
        out_shape=jax.ShapeDtypeStruct(shape, pieces[0].dtype),
        scratch_shapes=[
            pltpu.VMEM(shape, pieces[0].dtype),
            pltpu.SemaphoreType.DMA((total,)),
            pltpu.SemaphoreType.DMA((total,)),
        ],
        compiler_params=pltpu.CompilerParams(vmem_limit_bytes=VMEM_LIMIT),
        cost_estimate=pl.CostEstimate(flops=0, transcendentals=0, bytes_accessed=moved),
        name="place",
    )(slots, *pieces)


def pick_kernel(counts, slots, source, *refs):
    outs, (held, come, gone) = refs[: len(counts)], refs[len(counts) :]
    arrivals, departures = [], []
    for out, count in zip(outs, counts):
        for k in range(count):
            at = len(arrivals)
            arrivals.append(pltpu.make_async_copy(source.at[slots[at]], held.at[at], come.at[at]))
            departures.append(pltpu.make_async_copy(held.at[at], out.at[k], gone.at[at]))
    for copy in arrivals:
        copy.start()
    for arrival, departure in zip(arrivals, departures):
        arrival.wait()
        departure.start()
    for copy in departures:
        copy.wait()


def pick(source, slots, counts):
    total = sum(counts)
    block = source.shape[1:]
    moved = 2 * total * math.prod(block) * source.dtype.itemsize
    return pl.pallas_call(
        functools.partial(pick_kernel, counts),
        in_specs=[pl.BlockSpec(memory_space=pltpu.SMEM), pl.BlockSpec(memory_space=pl.ANY)],
        out_specs=[pl.BlockSpec(memory_space=pl.ANY)] * len(counts),
        out_shape=[jax.ShapeDtypeStruct((n,) + block, source.dtype) for n in counts],
        scratch_shapes=[
            pltpu.VMEM((total,) + block, source.dtype),
            pltpu.SemaphoreType.DMA((total,)),
            pltpu.SemaphoreType.DMA((total,)),
        ],
        compiler_params=pltpu.CompilerParams(vmem_limit_bytes=VMEM_LIMIT),
        cost_estimate=pl.CostEstimate(flops=0, transcendentals=0, bytes_accessed=moved),
        name="pick",
    )(slots, source)


class Places:
    def __init__(self, dp_size):
        self.size, self.far = dp_size, dp_size // 2
        self.dp, self.member = lax.axis_index("dp"), lax.axis_index("fsdp")

    def near_block(self, shift, near):
        return (self.dp // 2 + self.far + shift) % self.far * 2 + self.dp % 2 * (1 - near) + (
            1 - self.dp % 2
        ) * near

    def block(self, shift, near, member):
        return self.near_block(shift, near) * 4 + (self.member ^ member)


def gather_dp(piece, places, far_gate=None, near_gate=None):
    piece = gated(piece, far_gate)
    held = [piece]
    for r in far_order(places.far):
        held.append(lax.ppermute(piece, "dp", far_pairs(places.size, r)))
    mine = jnp.stack(held)
    return jnp.concatenate([mine, near_swap(gated(mine, near_gate), places)])


def gather_group(pair, across, places, gate=None):
    pair, across = gated((pair, across), gate)
    beside, both = member_swap(pair, 1), member_swap(across, 1)
    slots = [
        places.block(-r, near, member)
        for member in (0, 2, 1, 3)
        for near in (0, 1)
        for r in [0] + far_order(places.far)
    ]
    return place([pair, across, beside, both], jnp.stack(slots))


def gated(value, gate):
    return value if gate is None else lax.optimization_barrier((value, gate))[0]


def gather_quarters(quarters, places):
    mine = [
        lax.dynamic_index_in_dim(quarters, places.member ^ k, 0, keepdims=False) for k in range(4)
    ]
    across = member_swap(jnp.stack([mine[2], mine[3]]), 2)
    beside = member_swap(jnp.stack([mine[1], across[1]]), 1)
    out = jnp.zeros_like(quarters)
    for k, value in ((0, mine[0]), (1, beside[0]), (2, across[0]), (3, beside[1])):
        out = lax.dynamic_update_index_in_dim(out, value, places.member ^ k, 0)
    return out


def gather_rows(rows, gate=None):
    if gate is not None:
        rows, _ = lax.optimization_barrier((rows, gate))
    near = member_swap(rows, 1)
    far = member_swap(rows, 2)
    both = member_swap(far, 1)
    return jnp.concatenate([rows, near, far, both], axis=0)


def split_order(far):
    order = far_order(far) + [0]
    return order[: far // 2], order[far // 2 :]


def feed_parts(term, places):
    lots = split_order(places.far)
    slots = [places.near_block(r, near) for near in (1, 0) for lot in lots for r in lot]
    return pick(term, jnp.stack(slots), [len(lot) for _ in range(2) for lot in lots])


def whole_parts(term, places):
    order = sum(split_order(places.far), [])
    slots = [
        places.block(r, near, core + chip)
        for core in (1, 0)
        for chip in (2, 0)
        for near in (1, 0)
        for r in order
    ]
    return pick(term, jnp.stack(slots), [4 * len(order)] * 2)


def near_swap(value, places):
    return lax.ppermute(value, "dp", swap_pairs(places.size, 1))


def member_swap(value, bit):
    return lax.ppermute(value, "fsdp", swap_pairs(4, bit))


def added(own, got):
    return (own.astype(F32) + got.astype(F32)).astype(BF16)


def far_sends(lot, blocks, places):
    return [
        lax.ppermute(blocks[k], "dp", far_pairs(places.size, r)) if r else blocks[k]
        for k, r in enumerate(lot)
    ]


def total_of(parts):
    total = parts[0].astype(F32)
    for part in parts[1:]:
        total = total + part.astype(F32)
    return total


class Rounds:
    def __init__(self):
        self.results = ()

    def enter(self, *values):
        kept = lax.optimization_barrier((values, self.results))[0]
        self.results = ()
        return kept

    def leave(self, *values):
        self.results += values
        return list(values) if len(values) > 1 else values[0]


def sum_steps(value, axis, size, bit=1, end=None):
    while bit < (end or size):
        value = value + lax.ppermute(value, axis, swap_pairs(size, bit))
        bit *= 2
    return value


def local(
    tokens,
    cotangent,
    seq_lengths,
    deal_order,
    attn_gain,
    w_query,
    w_key,
    w_value,
    q_gain,
    k_gain,
    w_out,
    ffn_gain,
    w_gate,
    w_up,
    w_down,
):
    rows, width = tokens.shape
    dp_size = lax.axis_size("dp")
    shard = w_gate.shape[0]
    ff_rows = w_down.shape[0]
    member = lax.axis_index("fsdp")

    lengths = seq_lengths[0]
    slots = jnp.arange(lengths.shape[0], dtype=jnp.int32)
    starts = jnp.sum(jnp.where(slots[None, :] < slots[:, None], lengths[None, :], 0), axis=1)
    row_ids = member * rows + jnp.arange(rows, dtype=jnp.int32)
    begun = starts[None, :] <= row_ids[:, None]
    row_start = jnp.max(jnp.where(begun, starts[None, :], 0), axis=1)
    place = row_ids - row_start
    rel = jnp.broadcast_to((row_start - member * rows)[:, None], (rows, LANES))
    frequency = 10000.0 ** (-2.0 * jnp.arange(HD // 2, dtype=F32) / HD)
    angles = place.astype(F32)[:, None] * frequency[None, :]
    cosine, sine = jnp.cos(angles), jnp.sin(angles)
    cosine = jnp.concatenate([cosine] * 4, axis=1)
    sine = jnp.concatenate([-sine, sine, -sine, sine], axis=1)
    head_gains = jnp.concatenate([jnp.tile(q_gain, HEADS), jnp.tile(k_gain, KV_HEADS)])
    head_gains = jnp.broadcast_to(head_gains.astype(F32)[None, :], (8, head_gains.shape[0]))

    places = Places(dp_size)
    gain_columns = jnp.pad(
        jnp.stack([attn_gain, ffn_gain], axis=1), ((0, 0), (0, LANES - 2))
    )
    w_qkv = jnp.concatenate([w_query, w_key, w_value, gain_columns], axis=1)
    qkv_pair = gather_dp(w_qkv, places)
    out_pair = gather_dp(w_out, places, qkv_pair)
    qkv_across = member_swap(qkv_pair, 2)
    out_across = member_swap(gated(out_pair, qkv_across), 2)
    full_qkv = gather_group(qkv_pair, qkv_across, places).reshape(width, -1)

    ff_block = -(-ff_rows * dp_size // LANES) * LANES // dp_size
    ff_width = dp_size * ff_block

    both_low = quarters_of(w_gate, w_up, dp_size, ff_rows, ff_block)
    both_piece = gather_quarters(gated(both_low, qkv_pair), places).reshape(4 * shard, 2 * ff_width)
    down_piece = jnp.pad(w_down, ((0, ff_block - ff_rows), (0, 0)))
    my_down = lax.all_gather(down_piece, "dp", axis=0, tiled=True)
    my_both = lax.all_gather(both_piece, "dp", axis=0, tiled=True)

    gain_table = full_qkv[:, full_qkv.shape[1] - LANES :]
    pick = (
        lax.broadcasted_iota(jnp.int32, (8, LANES), 0)
        == lax.broadcasted_iota(jnp.int32, (8, LANES), 1)
    ).astype(BF16)
    gain_rows = right_transposed(pick, gain_table)
    attn_row, ffn_row = gain_rows[0:1], gain_rows[1:2]
    x = tokens.astype(F32)
    x_inverse = lax.rsqrt(jnp.mean(x * x, axis=-1, keepdims=True) + EPSILON)
    normed = (x * x_inverse * attn_row).astype(BF16)
    pre = product(normed, full_qkv)
    queries, kv = head_prep(pre, cosine, sine, head_gains)
    ahead_one = [(i, i + 1) for i in range(3)]
    ahead_two = [(i, i + 2) for i in range(2)]
    kv_one = lax.ppermute(kv, "fsdp", ahead_one)
    kv_two = lax.ppermute(kv, "fsdp", ahead_two)
    mixed = attend(queries, kv_two, kv_one, kv, rel)
    full_out = gather_group(out_pair, out_across, places, kv_one).reshape(-1, width)
    hidden = x + product(mixed, full_out)
    h_inverse = lax.rsqrt(jnp.mean(hidden * hidden, axis=-1, keepdims=True) + EPSILON)
    ffn_mine = (hidden * h_inverse * ffn_row).astype(BF16)

    upstream = gather_rows(cotangent, kv_one)
    ffn_low = gather_rows(ffn_mine)
    act_low, gate_slope, up_slope = feed(ffn_low, my_both)
    lot_a, lot_b = split_order(places.far)

    def parts_of(left, right):
        term = left_transposed(left, right).astype(BF16)
        return feed_parts(term.reshape(dp_size, -1, term.shape[1]), places)

    rounds = Rounds()

    d_oa, d_ob, d_wa, d_wb, upstream, my_down = rounds.enter(
        *parts_of(act_low, upstream), upstream, my_down
    )
    d_ga = rounds.leave(near_swap(d_oa, places))
    grad_gate, grad_up = feed_slopes(upstream, my_down, gate_slope, up_slope)
    grad_gate, grad_up, ffn_own, ffn_other = rounds.leave(
        grad_gate, grad_up, *feed_back(grad_gate, grad_up, my_both)
    )

    d_sa = added(d_wa, d_ga)
    d_sa, d_ob, grad_gate, grad_up, ffn_own, ffn_other = rounds.enter(
        d_sa, d_ob, grad_gate, grad_up, ffn_own, ffn_other
    )
    ffn_got = rounds.leave(member_swap(ffn_other, 1))
    far_got = rounds.leave(member_swap(added(ffn_own[1], ffn_got[1]), 2))
    d_za = rounds.leave(*far_sends(lot_a, d_sa, places))
    d_gb = rounds.leave(near_swap(d_ob, places))
    g_oa, g_ob, g_wa, g_wb = rounds.leave(*parts_of(ffn_low, grad_gate))
    u_oa, u_ob, u_wa, u_wb = rounds.leave(*parts_of(ffn_low, grad_up))

    d_sb = added(d_wb, d_gb)
    g_oa, d_sb, ffn_own, ffn_got, far_got = rounds.enter(g_oa, d_sb, ffn_own, ffn_got, far_got)
    g_ga = rounds.leave(near_swap(g_oa, places))
    d_zb = rounds.leave(*far_sends(lot_b, d_sb, places))
    grad_ffn = ffn_own[0] + ffn_got[0].astype(F32) + far_got.astype(F32)
    e = grad_ffn * ffn_row
    slope = jnp.mean(hidden * e, axis=-1, keepdims=True)
    grad_hidden = cotangent.astype(F32) + h_inverse * e - hidden * (h_inverse**3 * slope)
    ffn_gain_term = jnp.sum(grad_ffn * hidden * h_inverse, axis=0)
    grad_hidden_low = grad_hidden.astype(BF16)
    grad_mixed = right_transposed(grad_hidden_low, full_out).astype(BF16)
    gq, gkv_two, gkv_one, gkv = rounds.leave(
        *attend_back(queries, kv_two, kv_one, kv, rel, grad_mixed)
    )
    term_out = left_transposed(mixed, grad_hidden_low).astype(BF16)
    o_other, o_own = rounds.leave(
        *whole_parts(term_out.reshape(4 * dp_size, -1, width), places)
    )

    g_sa = added(g_wa, g_ga)
    g_sa, g_ob, gkv_one, gkv_two, o_other, o_own, gq, gkv = rounds.enter(
        g_sa, g_ob, gkv_one, gkv_two, o_other, o_own, gq, gkv
    )
    g_za = rounds.leave(*far_sends(lot_a, g_sa, places))
    g_gb = rounds.leave(near_swap(g_ob, places))
    got_one = lax.ppermute(gkv_one, "fsdp", [(b, a) for a, b in ahead_one])
    got_two = lax.ppermute(gkv_two, "fsdp", [(b, a) for a, b in ahead_two])
    o_sum = added(o_own, member_swap(o_other, 1))
    half = o_sum.shape[0] // 2
    quarter, lot = half // 2, half // 2
    o_across = rounds.leave(member_swap(gated(o_sum[:half], got_two), 2))
    o_sum = rounds.leave(o_sum[half:])
    grad_pre, head_sums = head_back(gq, gkv, got_one, got_two, pre, cosine, sine, head_gains)
    term_qkv = left_transposed(normed, grad_pre).astype(BF16)
    q_other, q_own = rounds.leave(
        *whole_parts(term_qkv.reshape(4 * dp_size, shard, -1), places)
    )

    g_sb = added(g_wb, g_gb)
    o_sum = added(o_sum, o_across)
    u_oa, g_sb, q_other, q_own, grad_pre, o_sum = rounds.enter(
        u_oa, g_sb, q_other, q_own, grad_pre, o_sum
    )
    o_got = rounds.leave(near_swap(o_sum[:quarter], places))
    o_sum = o_sum[quarter:]
    q_sum = rounds.leave(added(q_own, member_swap(q_other, 1)))
    q_xa = rounds.leave(member_swap(q_sum[:lot], 2))
    u_ga = rounds.leave(near_swap(u_oa, places))
    g_zb = rounds.leave(*far_sends(lot_b, g_sb, places))
    u_sa = added(u_wa, u_ga)
    o_sum = added(o_sum, o_got)
    u_sa, u_ob, q_xb, grad_pre, act_low, o_sum = rounds.enter(
        u_sa, u_ob, q_sum[lot:half], grad_pre, act_low, o_sum
    )
    o_parts = rounds.leave(*far_sends(lot_a + lot_b, o_sum, places))
    q_xb = rounds.leave(member_swap(q_xb, 2))
    grad_normed = right_transposed(grad_pre, full_qkv)
    out_part = product(act_low, my_down).reshape(2, 2, rows, width)
    out_own, out_other = rounds.leave(out_part[:, 0], out_part[:, 1].astype(BF16))
    u_za = rounds.leave(*far_sends(lot_a, u_sa, places))
    u_gb = rounds.leave(near_swap(u_ob, places))
    gate_low = total_of(g_za + g_zb).astype(BF16).reshape(4, shard, ff_width)
    gate_low = rounds.leave(gate_low)
    down_grad = rounds.leave(total_of(d_za + d_zb)[:ff_rows])
    e = grad_normed * attn_row
    slope = jnp.mean(x * e, axis=-1, keepdims=True)
    input_grad = grad_hidden + x_inverse * e - x * (x_inverse**3 * slope)
    input_grad = rounds.leave(input_grad.astype(BF16))
    attn_gain_term = rounds.leave(jnp.sum(grad_normed * x * x_inverse, axis=0))

    small = jnp.concatenate([attn_gain_term, ffn_gain_term, head_sums.reshape(-1)])
    small = rounds.leave(small.reshape(-1, LANES))

    u_sb = added(u_wb, u_gb)
    q_y = added(q_sum[half:], jnp.concatenate([q_xa, q_xb]))
    u_sb, q_yo, q_yw, gate_low, out_own, out_other = rounds.enter(
        u_sb, q_y[:quarter], q_y[quarter:], gate_low, out_own, out_other
    )
    out_got = member_swap(out_other, 1)
    out_far = added(out_own[1], out_got[1])
    u_zb = rounds.leave(*far_sends(lot_b, u_sb, places))
    q_yo = rounds.leave(near_swap(q_yo, places))
    out_far = rounds.leave(member_swap(out_far, 2))
    gate_got = rounds.leave(lax.all_to_all(gate_low, "fsdp", 0, 0, tiled=True))
    out_grad = rounds.leave(total_of(o_parts))

    q_z = added(q_yw, q_yo)
    up_low = total_of(u_za + u_zb).astype(BF16).reshape(4, shard, ff_width)
    q_z, up_low, gate_got, out_far, small = rounds.enter(q_z, up_low, gate_got, out_far, small)
    small = sum_steps(sum_steps(small, "fsdp", 4), "dp", dp_size, 1, 2)
    q_parts = rounds.leave(*far_sends(lot_a + lot_b, q_z, places))
    up_got = rounds.leave(lax.all_to_all(up_low, "fsdp", 0, 0, tiled=True))
    gate_grad = rounds.leave(columns_of(gate_got, dp_size, ff_rows, ff_block))

    small, up_got = rounds.enter(small, up_got)
    small = sum_steps(small, "dp", dp_size, 2).reshape(-1)
    qkv_grad = total_of(q_parts)

    up_grad = columns_of(up_got, dp_size, ff_rows, ff_block)
    output = (hidden + out_own[0] + out_got[0].astype(F32) + out_far.astype(F32)).astype(BF16)

    mine = (lax.axis_index("dp") * 4 + member) * shard
    attn_gain_grad = lax.dynamic_slice(small, (mine,), (shard,))
    ffn_gain_grad = lax.dynamic_slice(small, (width + mine,), (shard,))
    head_total = small[2 * width : 2 * width + 2 * LANES].reshape(2, 2, HD).sum(axis=1)

    q_end = HEADS * HD
    k_end = q_end + KV_HEADS * HD
    v_end = k_end + KV_HEADS * HD
    return (
        output,
        input_grad.astype(BF16),
        attn_gain_grad,
        qkv_grad[:, :q_end],
        qkv_grad[:, q_end:k_end],
        qkv_grad[:, k_end:v_end],
        head_total[0],
        head_total[1],
        out_grad,
        ffn_gain_grad,
        gate_grad,
        up_grad,
        down_grad,
    )


def solution(mesh):
    rows = P(BOTH, None)
    vector = P(BOTH)
    in_specs = (
        rows,
        rows,
        P("dp", None),
        P("dp", None),
        vector,
        rows,
        rows,
        rows,
        P(),
        P(),
        rows,
        vector,
        rows,
        rows,
        rows,
    )
    out_specs = (rows, rows, vector, rows, rows, rows, P(), P(), rows, vector, rows, rows, rows)
    return jax.shard_map(local, mesh=mesh, in_specs=in_specs, out_specs=out_specs, check_vma=False)
```

```python
import functools
import math

import jax
import jax.numpy as jnp
from jax import lax
from jax.experimental import pallas as pl
from jax.experimental.pallas import tpu as pltpu
from jax.sharding import PartitionSpec as P

HEADS = 24
KV_HEADS = 6
HD = 64
EPSILON = 1e-06
MASKED = -1e30
LANES = 128
BOTH = ("dp", "fsdp")
F32 = jnp.float32
BF16 = jnp.bfloat16
VMEM_LIMIT = 48 * 1024 * 1024


def product(left, right):
    return jnp.dot(left, right, preferred_element_type=F32)


def right_transposed(left, right):
    return lax.dot_general(left, right, (((1,), (1,)), ((), ())), preferred_element_type=F32)


def left_transposed(left, right):
    return lax.dot_general(left, right, (((0,), (0,)), ((), ())), preferred_element_type=F32)


def half_sums(values):
    rows = lax.broadcasted_iota(jnp.int32, (LANES, LANES), 0) // HD
    cols = lax.broadcasted_iota(jnp.int32, (LANES, LANES), 1) // HD
    same = (rows == cols).astype(F32)
    return jnp.dot(values, same, precision=lax.Precision.HIGHEST, preferred_element_type=F32)


def swapped_halves(values):
    lane = lax.broadcasted_iota(jnp.int32, values.shape, 1) % HD
    return jnp.where(
        lane < HD // 2, pltpu.roll(values, LANES - HD // 2, 1), pltpu.roll(values, HD // 2, 1)
    )


def head_prep_kernel(pre_ref, cos_ref, sin_ref, gain_ref, q_ref, kv_ref):
    q_blocks = HEADS * HD // LANES
    k_blocks = KV_HEADS * HD // LANES
    cosine, sine = cos_ref[...], sin_ref[...]
    for block in range(q_blocks + k_blocks):
        at = pl.ds(block * LANES, LANES)
        u = pre_ref[:, at]
        n = u * lax.rsqrt(half_sums(u * u) / HD + EPSILON) * gain_ref[:1, at]
        turned = n * cosine + swapped_halves(n) * sine
        if block < q_blocks:
            q_ref[:, at] = (turned.astype(BF16).astype(F32) * (1.0 / math.sqrt(HD))).astype(BF16)
        else:
            kv_ref[0, :, pl.ds((block - q_blocks) * LANES, LANES)] = turned.astype(BF16)
    v_at = (q_blocks + k_blocks) * LANES
    kv_ref[1] = pre_ref[:, v_at : v_at + k_blocks * LANES].astype(BF16)


def head_prep(pre, cosine, sine, gains):
    rows = pre.shape[0]
    return pl.pallas_call(
        head_prep_kernel,
        out_shape=(
            jax.ShapeDtypeStruct((rows, HEADS * HD), BF16),
            jax.ShapeDtypeStruct((2, rows, KV_HEADS * HD), BF16),
        ),
        compiler_params=pltpu.CompilerParams(vmem_limit_bytes=VMEM_LIMIT),
        name="head_prep",
    )(pre, cosine, sine, gains)


def head_back_kernel(
    gq_ref, gkv_ref, one_ref, two_ref, pre_ref, cos_ref, sin_ref, gain_ref, out_ref, sums_ref
):
    q_blocks = HEADS * HD // LANES
    k_blocks = KV_HEADS * HD // LANES
    cosine, sine = cos_ref[...], sin_ref[...]
    sums_ref[...] = jnp.zeros_like(sums_ref)
    for block in range(q_blocks + k_blocks):
        at = pl.ds(block * LANES, LANES)
        if block < q_blocks:
            g = gq_ref[:, at]
        else:
            k_at = pl.ds((block - q_blocks) * LANES, LANES)
            g = gkv_ref[0, :, k_at] + one_ref[0, :, k_at].astype(F32) + two_ref[0, :, k_at].astype(F32)
        g = g * cosine - swapped_halves(g) * sine
        u = pre_ref[:, at]
        inverse = lax.rsqrt(half_sums(u * u) / HD + EPSILON)
        unit = u * inverse
        row = 0 if block < q_blocks else 1
        sums_ref[row : row + 1, :] += jnp.sum(unit * g, axis=0, keepdims=True)
        e = g * gain_ref[:1, at]
        out_ref[:, at] = (inverse * (e - unit * (half_sums(e * unit) / HD))).astype(BF16)
    v_at = (q_blocks + k_blocks) * LANES
    width = k_blocks * LANES
    out_ref[:, v_at : v_at + width] = (
        gkv_ref[1] + one_ref[1].astype(F32) + two_ref[1].astype(F32)
    ).astype(BF16)
    tail = out_ref.shape[1] - v_at - width
    out_ref[:, v_at + width :] = jnp.zeros((out_ref.shape[0], tail), BF16)


def head_back(gq, gkv, one, two, pre, cosine, sine, gains):
    rows, width = pre.shape
    return pl.pallas_call(
        head_back_kernel,
        out_shape=(
            jax.ShapeDtypeStruct((rows, width), BF16),
            jax.ShapeDtypeStruct((8, LANES), F32),
        ),
        compiler_params=pltpu.CompilerParams(vmem_limit_bytes=VMEM_LIMIT),
        name="head_back",
    )(gq, gkv, one, two, pre, cosine, sine, gains)


def stacked_heads(ref, pair, repeat):
    return jnp.concatenate(
        [ref[:, pl.ds((pair * repeat + h) * HD, HD)] for h in range(repeat)], axis=0
    )


def window_probs(q4, keys, rel, repeat):
    rows, span = rel.shape[0], keys.shape[0]
    scores = right_transposed(q4, keys).reshape(repeat, rows, span)
    key_at = lax.broadcasted_iota(jnp.int32, (rows, span), 1) - (span - rows)
    row_at = lax.broadcasted_iota(jnp.int32, (rows, span), 0)
    allowed = (key_at <= row_at) & (key_at >= rel)
    scores = jnp.where(allowed[None], scores, MASKED)
    top = jnp.max(scores, axis=-1, keepdims=True)
    raised = jnp.exp(scores - top)
    return raised * (1.0 / jnp.sum(raised, axis=-1, keepdims=True))


def attend_kernel(q_ref, two_ref, one_ref, kv_ref, rel_ref, out_ref):
    repeat = HEADS // KV_HEADS
    rows = q_ref.shape[0]
    rel = rel_ref[:, :1]
    keys = jnp.concatenate([two_ref[0], one_ref[0], kv_ref[0]], axis=0)
    vals = jnp.concatenate([two_ref[1], one_ref[1], kv_ref[1]], axis=0)
    for pair in range(2):
        part = slice(pair * HD, (pair + 1) * HD)
        q4 = stacked_heads(q_ref, pair, repeat)
        probs = window_probs(q4, keys[:, part], rel, repeat)
        low = probs.astype(BF16).reshape(repeat * rows, -1)
        mixed = product(low, vals[:, part])
        for h in range(repeat):
            out_ref[:, pl.ds((pair * repeat + h) * HD, HD)] = mixed[
                h * rows : (h + 1) * rows
            ].astype(BF16)


def attend_specs(rows):
    q_spec = pl.BlockSpec((rows, HEADS * HD // 3), lambda g: (0, g))
    kv_spec = pl.BlockSpec((2, rows, LANES), lambda g: (0, 0, g))
    rel_spec = pl.BlockSpec((rows, LANES), lambda g: (0, 0))
    return q_spec, kv_spec, rel_spec


def attend(q, two, one, kv, rel):
    rows = q.shape[0]
    q_spec, kv_spec, rel_spec = attend_specs(rows)
    return pl.pallas_call(
        attend_kernel,
        grid=(3,),
        in_specs=[q_spec, kv_spec, kv_spec, kv_spec, rel_spec],
        out_specs=q_spec,
        out_shape=jax.ShapeDtypeStruct((rows, HEADS * HD), BF16),
        compiler_params=pltpu.CompilerParams(vmem_limit_bytes=VMEM_LIMIT),
        name="attend",
    )(q, two, one, kv, rel)


def attend_back_kernel(
    q_ref, two_ref, one_ref, kv_ref, rel_ref, gm_ref, gq_ref, gtwo_ref, gone_ref, gkv_ref
):
    repeat = HEADS // KV_HEADS
    rows = q_ref.shape[0]
    rel = rel_ref[:, :1]
    keys = jnp.concatenate([two_ref[0], one_ref[0], kv_ref[0]], axis=0)
    vals = jnp.concatenate([two_ref[1], one_ref[1], kv_ref[1]], axis=0)
    key_grads, val_grads = [], []
    for pair in range(2):
        part = slice(pair * HD, (pair + 1) * HD)
        q4 = stacked_heads(q_ref, pair, repeat)
        gm4 = stacked_heads(gm_ref, pair, repeat)
        probs = window_probs(q4, keys[:, part], rel, repeat)
        grad_probs = right_transposed(gm4, vals[:, part]).reshape(probs.shape)
        weighted = jnp.sum(probs * grad_probs, axis=-1, keepdims=True)
        span = probs.shape[-1]
        gs = (probs * (grad_probs - weighted)).astype(BF16).reshape(repeat * rows, span)
        low = probs.astype(BF16).reshape(repeat * rows, span)
        gq = product(gs, keys[:, part]) * (1.0 / math.sqrt(HD))
        for h in range(repeat):
            gq_ref[:, pl.ds((pair * repeat + h) * HD, HD)] = gq[h * rows : (h + 1) * rows]
        key_grads.append(product(q4.T, gs).T)
        val_grads.append(product(gm4.T, low).T)
    for at, parts in ((0, key_grads), (1, val_grads)):
        both = jnp.concatenate(parts, axis=1)
        gtwo_ref[at] = both[:rows].astype(gtwo_ref.dtype)
        gone_ref[at] = both[rows : 2 * rows].astype(gone_ref.dtype)
        gkv_ref[at] = both[2 * rows :]


def attend_back(q, two, one, kv, rel, gm):
    rows = q.shape[0]
    q_spec, kv_spec, rel_spec = attend_specs(rows)
    return pl.pallas_call(
        attend_back_kernel,
        grid=(3,),
        in_specs=[q_spec, kv_spec, kv_spec, kv_spec, rel_spec, q_spec],
        out_specs=(q_spec, kv_spec, kv_spec, kv_spec),
        out_shape=(
            jax.ShapeDtypeStruct((rows, HEADS * HD), F32),
            jax.ShapeDtypeStruct((2, rows, KV_HEADS * HD), BF16),
            jax.ShapeDtypeStruct((2, rows, KV_HEADS * HD), BF16),
            jax.ShapeDtypeStruct((2, rows, KV_HEADS * HD), F32),
        ),
        compiler_params=pltpu.CompilerParams(vmem_limit_bytes=VMEM_LIMIT),
        name="attend_back",
    )(q, two, one, kv, rel, gm)


def feed_kernel(x_ref, both_ref, act_ref, slopes_ref):
    units = act_ref.shape[1]
    mixed = product(x_ref[...], both_ref[...])
    gate, up = mixed[:, :units], mixed[:, units:]
    sig = 1.0 / (1.0 + jnp.exp(-gate))
    silu = gate * sig
    act_ref[...] = (silu * up).astype(BF16)
    slopes_ref[:, :units] = (up * sig * (1.0 + gate * (1.0 - sig))).astype(BF16)
    slopes_ref[:, units:] = silu.astype(BF16)


def feed(x, both, tile):
    rows, width = x.shape
    units = both.shape[1] // 2
    return pl.pallas_call(
        feed_kernel,
        grid=(rows // tile,),
        in_specs=[
            pl.BlockSpec((tile, width), lambda i: (i, 0)),
            pl.BlockSpec((width, 2 * units), lambda i: (0, 0)),
        ],
        out_specs=[
            pl.BlockSpec((tile, units), lambda i: (i, 0)),
            pl.BlockSpec((tile, 2 * units), lambda i: (i, 0)),
        ],
        out_shape=[
            jax.ShapeDtypeStruct((rows, units), BF16),
            jax.ShapeDtypeStruct((rows, 2 * units), BF16),
        ],
        compiler_params=pltpu.CompilerParams(vmem_limit_bytes=VMEM_LIMIT),
        cost_estimate=pl.CostEstimate(
            flops=4 * rows * width * units,
            transcendentals=rows * units,
            bytes_accessed=2 * (rows * width + 2 * width * units + 3 * rows * units),
        ),
        name="feed",
    )(x, both)


def feed_back_kernel(x_ref, down_ref, slopes_ref, both_ref, grads_ref, own_ref, other_ref):
    step, steps = pl.program_id(0), pl.num_programs(0)
    lots = own_ref.shape[0]
    grad_act = right_transposed(x_ref[...], down_ref[...])
    both_act = jnp.concatenate([grad_act, grad_act], axis=1)
    grads = (both_act * slopes_ref[...].astype(F32)).astype(BF16)
    grads_ref[...] = grads
    total = right_transposed(grads, both_ref[...])
    total = total.reshape(lots, -1, total.shape[1])

    total = total.astype(BF16)

    @pl.when(step < steps // 2)
    def _():
        own_ref[...] = total

    @pl.when(step >= steps // 2)
    def _():
        other_ref[...] = total


def feed_back(upstream, down, slopes, both, lot, tile):
    rows, width = upstream.shape
    units = down.shape[0]
    steps = rows // tile
    lots = rows // lot
    per = tile // lot
    return pl.pallas_call(
        feed_back_kernel,
        grid=(steps,),
        in_specs=[
            pl.BlockSpec((tile, width), lambda i: (i, 0)),
            pl.BlockSpec((units, width), lambda i: (0, 0)),
            pl.BlockSpec((tile, 2 * units), lambda i: (i, 0)),
            pl.BlockSpec((width, 2 * units), lambda i: (0, 0)),
        ],
        out_specs=[
            pl.BlockSpec((tile, 2 * units), lambda i: (i, 0)),
            pl.BlockSpec((per, lot, width), lambda i: (jnp.minimum(i, steps // 2 - 1), 0, 0)),
            pl.BlockSpec((per, lot, width), lambda i: (jnp.maximum(i - steps // 2, 0), 0, 0)),
        ],
        out_shape=[
            jax.ShapeDtypeStruct((rows, 2 * units), BF16),
            jax.ShapeDtypeStruct((lots // 2, lot, width), BF16),
            jax.ShapeDtypeStruct((lots // 2, lot, width), BF16),
        ],
        compiler_params=pltpu.CompilerParams(vmem_limit_bytes=VMEM_LIMIT),
        cost_estimate=pl.CostEstimate(
            flops=6 * rows * width * units,
            transcendentals=0,
            bytes_accessed=2 * (3 * rows * width + 3 * width * units + 4 * rows * units),
        ),
        name="feed_back",
    )(upstream, down, slopes, both)


def lane_window(read, tiles, start):
    tile, shift = start // LANES, start % LANES
    first = read(min(max(tile, 0), tiles - 1))
    if shift == 0:
        return first
    second = read(min(max(tile + 1, 0), tiles - 1))
    lane = lax.broadcasted_iota(jnp.int32, first.shape, 1)
    return jnp.where(
        lane < LANES - shift,
        pltpu.roll(first, LANES - shift, 1),
        pltpu.roll(second, LANES - shift, 1),
    )


def lane_runs(target, runs, source_of):
    total = None
    for first, length, source in runs:
        low, high = max(first, target), min(first + length, target + LANES)
        if low >= high:
            continue
        window = source_of(source, target - first)
        lane = lax.broadcasted_iota(jnp.int32, window.shape, 1) + target
        kept = jnp.where((lane >= low) & (lane < high), window, 0.0)
        total = kept if total is None else total + kept
    return total


def split_kernel(far, unit, block, me_ref, gate_ref, up_ref, out_ref):
    units = far * block
    tiles = -(-gate_ref.shape[1] // LANES)
    for at, ref in ((0, gate_ref), (units, up_ref)):
        for part in range(8):
            runs = [(d * block, unit, (8 * d + part) * unit) for d in range(far)]

            def source_of(source, offset):
                read = lambda t: ref[:, t * LANES : (t + 1) * LANES].astype(F32)
                return lane_window(read, tiles, source + offset)

            for target in range(0, units, LANES):
                value = lane_runs(target, runs, source_of)
                to = pl.ds(at + target, LANES)
                turned = part // 2 % 2 * 4 + part // 4 * 2 + part % 2
                out_ref[turned ^ me_ref[0], :, to] = value.astype(BF16)


def split_units(gate, up, me, far, unit, block):
    return pl.pallas_call(
        functools.partial(split_kernel, far, unit, block),
        in_specs=[
            pl.BlockSpec(memory_space=pltpu.SMEM),
            pl.BlockSpec(memory_space=pltpu.VMEM),
            pl.BlockSpec(memory_space=pltpu.VMEM),
        ],
        out_shape=jax.ShapeDtypeStruct((8, gate.shape[0], 2 * far * block), BF16),
        compiler_params=pltpu.CompilerParams(vmem_limit_bytes=VMEM_LIMIT),
        name="split_units",
    )(me, gate, up)


def join_kernel(far, unit, block, me_ref, got_ref, gate_ref, up_ref):
    units = far * block
    tiles = got_ref.shape[2] // LANES
    runs = [
        ((8 * d + part) * unit, unit, (part, d * block)) for d in range(far) for part in range(8)
    ]
    for at, ref in ((0, gate_ref), (units, up_ref)):

        def source_of(source, offset):
            read = lambda t: got_ref[
                source[0] ^ me_ref[0], :, t * LANES : (t + 1) * LANES
            ].astype(F32)
            return lane_window(read, tiles, at + source[1] + offset)

        for target in range(0, ref.shape[1], LANES):
            ref[:, target : target + LANES] = lane_runs(target, runs, source_of)


def join_units(got, me, far, unit, block):
    out = jax.ShapeDtypeStruct((got.shape[1], 8 * far * unit), F32)
    return pl.pallas_call(
        functools.partial(join_kernel, far, unit, block),
        in_specs=[
            pl.BlockSpec(memory_space=pltpu.SMEM),
            pl.BlockSpec(memory_space=pltpu.VMEM),
        ],
        out_shape=[out, out],
        compiler_params=pltpu.CompilerParams(vmem_limit_bytes=VMEM_LIMIT),
        name="join_units",
    )(me, got)


def swap_pairs(size, bit):
    return [(i, i ^ bit) for i in range(size)]


def far_pairs(size, shift):
    far = size // 2
    return [(i, (i // 2 + shift) % far * 2 + i % 2) for i in range(size)]


def far_order(far):
    order = []
    for step in range(1, far // 2 + 1):
        order.append(step)
        if far - step != step:
            order.append(far - step)
    return order


def place_kernel(counts, slots, *refs):
    pieces, out, held, come, gone = refs[: len(counts)], *refs[len(counts) :]
    arrivals, departures = [], []
    for piece, count in zip(pieces, counts):
        for k in range(count):
            at = len(arrivals)
            arrivals.append(pltpu.make_async_copy(piece.at[k], held.at[at], come.at[at]))
            departures.append(pltpu.make_async_copy(held.at[at], out.at[slots[at]], gone.at[at]))
    for copy in arrivals:
        copy.start()
    for arrival, departure in zip(arrivals, departures):
        arrival.wait()
        departure.start()
    for copy in departures:
        copy.wait()


def place(pieces, slots):
    counts = [piece.shape[0] for piece in pieces]
    total = sum(counts)
    shape = (total,) + pieces[0].shape[1:]
    moved = 2 * math.prod(shape) * pieces[0].dtype.itemsize
    return pl.pallas_call(
        functools.partial(place_kernel, counts),
        in_specs=[pl.BlockSpec(memory_space=pltpu.SMEM)]
        + [pl.BlockSpec(memory_space=pl.ANY)] * len(pieces),
        out_specs=pl.BlockSpec(memory_space=pl.ANY),
        out_shape=jax.ShapeDtypeStruct(shape, pieces[0].dtype),
        scratch_shapes=[
            pltpu.VMEM(shape, pieces[0].dtype),
            pltpu.SemaphoreType.DMA((total,)),
            pltpu.SemaphoreType.DMA((total,)),
        ],
        compiler_params=pltpu.CompilerParams(vmem_limit_bytes=VMEM_LIMIT),
        cost_estimate=pl.CostEstimate(flops=0, transcendentals=0, bytes_accessed=moved),
        name="place",
    )(slots, *pieces)


def pick_kernel(counts, slots, source, *refs):
    outs, (held, come, gone) = refs[: len(counts)], refs[len(counts) :]
    arrivals, departures = [], []
    for out, count in zip(outs, counts):
        for k in range(count):
            at = len(arrivals)
            arrivals.append(pltpu.make_async_copy(source.at[slots[at]], held.at[at], come.at[at]))
            departures.append(pltpu.make_async_copy(held.at[at], out.at[k], gone.at[at]))
    for copy in arrivals:
        copy.start()
    for arrival, departure in zip(arrivals, departures):
        arrival.wait()
        departure.start()
    for copy in departures:
        copy.wait()


def pick(source, slots, counts):
    total = sum(counts)
    block = source.shape[1:]
    moved = 2 * total * math.prod(block) * source.dtype.itemsize
    return pl.pallas_call(
        functools.partial(pick_kernel, counts),
        in_specs=[pl.BlockSpec(memory_space=pltpu.SMEM), pl.BlockSpec(memory_space=pl.ANY)],
        out_specs=[pl.BlockSpec(memory_space=pl.ANY)] * len(counts),
        out_shape=[jax.ShapeDtypeStruct((n,) + block, source.dtype) for n in counts],
        scratch_shapes=[
            pltpu.VMEM((total,) + block, source.dtype),
            pltpu.SemaphoreType.DMA((total,)),
            pltpu.SemaphoreType.DMA((total,)),
        ],
        compiler_params=pltpu.CompilerParams(vmem_limit_bytes=VMEM_LIMIT),
        cost_estimate=pl.CostEstimate(flops=0, transcendentals=0, bytes_accessed=moved),
        name="pick",
    )(slots, source)


class Places:
    def __init__(self, dp_size):
        self.size, self.far = dp_size, dp_size // 2
        self.dp, self.member = lax.axis_index("dp"), lax.axis_index("fsdp")
        self.me = self.dp % 2 * 4 + self.member
        self.groups = [[2 * z + y for z in range(self.far)] for y in range(2)]

    def near_block(self, shift, near):
        return (self.dp // 2 + self.far + shift) % self.far * 2 + self.dp % 2 * (1 - near) + (
            1 - self.dp % 2
        ) * near

    def block(self, shift, near, member):
        return self.near_block(shift, near) * 4 + (self.member ^ member)


def far_gather(piece, places):
    held = {0: piece}
    for r in far_order(places.far):
        held[r] = lax.ppermute(piece, "dp", far_pairs(places.size, r))
    return held


def whole_slots(lots, places):
    return jnp.stack(
        [
            places.block(-r, near, member)
            for lot in lots
            for member in (0, 2, 1, 3)
            for near in (0, 1)
            for r in lot
        ]
    )


def gated(value, gate):
    return value if gate is None else lax.optimization_barrier((value, gate))[0]


def exchange_units(parts, places):
    across = member_swap(parts[4:], 2)
    parts = jnp.stack([parts[:4], across])
    near = near_swap(parts[:, 2:], places)
    parts = jnp.stack([parts[:, :2], near])
    beside = member_swap(parts[:, :, 1], 1)
    own = parts[:, :, 0]
    blocks = [own.reshape(4, *own.shape[2:]), beside.reshape(4, *own.shape[2:])]
    slots = [
        places.me ^ (4 * near + 2 * chip + core)
        for core in (0, 1)
        for near in (0, 1)
        for chip in (0, 1)
    ]
    return place(blocks, jnp.stack(slots)), beside


def return_units(blocks, places):
    slots = [
        places.me ^ (4 * near + 2 * chip + core)
        for core in (1, 0)
        for chip in (1, 0)
        for near in (1, 0)
    ]
    other, own = pick(blocks, jnp.stack(slots), [4, 4])
    beside = member_swap(other, 1)
    held = jnp.stack([own, beside])
    across = member_swap(held[:, :2], 2)
    held = jnp.stack([held[:, 2:], across])
    near = near_swap(held[:, :, 0], places)
    held = jnp.stack([held[:, :, 1], near])
    return held.reshape(8, *blocks.shape[1:])


def assemble_kernel(*refs):
    pieces, (out, held, come, gone) = refs[:-4], refs[-4:]
    half = out.shape[2] // 2
    arrivals, departures = [], []
    for k, piece in enumerate(pieces):
        core, at = k // 5, k % 5
        columns = pl.ds(0, 2 * half) if at < 3 else pl.ds((at - 3) * half, half)
        spot = (core * 4 + min(at, 3), slice(None), columns)
        arrivals.append(pltpu.make_async_copy(piece, held.at[spot], come.at[k]))
        departures.append(pltpu.make_async_copy(held.at[spot], out.at[spot], gone.at[k]))
    for copy in arrivals:
        copy.start()
    for arrival, departure in zip(arrivals, departures):
        arrival.wait()
        departure.start()
    for copy in departures:
        copy.wait()


def assemble(pieces):
    rows, width = pieces[0].shape
    shape = (8, rows, width)
    return pl.pallas_call(
        assemble_kernel,
        in_specs=[pl.BlockSpec(memory_space=pl.ANY)] * len(pieces),
        out_specs=pl.BlockSpec(memory_space=pl.ANY),
        out_shape=jax.ShapeDtypeStruct(shape, BF16),
        scratch_shapes=[
            pltpu.VMEM(shape, BF16),
            pltpu.SemaphoreType.DMA((len(pieces),)),
            pltpu.SemaphoreType.DMA((len(pieces),)),
        ],
        compiler_params=pltpu.CompilerParams(vmem_limit_bytes=VMEM_LIMIT),
        cost_estimate=pl.CostEstimate(
            flops=0, transcendentals=0, bytes_accessed=4 * math.prod(shape)
        ),
        name="assemble",
    )(*pieces)


def gather_rows(rows, places, gate=None):
    rows = gated(rows, gate)
    half = rows.shape[1] // 2
    across, near = member_swap(rows, 2), near_swap(rows, places)
    left = near_swap(across[:, :half], places)
    right = member_swap(near[:, half:], 2)
    pieces = [rows, across, near, left, right]
    out = assemble(pieces + [member_swap(piece, 1) for piece in pieces])
    return out.reshape(8 * rows.shape[0], rows.shape[1])


def merge_kernel(own_ref, got_ref, near_ref, across_ref, left_ref, right_ref):
    half = own_ref.shape[2] // 2
    left, right = pl.ds(0, half), pl.ds(half, half)

    def total(lot, columns):
        return own_ref[lot, :, columns].astype(F32) + got_ref[lot, :, columns].astype(F32)

    for k, lot in enumerate((2, 3)):
        near_ref[k] = total(lot, left).astype(BF16)
    for k, lot in enumerate((1, 3)):
        across_ref[k] = total(lot, right).astype(BF16)
    for k, lot in enumerate((0, 1)):
        left_ref[k] = total(lot, left)
    for k, lot in enumerate((0, 2)):
        right_ref[k] = total(lot, right)


def merge(own, got):
    shape = (2, own.shape[1], own.shape[2] // 2)
    low, wide = jax.ShapeDtypeStruct(shape, BF16), jax.ShapeDtypeStruct(shape, F32)
    return pl.pallas_call(
        merge_kernel,
        out_shape=[low, low, wide, wide],
        compiler_params=pltpu.CompilerParams(vmem_limit_bytes=VMEM_LIMIT),
        cost_estimate=pl.CostEstimate(
            flops=own.size, transcendentals=0, bytes_accessed=7 * own.size
        ),
        name="merge",
    )(own, got)


def scatter_first(own, other, places):
    near, across, left, right = merge(own, member_swap(other, 1))
    near, across = near_swap(near, places), member_swap(across, 2)
    return left, near, right, across


def scatter_second(left, near, right, across, places):
    left_out = (left[1] + near[1].astype(F32)).astype(BF16)
    right_out = (right[1] + across[1].astype(F32)).astype(BF16)
    left_got, right_got = member_swap(left_out, 2), near_swap(right_out, places)
    left = left[0] + near[0].astype(F32) + left_got.astype(F32)
    right = right[0] + across[0].astype(F32) + right_got.astype(F32)
    return jnp.concatenate([left, right], axis=1)


def split_order(far):
    order = far_order(far) + [0]
    return order[: far // 2], order[far // 2 :]


def far_parts(term, places):
    order = sum(split_order(places.far), [])
    slots = [(places.dp // 2 + r) % places.far for r in order]
    return pick(term, jnp.stack(slots), [1] * len(order))


def whole_parts(term, places):
    lots = split_order(places.far)
    slots = []
    for core in (1, 0):
        slots += [places.block(r, n, core + c) for c in (2, 0) for n in (1, 0) for r in lots[0]]
        slots += [places.block(r, n, core + c) for n in (1, 0) for c in (2, 0) for r in lots[1]]
    return pick(term, jnp.stack(slots), [4 * places.far] * 2)


def near_swap(value, places):
    return lax.ppermute(value, "dp", swap_pairs(places.size, 1))


def member_swap(value, bit):
    return lax.ppermute(value, "fsdp", swap_pairs(4, bit))


def added(own, got):
    return (own.astype(F32) + got.astype(F32)).astype(BF16)


def far_sends(lot, blocks, places):
    return [
        lax.ppermute(blocks[k], "dp", far_pairs(places.size, r)) if r else blocks[k]
        for k, r in enumerate(lot)
    ]


def total_of(parts):
    total = parts[0].astype(F32)
    for part in parts[1:]:
        total = total + part.astype(F32)
    return total


class Rounds:
    def __init__(self):
        self.results = ()

    def enter(self, *values):
        kept = lax.optimization_barrier((values, self.results))[0]
        self.results = ()
        return kept

    def leave(self, *values):
        self.results += values
        return list(values) if len(values) > 1 else values[0]


def sum_steps(value, axis, size, bit=1, end=None):
    while bit < (end or size):
        value = value + lax.ppermute(value, axis, swap_pairs(size, bit))
        bit *= 2
    return value


def local(
    tokens,
    cotangent,
    seq_lengths,
    deal_order,
    attn_gain,
    w_query,
    w_key,
    w_value,
    q_gain,
    k_gain,
    w_out,
    ffn_gain,
    w_gate,
    w_up,
    w_down,
):
    rows, width = tokens.shape
    dp_size = lax.axis_size("dp")
    shard = w_gate.shape[0]
    ff_rows = w_down.shape[0]
    member = lax.axis_index("fsdp")

    lengths = seq_lengths[0]
    slots = jnp.arange(lengths.shape[0], dtype=jnp.int32)
    starts = jnp.sum(jnp.where(slots[None, :] < slots[:, None], lengths[None, :], 0), axis=1)
    row_ids = member * rows + jnp.arange(rows, dtype=jnp.int32)
    begun = starts[None, :] <= row_ids[:, None]
    row_start = jnp.max(jnp.where(begun, starts[None, :], 0), axis=1)
    row_place = row_ids - row_start
    rel = jnp.broadcast_to((row_start - member * rows)[:, None], (rows, LANES))
    frequency = 10000.0 ** (-2.0 * jnp.arange(HD // 2, dtype=F32) / HD)
    angles = row_place.astype(F32)[:, None] * frequency[None, :]
    cosine, sine = jnp.cos(angles), jnp.sin(angles)
    cosine = jnp.concatenate([cosine] * 4, axis=1)
    sine = jnp.concatenate([-sine, sine, -sine, sine], axis=1)
    head_gains = jnp.concatenate([jnp.tile(q_gain, HEADS), jnp.tile(k_gain, KV_HEADS)])
    head_gains = jnp.broadcast_to(head_gains.astype(F32)[None, :], (8, head_gains.shape[0]))

    places = Places(dp_size)
    gain_columns = jnp.pad(
        jnp.stack([attn_gain, ffn_gain], axis=1), ((0, 0), (0, LANES - 2))
    )
    w_qkv = jnp.concatenate([w_query, w_key, w_value, gain_columns], axis=1)
    far = places.far
    ff_block = -(-ff_rows * far // LANES) * LANES // far
    ff_width = far * ff_block
    me = places.me.reshape(1)
    turned = places.member // 2 * 4 + places.dp % 2 * 2 + places.member % 2
    units = split_units(w_gate, w_up, turned.reshape(1), far, ff_rows, ff_block)
    both_piece, last_units = exchange_units(units, places)
    both_piece = both_piece.reshape(8 * shard, 2 * ff_width)
    sends = far_order(far)
    lots = ([0] + sends[: far // 2 - 1], sends[far // 2 - 1 :])
    qkv_held = far_gather(w_qkv, places)
    out_held = far_gather(gated(w_out, qkv_held[sends[-1]]), places)
    out_mine = jnp.stack([out_held[r] for r in [0] + sends])
    mine_a, mine_b = (jnp.stack([qkv_held[r] for r in lot]) for lot in lots)
    pair_a = jnp.concatenate([mine_a, near_swap(mine_a, places)])
    pair_b = jnp.concatenate([mine_b, near_swap(gated(mine_b, out_mine), places)])
    across_a = member_swap(gated(pair_a, last_units), 2)
    out_pair = jnp.concatenate([out_mine, near_swap(gated(out_mine, pair_b), places)])
    across_b = member_swap(pair_b, 2)
    out_across = member_swap(gated(out_pair, across_b), 2)
    full_qkv = place(
        [
            blocks
            for pair, across in ((pair_a, across_a), (pair_b, across_b))
            for blocks in (pair, across, member_swap(pair, 1), member_swap(across, 1))
        ],
        whole_slots(lots, places),
    ).reshape(width, -1)

    down_piece = jnp.pad(w_down, ((0, ff_block - ff_rows), (0, 0)))
    gather_far = functools.partial(
        lax.all_gather, axis_name="dp", axis=0, tiled=True, axis_index_groups=places.groups
    )
    my_down = gather_far(gated(down_piece, qkv_held[sends[-1]]))
    my_both = gather_far(gated(both_piece, my_down))

    gain_table = full_qkv[:, full_qkv.shape[1] - LANES :]
    pick = (
        lax.broadcasted_iota(jnp.int32, (8, LANES), 0)
        == lax.broadcasted_iota(jnp.int32, (8, LANES), 1)
    ).astype(BF16)
    gain_rows = right_transposed(pick, gain_table)
    attn_row, ffn_row = gain_rows[0:1], gain_rows[1:2]
    x = tokens.astype(F32)
    x_inverse = lax.rsqrt(jnp.mean(x * x, axis=-1, keepdims=True) + EPSILON)
    normed = (x * x_inverse * attn_row).astype(BF16)
    pre = product(normed, full_qkv)
    queries, kv = head_prep(pre, cosine, sine, head_gains)
    ahead_one = [(i, i + 1) for i in range(3)]
    ahead_two = [(i, i + 2) for i in range(2)]
    kv = gated(kv, out_across)
    kv_one = lax.ppermute(kv, "fsdp", ahead_one)
    kv_two = lax.ppermute(kv, "fsdp", ahead_two)
    mixed = attend(queries, kv_two, kv_one, kv, rel)
    out_pair, out_across = gated((out_pair, out_across), kv_one)
    full_out = place(
        [out_pair, out_across, member_swap(out_pair, 1), member_swap(out_across, 1)],
        whole_slots([[0] + sends], places),
    ).reshape(-1, width)
    hidden = x + product(mixed, full_out)
    h_inverse = lax.rsqrt(jnp.mean(hidden * hidden, axis=-1, keepdims=True) + EPSILON)
    ffn_mine = (hidden * h_inverse * ffn_row).astype(BF16)

    upstream = gather_rows(cotangent, places, kv_one)
    ffn_low = gather_rows(ffn_mine, places)
    tile = 2 * rows
    act_low, slopes = feed(ffn_low, my_both, tile)
    order = sum(split_order(far), [])

    def parts_of(left, right):
        term = left_transposed(left, right).astype(BF16)
        return far_parts(term.reshape(far, -1, term.shape[1]), places)

    def far_sent(blocks, which):
        return [
            lax.ppermute(blocks[k], "dp", far_pairs(dp_size, order[k])) if order[k] else blocks[k]
            for k in which
        ]

    first, second = range(far // 2), range(far // 2, far)
    rounds = Rounds()

    *d_blocks, upstream, my_down, slopes = rounds.enter(
        *parts_of(act_low, upstream), upstream, my_down, slopes
    )
    d_first, d_second = far_sent(d_blocks, first), far_sent(d_blocks, second)
    rounds.leave(*d_first)
    grads, ffn_own, ffn_other = rounds.leave(
        *feed_back(upstream, my_down, slopes, my_both, rows, tile)
    )

    grads, ffn_own, ffn_other, act_low = rounds.enter(grads, ffn_own, ffn_other, act_low)
    grad_ffn = scatter_second(*scatter_first(ffn_own, ffn_other, places), places)
    grad_ffn = rounds.leave(grad_ffn)
    u_blocks = rounds.leave(*parts_of(ffn_low, grads))
    out_own, out_other = rounds.leave(
        *(
            product(part, my_down).astype(BF16).reshape(4, rows, width)
            for part in (act_low[: 4 * rows], act_low[4 * rows :])
        )
    )
    rounds.leave(*d_second)

    *u_blocks, grad_ffn, out_own, out_other = rounds.enter(
        *u_blocks, grad_ffn, out_own, out_other
    )
    u_first = far_sent(u_blocks, first)
    out_steps = rounds.leave(*scatter_first(out_own, out_other, places))
    e = grad_ffn * ffn_row
    slope = jnp.mean(hidden * e, axis=-1, keepdims=True)
    grad_hidden = cotangent.astype(F32) + h_inverse * e - hidden * (h_inverse**3 * slope)
    ffn_gain_term = jnp.sum(grad_ffn * hidden * h_inverse, axis=0)
    grad_hidden_low = grad_hidden.astype(BF16)
    grad_mixed = right_transposed(grad_hidden_low, full_out).astype(BF16)
    gq, gkv_two, gkv_one, gkv = rounds.leave(
        *attend_back(queries, kv_two, kv_one, kv, rel, grad_mixed)
    )
    grad_hidden_low = rounds.leave(grad_hidden_low)
    down_grad = rounds.leave(total_of(d_first + d_second)[0, :ff_rows])

    gkv_one, gkv_two, gq, gkv, grad_hidden_low, *out_steps = rounds.enter(
        gkv_one, gkv_two, gq, gkv, grad_hidden_low, *out_steps
    )
    got_one = lax.ppermute(gkv_one, "fsdp", [(b, a) for a, b in ahead_one])
    got_two = lax.ppermute(gkv_two, "fsdp", [(b, a) for a, b in ahead_two])
    output = rounds.leave((hidden + scatter_second(*out_steps, places)).astype(BF16))
    term_out = left_transposed(mixed, grad_hidden_low).astype(BF16)
    out_grad = lax.psum_scatter(term_out, BOTH, scatter_dimension=0, tiled=True).astype(F32)
    grad_pre, head_sums = head_back(gq, gkv, got_one, got_two, pre, cosine, sine, head_gains)
    term_qkv = left_transposed(normed, grad_pre).astype(BF16)
    q_other, q_own = rounds.leave(
        *whole_parts(term_qkv.reshape(4 * dp_size, shard, -1), places)
    )
    grad_pre = rounds.leave(grad_pre)
    rounds.leave(*u_first)

    u_blocks[far // 2], q_other, q_own, grad_pre = rounds.enter(
        u_blocks[far // 2], q_other, q_own, grad_pre
    )
    q_got = rounds.leave(member_swap(q_other, 1))
    u_second = far_sent(u_blocks, second)
    grad_normed = rounds.leave(right_transposed(grad_pre, full_qkv))

    half = 2 * far
    quarter, eighth = half // 2, half // 4
    q_a = added(q_own[:half], q_got[:half])
    q_b = added(q_own[half:], q_got[half:])
    q_a, q_b, grad_normed = rounds.enter(q_a, q_b, grad_normed)
    a_got = rounds.leave(member_swap(q_a[:quarter], 2))
    b_got = rounds.leave(near_swap(q_b[:quarter], places))
    e = grad_normed * attn_row
    slope = jnp.mean(x * e, axis=-1, keepdims=True)
    input_grad = grad_hidden + x_inverse * e - x * (x_inverse**3 * slope)
    input_grad = rounds.leave(input_grad.astype(BF16))
    attn_gain_term = jnp.sum(grad_normed * x * x_inverse, axis=0)
    small = jnp.concatenate([attn_gain_term, ffn_gain_term, head_sums.reshape(-1)])
    small = rounds.leave(small.reshape(-1, LANES))

    q_a, q_b = rounds.enter(added(q_a[quarter:], a_got), added(q_b[quarter:], b_got))
    a_got = rounds.leave(near_swap(q_a[:eighth], places))
    b_got = rounds.leave(member_swap(q_b[:eighth], 2))
    rounds.leave(*u_second)

    unit_sum = total_of(u_first + u_second)[0].astype(BF16).reshape(8, shard, 2 * ff_width)
    q_a, q_b = added(q_a[eighth:], a_got), added(q_b[eighth:], b_got)
    q_a, q_b, unit_sum, small = rounds.enter(q_a, q_b, unit_sum, small)
    q_parts = far_sends(order[: far // 2], q_a, places) + far_sends(order[far // 2 :], q_b, places)
    unit_all = rounds.leave(return_units(unit_sum, places))
    small = sum_steps(sum_steps(small, "fsdp", 4), "dp", dp_size).reshape(-1)
    qkv_grad = total_of(q_parts)
    gate_grad, up_grad = join_units(unit_all, me, far, ff_rows, ff_block)

    mine = (lax.axis_index("dp") * 4 + member) * shard
    attn_gain_grad = lax.dynamic_slice(small, (mine,), (shard,))
    ffn_gain_grad = lax.dynamic_slice(small, (width + mine,), (shard,))
    head_total = small[2 * width : 2 * width + 2 * LANES].reshape(2, 2, HD).sum(axis=1)

    q_end = HEADS * HD
    k_end = q_end + KV_HEADS * HD
    v_end = k_end + KV_HEADS * HD
    return (
        output,
        input_grad.astype(BF16),
        attn_gain_grad,
        qkv_grad[:, :q_end],
        qkv_grad[:, q_end:k_end],
        qkv_grad[:, k_end:v_end],
        head_total[0],
        head_total[1],
        out_grad,
        ffn_gain_grad,
        gate_grad,
        up_grad,
        down_grad,
    )


def solution(mesh):
    rows = P(BOTH, None)
    vector = P(BOTH)
    in_specs = (
        rows,
        rows,
        P("dp", None),
        P("dp", None),
        vector,
        rows,
        rows,
        rows,
        P(),
        P(),
        rows,
        vector,
        rows,
        rows,
        rows,
    )
    out_specs = (rows, rows, vector, rows, rows, rows, P(), P(), rows, vector, rows, rows, rows)
    return jax.shard_map(local, mesh=mesh, in_specs=in_specs, out_specs=out_specs, check_vma=False)
```

```python
import functools
import math

import jax
import jax.numpy as jnp
from jax import lax
from jax.experimental import pallas as pl
from jax.experimental.pallas import tpu as pltpu
from jax.sharding import PartitionSpec as P

HEADS = 24
KV_HEADS = 6
HD = 64
EPSILON = 1e-06
MASKED = -1e30
LANES = 128
BOTH = ("dp", "fsdp")
F32 = jnp.float32
BF16 = jnp.bfloat16
VMEM_LIMIT = 48 * 1024 * 1024


def product(left, right):
    return jnp.dot(left, right, preferred_element_type=F32)


def right_transposed(left, right):
    return lax.dot_general(left, right, (((1,), (1,)), ((), ())), preferred_element_type=F32)


def left_transposed(left, right):
    return lax.dot_general(left, right, (((0,), (0,)), ((), ())), preferred_element_type=F32)


def half_sums(values):
    rows = lax.broadcasted_iota(jnp.int32, (LANES, LANES), 0) // HD
    cols = lax.broadcasted_iota(jnp.int32, (LANES, LANES), 1) // HD
    same = (rows == cols).astype(F32)
    return jnp.dot(values, same, precision=lax.Precision.HIGHEST, preferred_element_type=F32)


def swapped_halves(values):
    lane = lax.broadcasted_iota(jnp.int32, values.shape, 1) % HD
    return jnp.where(
        lane < HD // 2, pltpu.roll(values, LANES - HD // 2, 1), pltpu.roll(values, HD // 2, 1)
    )


def head_prep_kernel(pre_ref, cos_ref, sin_ref, gain_ref, q_ref, kv_ref):
    q_blocks = HEADS * HD // LANES
    k_blocks = KV_HEADS * HD // LANES
    cosine, sine = cos_ref[...], sin_ref[...]
    for block in range(q_blocks + k_blocks):
        at = pl.ds(block * LANES, LANES)
        u = pre_ref[:, at]
        n = u * lax.rsqrt(half_sums(u * u) / HD + EPSILON) * gain_ref[:1, at]
        turned = n * cosine + swapped_halves(n) * sine
        if block < q_blocks:
            q_ref[:, at] = (turned.astype(BF16).astype(F32) * (1.0 / math.sqrt(HD))).astype(BF16)
        else:
            kv_ref[0, :, pl.ds((block - q_blocks) * LANES, LANES)] = turned.astype(BF16)
    v_at = (q_blocks + k_blocks) * LANES
    kv_ref[1] = pre_ref[:, v_at : v_at + k_blocks * LANES].astype(BF16)


def head_prep(pre, cosine, sine, gains):
    rows = pre.shape[0]
    return pl.pallas_call(
        head_prep_kernel,
        out_shape=(
            jax.ShapeDtypeStruct((rows, HEADS * HD), BF16),
            jax.ShapeDtypeStruct((2, rows, KV_HEADS * HD), BF16),
        ),
        compiler_params=pltpu.CompilerParams(vmem_limit_bytes=VMEM_LIMIT),
        name="head_prep",
    )(pre, cosine, sine, gains)


def head_back_kernel(
    gq_ref, gkv_ref, one_ref, two_ref, pre_ref, cos_ref, sin_ref, gain_ref, out_ref, sums_ref
):
    q_blocks = HEADS * HD // LANES
    k_blocks = KV_HEADS * HD // LANES
    cosine, sine = cos_ref[...], sin_ref[...]
    sums_ref[...] = jnp.zeros_like(sums_ref)
    for block in range(q_blocks + k_blocks):
        at = pl.ds(block * LANES, LANES)
        if block < q_blocks:
            g = gq_ref[:, at]
        else:
            k_at = pl.ds((block - q_blocks) * LANES, LANES)
            g = gkv_ref[0, :, k_at] + one_ref[0, :, k_at].astype(F32) + two_ref[0, :, k_at].astype(F32)
        g = g * cosine - swapped_halves(g) * sine
        u = pre_ref[:, at]
        inverse = lax.rsqrt(half_sums(u * u) / HD + EPSILON)
        unit = u * inverse
        row = 0 if block < q_blocks else 1
        sums_ref[row : row + 1, :] += jnp.sum(unit * g, axis=0, keepdims=True)
        e = g * gain_ref[:1, at]
        out_ref[:, at] = (inverse * (e - unit * (half_sums(e * unit) / HD))).astype(BF16)
    v_at = (q_blocks + k_blocks) * LANES
    width = k_blocks * LANES
    out_ref[:, v_at : v_at + width] = (
        gkv_ref[1] + one_ref[1].astype(F32) + two_ref[1].astype(F32)
    ).astype(BF16)
    tail = out_ref.shape[1] - v_at - width
    out_ref[:, v_at + width :] = jnp.zeros((out_ref.shape[0], tail), BF16)


def head_back(gq, gkv, one, two, pre, cosine, sine, gains):
    rows, width = pre.shape
    return pl.pallas_call(
        head_back_kernel,
        out_shape=(
            jax.ShapeDtypeStruct((rows, width), BF16),
            jax.ShapeDtypeStruct((8, LANES), F32),
        ),
        compiler_params=pltpu.CompilerParams(vmem_limit_bytes=VMEM_LIMIT),
        name="head_back",
    )(gq, gkv, one, two, pre, cosine, sine, gains)


def stacked_heads(ref, pair, repeat):
    return jnp.concatenate(
        [ref[:, pl.ds((pair * repeat + h) * HD, HD)] for h in range(repeat)], axis=0
    )


def window_probs(q4, keys, rel, repeat):
    rows, span = rel.shape[0], keys.shape[0]
    scores = right_transposed(q4, keys).reshape(repeat, rows, span)
    key_at = lax.broadcasted_iota(jnp.int32, (rows, span), 1) - (span - rows)
    row_at = lax.broadcasted_iota(jnp.int32, (rows, span), 0)
    allowed = (key_at <= row_at) & (key_at >= rel)
    scores = jnp.where(allowed[None], scores, MASKED)
    top = jnp.max(scores, axis=-1, keepdims=True)
    raised = jnp.exp(scores - top)
    return raised * (1.0 / jnp.sum(raised, axis=-1, keepdims=True))


def attend_kernel(q_ref, two_ref, one_ref, kv_ref, rel_ref, out_ref):
    repeat = HEADS // KV_HEADS
    rows = q_ref.shape[0]
    rel = rel_ref[:, :1]
    keys = jnp.concatenate([two_ref[0], one_ref[0], kv_ref[0]], axis=0)
    vals = jnp.concatenate([two_ref[1], one_ref[1], kv_ref[1]], axis=0)
    for pair in range(2):
        part = slice(pair * HD, (pair + 1) * HD)
        q4 = stacked_heads(q_ref, pair, repeat)
        probs = window_probs(q4, keys[:, part], rel, repeat)
        low = probs.astype(BF16).reshape(repeat * rows, -1)
        mixed = product(low, vals[:, part])
        for h in range(repeat):
            out_ref[:, pl.ds((pair * repeat + h) * HD, HD)] = mixed[
                h * rows : (h + 1) * rows
            ].astype(BF16)


def attend_specs(rows):
    q_spec = pl.BlockSpec((rows, HEADS * HD // 3), lambda g: (0, g))
    kv_spec = pl.BlockSpec((2, rows, LANES), lambda g: (0, 0, g))
    rel_spec = pl.BlockSpec((rows, LANES), lambda g: (0, 0))
    return q_spec, kv_spec, rel_spec


def attend(q, two, one, kv, rel):
    rows = q.shape[0]
    q_spec, kv_spec, rel_spec = attend_specs(rows)
    return pl.pallas_call(
        attend_kernel,
        grid=(3,),
        in_specs=[q_spec, kv_spec, kv_spec, kv_spec, rel_spec],
        out_specs=q_spec,
        out_shape=jax.ShapeDtypeStruct((rows, HEADS * HD), BF16),
        compiler_params=pltpu.CompilerParams(vmem_limit_bytes=VMEM_LIMIT),
        name="attend",
    )(q, two, one, kv, rel)


def attend_back_kernel(
    q_ref, two_ref, one_ref, kv_ref, rel_ref, gm_ref, gq_ref, gtwo_ref, gone_ref, gkv_ref
):
    repeat = HEADS // KV_HEADS
    rows = q_ref.shape[0]
    rel = rel_ref[:, :1]
    keys = jnp.concatenate([two_ref[0], one_ref[0], kv_ref[0]], axis=0)
    vals = jnp.concatenate([two_ref[1], one_ref[1], kv_ref[1]], axis=0)
    key_grads, val_grads = [], []
    for pair in range(2):
        part = slice(pair * HD, (pair + 1) * HD)
        q4 = stacked_heads(q_ref, pair, repeat)
        gm4 = stacked_heads(gm_ref, pair, repeat)
        probs = window_probs(q4, keys[:, part], rel, repeat)
        grad_probs = right_transposed(gm4, vals[:, part]).reshape(probs.shape)
        weighted = jnp.sum(probs * grad_probs, axis=-1, keepdims=True)
        span = probs.shape[-1]
        gs = (probs * (grad_probs - weighted)).astype(BF16).reshape(repeat * rows, span)
        low = probs.astype(BF16).reshape(repeat * rows, span)
        gq = product(gs, keys[:, part]) * (1.0 / math.sqrt(HD))
        for h in range(repeat):
            gq_ref[:, pl.ds((pair * repeat + h) * HD, HD)] = gq[h * rows : (h + 1) * rows]
        key_grads.append(product(q4.T, gs).T)
        val_grads.append(product(gm4.T, low).T)
    for at, parts in ((0, key_grads), (1, val_grads)):
        both = jnp.concatenate(parts, axis=1)
        gtwo_ref[at] = both[:rows].astype(gtwo_ref.dtype)
        gone_ref[at] = both[rows : 2 * rows].astype(gone_ref.dtype)
        gkv_ref[at] = both[2 * rows :]


def attend_back(q, two, one, kv, rel, gm):
    rows = q.shape[0]
    q_spec, kv_spec, rel_spec = attend_specs(rows)
    return pl.pallas_call(
        attend_back_kernel,
        grid=(3,),
        in_specs=[q_spec, kv_spec, kv_spec, kv_spec, rel_spec, q_spec],
        out_specs=(q_spec, kv_spec, kv_spec, kv_spec),
        out_shape=(
            jax.ShapeDtypeStruct((rows, HEADS * HD), F32),
            jax.ShapeDtypeStruct((2, rows, KV_HEADS * HD), BF16),
            jax.ShapeDtypeStruct((2, rows, KV_HEADS * HD), BF16),
            jax.ShapeDtypeStruct((2, rows, KV_HEADS * HD), F32),
        ),
        compiler_params=pltpu.CompilerParams(vmem_limit_bytes=VMEM_LIMIT),
        name="attend_back",
    )(q, two, one, kv, rel, gm)


def feed_kernel(x_ref, both_ref, act_ref, slopes_ref):
    units = act_ref.shape[1]
    mixed = product(x_ref[...], both_ref[...])
    gate, up = mixed[:, :units], mixed[:, units:]
    sig = 1.0 / (1.0 + jnp.exp(-gate))
    silu = gate * sig
    act_ref[...] = (silu * up).astype(BF16)
    slopes_ref[:, :units] = (up * sig * (1.0 + gate * (1.0 - sig))).astype(BF16)
    slopes_ref[:, units:] = silu.astype(BF16)


def feed(x, both, tile):
    rows, width = x.shape
    units = both.shape[1] // 2
    return pl.pallas_call(
        feed_kernel,
        grid=(rows // tile,),
        in_specs=[
            pl.BlockSpec((tile, width), lambda i: (i, 0)),
            pl.BlockSpec((width, 2 * units), lambda i: (0, 0)),
        ],
        out_specs=[
            pl.BlockSpec((tile, units), lambda i: (i, 0)),
            pl.BlockSpec((tile, 2 * units), lambda i: (i, 0)),
        ],
        out_shape=[
            jax.ShapeDtypeStruct((rows, units), BF16),
            jax.ShapeDtypeStruct((rows, 2 * units), BF16),
        ],
        compiler_params=pltpu.CompilerParams(vmem_limit_bytes=VMEM_LIMIT),
        cost_estimate=pl.CostEstimate(
            flops=4 * rows * width * units,
            transcendentals=rows * units,
            bytes_accessed=2 * (rows * width + 2 * width * units + 3 * rows * units),
        ),
        name="feed",
    )(x, both)


def feed_back_kernel(x_ref, down_ref, slopes_ref, both_ref, grads_ref, own_ref, other_ref):
    step, steps = pl.program_id(0), pl.num_programs(0)
    lots = own_ref.shape[0]
    grad_act = right_transposed(x_ref[...], down_ref[...])
    both_act = jnp.concatenate([grad_act, grad_act], axis=1)
    grads = (both_act * slopes_ref[...].astype(F32)).astype(BF16)
    grads_ref[...] = grads
    total = right_transposed(grads, both_ref[...])
    total = total.reshape(lots, -1, total.shape[1])

    total = total.astype(BF16)

    @pl.when(step < steps // 2)
    def _():
        own_ref[...] = total

    @pl.when(step >= steps // 2)
    def _():
        other_ref[...] = total


def feed_back(upstream, down, slopes, both, lot, tile):
    rows, width = upstream.shape
    units = down.shape[0]
    steps = rows // tile
    lots = rows // lot
    per = tile // lot
    return pl.pallas_call(
        feed_back_kernel,
        grid=(steps,),
        in_specs=[
            pl.BlockSpec((tile, width), lambda i: (i, 0)),
            pl.BlockSpec((units, width), lambda i: (0, 0)),
            pl.BlockSpec((tile, 2 * units), lambda i: (i, 0)),
            pl.BlockSpec((width, 2 * units), lambda i: (0, 0)),
        ],
        out_specs=[
            pl.BlockSpec((tile, 2 * units), lambda i: (i, 0)),
            pl.BlockSpec((per, lot, width), lambda i: (jnp.minimum(i, steps // 2 - 1), 0, 0)),
            pl.BlockSpec((per, lot, width), lambda i: (jnp.maximum(i - steps // 2, 0), 0, 0)),
        ],
        out_shape=[
            jax.ShapeDtypeStruct((rows, 2 * units), BF16),
            jax.ShapeDtypeStruct((lots // 2, lot, width), BF16),
            jax.ShapeDtypeStruct((lots // 2, lot, width), BF16),
        ],
        compiler_params=pltpu.CompilerParams(vmem_limit_bytes=VMEM_LIMIT),
        cost_estimate=pl.CostEstimate(
            flops=6 * rows * width * units,
            transcendentals=0,
            bytes_accessed=2 * (3 * rows * width + 3 * width * units + 4 * rows * units),
        ),
        name="feed_back",
    )(upstream, down, slopes, both)


def lane_window(read, tiles, start):
    tile, shift = start // LANES, start % LANES
    first = read(min(max(tile, 0), tiles - 1))
    if shift == 0:
        return first
    second = read(min(max(tile + 1, 0), tiles - 1))
    lane = lax.broadcasted_iota(jnp.int32, first.shape, 1)
    return jnp.where(
        lane < LANES - shift,
        pltpu.roll(first, LANES - shift, 1),
        pltpu.roll(second, LANES - shift, 1),
    )


def lane_runs(target, runs, source_of):
    total = None
    for first, length, source in runs:
        low, high = max(first, target), min(first + length, target + LANES)
        if low >= high:
            continue
        window = source_of(source, target - first)
        lane = lax.broadcasted_iota(jnp.int32, window.shape, 1) + target
        kept = jnp.where((lane >= low) & (lane < high), window, 0.0)
        total = kept if total is None else total + kept
    return total


def split_kernel(far, unit, block, me_ref, gate_ref, up_ref, out_ref):
    units = far * block
    tiles = -(-gate_ref.shape[1] // LANES)
    for at, ref in ((0, gate_ref), (units, up_ref)):
        for part in range(8):
            runs = [(d * block, unit, (8 * d + part) * unit) for d in range(far)]

            def source_of(source, offset):
                read = lambda t: ref[:, t * LANES : (t + 1) * LANES].astype(F32)
                return lane_window(read, tiles, source + offset)

            for target in range(0, units, LANES):
                value = lane_runs(target, runs, source_of)
                to = pl.ds(at + target, LANES)
                turned = part // 2 % 2 * 4 + part // 4 * 2 + part % 2
                out_ref[turned ^ me_ref[0], :, to] = value.astype(BF16)


def split_units(gate, up, me, far, unit, block):
    return pl.pallas_call(
        functools.partial(split_kernel, far, unit, block),
        in_specs=[
            pl.BlockSpec(memory_space=pltpu.SMEM),
            pl.BlockSpec(memory_space=pltpu.VMEM),
            pl.BlockSpec(memory_space=pltpu.VMEM),
        ],
        out_shape=jax.ShapeDtypeStruct((8, gate.shape[0], 2 * far * block), BF16),
        compiler_params=pltpu.CompilerParams(vmem_limit_bytes=VMEM_LIMIT),
        name="split_units",
    )(me, gate, up)


def join_kernel(far, unit, block, me_ref, got_ref, gate_ref, up_ref):
    units = far * block
    tiles = got_ref.shape[2] // LANES
    runs = [
        ((8 * d + part) * unit, unit, (part, d * block)) for d in range(far) for part in range(8)
    ]
    for at, ref in ((0, gate_ref), (units, up_ref)):

        def source_of(source, offset):
            read = lambda t: got_ref[
                source[0] ^ me_ref[0], :, t * LANES : (t + 1) * LANES
            ].astype(F32)
            return lane_window(read, tiles, at + source[1] + offset)

        for target in range(0, ref.shape[1], LANES):
            ref[:, target : target + LANES] = lane_runs(target, runs, source_of)


def join_units(got, me, far, unit, block):
    out = jax.ShapeDtypeStruct((got.shape[1], 8 * far * unit), F32)
    return pl.pallas_call(
        functools.partial(join_kernel, far, unit, block),
        in_specs=[
            pl.BlockSpec(memory_space=pltpu.SMEM),
            pl.BlockSpec(memory_space=pltpu.VMEM),
        ],
        out_shape=[out, out],
        compiler_params=pltpu.CompilerParams(vmem_limit_bytes=VMEM_LIMIT),
        name="join_units",
    )(me, got)


def swap_pairs(size, bit):
    return [(i, i ^ bit) for i in range(size)]


def far_pairs(size, shift):
    far = size // 2
    return [(i, (i // 2 + shift) % far * 2 + i % 2) for i in range(size)]


def far_order(far):
    order = []
    for step in range(1, far // 2 + 1):
        order.append(step)
        if far - step != step:
            order.append(far - step)
    return order


def place_kernel(counts, slots, *refs):
    pieces, out, held, come, gone = refs[: len(counts)], *refs[len(counts) :]
    arrivals, departures = [], []
    for piece, count in zip(pieces, counts):
        for k in range(count):
            at = len(arrivals)
            arrivals.append(pltpu.make_async_copy(piece.at[k], held.at[at], come.at[at]))
            departures.append(pltpu.make_async_copy(held.at[at], out.at[slots[at]], gone.at[at]))
    for copy in arrivals:
        copy.start()
    for arrival, departure in zip(arrivals, departures):
        arrival.wait()
        departure.start()
    for copy in departures:
        copy.wait()


def place(pieces, slots):
    counts = [piece.shape[0] for piece in pieces]
    total = sum(counts)
    shape = (total,) + pieces[0].shape[1:]
    moved = 2 * math.prod(shape) * pieces[0].dtype.itemsize
    return pl.pallas_call(
        functools.partial(place_kernel, counts),
        in_specs=[pl.BlockSpec(memory_space=pltpu.SMEM)]
        + [pl.BlockSpec(memory_space=pl.ANY)] * len(pieces),
        out_specs=pl.BlockSpec(memory_space=pl.ANY),
        out_shape=jax.ShapeDtypeStruct(shape, pieces[0].dtype),
        scratch_shapes=[
            pltpu.VMEM(shape, pieces[0].dtype),
            pltpu.SemaphoreType.DMA((total,)),
            pltpu.SemaphoreType.DMA((total,)),
        ],
        compiler_params=pltpu.CompilerParams(vmem_limit_bytes=VMEM_LIMIT),
        cost_estimate=pl.CostEstimate(flops=0, transcendentals=0, bytes_accessed=moved),
        name="place",
    )(slots, *pieces)


def pick_kernel(counts, slots, source, *refs):
    outs, (held, come, gone) = refs[: len(counts)], refs[len(counts) :]
    arrivals, departures = [], []
    for out, count in zip(outs, counts):
        for k in range(count):
            at = len(arrivals)
            arrivals.append(pltpu.make_async_copy(source.at[slots[at]], held.at[at], come.at[at]))
            departures.append(pltpu.make_async_copy(held.at[at], out.at[k], gone.at[at]))
    for copy in arrivals:
        copy.start()
    for arrival, departure in zip(arrivals, departures):
        arrival.wait()
        departure.start()
    for copy in departures:
        copy.wait()


def pick(source, slots, counts):
    total = sum(counts)
    block = source.shape[1:]
    moved = 2 * total * math.prod(block) * source.dtype.itemsize
    return pl.pallas_call(
        functools.partial(pick_kernel, counts),
        in_specs=[pl.BlockSpec(memory_space=pltpu.SMEM), pl.BlockSpec(memory_space=pl.ANY)],
        out_specs=[pl.BlockSpec(memory_space=pl.ANY)] * len(counts),
        out_shape=[jax.ShapeDtypeStruct((n,) + block, source.dtype) for n in counts],
        scratch_shapes=[
            pltpu.VMEM((total,) + block, source.dtype),
            pltpu.SemaphoreType.DMA((total,)),
            pltpu.SemaphoreType.DMA((total,)),
        ],
        compiler_params=pltpu.CompilerParams(vmem_limit_bytes=VMEM_LIMIT),
        cost_estimate=pl.CostEstimate(flops=0, transcendentals=0, bytes_accessed=moved),
        name="pick",
    )(slots, source)


class Places:
    def __init__(self, dp_size):
        self.size, self.far = dp_size, dp_size // 2
        self.dp, self.member = lax.axis_index("dp"), lax.axis_index("fsdp")
        self.me = self.dp % 2 * 4 + self.member
        self.groups = [[2 * z + y for z in range(self.far)] for y in range(2)]

    def near_block(self, shift, near):
        return (self.dp // 2 + self.far + shift) % self.far * 2 + self.dp % 2 * (1 - near) + (
            1 - self.dp % 2
        ) * near

    def block(self, shift, near, member):
        return self.near_block(shift, near) * 4 + (self.member ^ member)


def far_gather(piece, places):
    held = {0: piece}
    for r in far_order(places.far):
        held[r] = lax.ppermute(piece, "dp", far_pairs(places.size, r))
    return held


def plane_first(mine, places):
    half = mine.shape[0] // 2
    first, second = mine[:half], mine[half:]
    near, across = near_swap(first, places), member_swap(second, 2)
    return jnp.concatenate([first, near]), jnp.concatenate([second, across])


def plane_second(first, second, places):
    across, near = member_swap(first, 2), near_swap(second, places)
    return jnp.concatenate([first, across]), jnp.concatenate([second, near])


def plane_last(first, second, sends, places):
    half = places.far // 2
    lots = [0, *sends][:half], [0, *sends][half:]
    slots = [
        places.block(-r, inner, 2 * outer + core)
        for core in (0, 1)
        for outer in (0, 1)
        for inner in (0, 1)
        for r in lots[0]
    ]
    later = [
        places.block(-r, outer, 2 * inner + core)
        for core in (0, 1)
        for outer in (0, 1)
        for inner in (0, 1)
        for r in lots[1]
    ]
    blocks = [first, member_swap(first, 1), second, member_swap(second, 1)]
    return place(blocks, jnp.stack(slots + later))


def gated(value, gate):
    return value if gate is None else lax.optimization_barrier((value, gate))[0]


def exchange_chips(parts):
    return jnp.stack([parts[:4], member_swap(parts[4:], 2)])


def exchange_near(parts, places):
    return jnp.stack([parts[:, :2], near_swap(parts[:, 2:], places)])


def exchange_units(parts, places):
    beside = member_swap(parts[:, :, 1], 1)
    own = parts[:, :, 0]
    blocks = [own.reshape(4, *own.shape[2:]), beside.reshape(4, *own.shape[2:])]
    slots = [
        places.me ^ (4 * near + 2 * chip + core)
        for core in (0, 1)
        for near in (0, 1)
        for chip in (0, 1)
    ]
    return place(blocks, jnp.stack(slots))


def return_core(blocks, places):
    slots = [
        places.me ^ (4 * near + 2 * chip + core)
        for core in (1, 0)
        for chip in (1, 0)
        for near in (1, 0)
    ]
    other, own = pick(blocks, jnp.stack(slots), [4, 4])
    return jnp.stack([own, member_swap(other, 1)])


def return_units(held, places):
    across = member_swap(held[:, :2], 2)
    held = jnp.stack([held[:, 2:], across])
    near = near_swap(held[:, :, 0], places)
    held = jnp.stack([held[:, :, 1], near])
    return held.reshape(8, *held.shape[3:])


def assemble_kernel(*refs):
    pieces, (out, held, come, gone) = refs[:-4], refs[-4:]
    half = out.shape[2] // 2
    arrivals, departures = [], []
    for k, piece in enumerate(pieces):
        core, at = k // 5, k % 5
        columns = pl.ds(0, 2 * half) if at < 3 else pl.ds((at - 3) * half, half)
        spot = (core * 4 + min(at, 3), slice(None), columns)
        arrivals.append(pltpu.make_async_copy(piece, held.at[spot], come.at[k]))
        departures.append(pltpu.make_async_copy(held.at[spot], out.at[spot], gone.at[k]))
    for copy in arrivals:
        copy.start()
    for arrival, departure in zip(arrivals, departures):
        arrival.wait()
        departure.start()
    for copy in departures:
        copy.wait()


def assemble(pieces):
    rows, width = pieces[0].shape
    shape = (8, rows, width)
    return pl.pallas_call(
        assemble_kernel,
        in_specs=[pl.BlockSpec(memory_space=pl.ANY)] * len(pieces),
        out_specs=pl.BlockSpec(memory_space=pl.ANY),
        out_shape=jax.ShapeDtypeStruct(shape, BF16),
        scratch_shapes=[
            pltpu.VMEM(shape, BF16),
            pltpu.SemaphoreType.DMA((len(pieces),)),
            pltpu.SemaphoreType.DMA((len(pieces),)),
        ],
        compiler_params=pltpu.CompilerParams(vmem_limit_bytes=VMEM_LIMIT),
        cost_estimate=pl.CostEstimate(
            flops=0, transcendentals=0, bytes_accessed=4 * math.prod(shape)
        ),
        name="assemble",
    )(*pieces)


def gather_first(rows, places):
    return rows, member_swap(rows, 2), near_swap(rows, places)


def gather_second(rows, across, near, places):
    half = rows.shape[1] // 2
    left = near_swap(across[:, :half], places)
    right = member_swap(near[:, half:], 2)
    return rows, across, near, left, right


def gather_last(*pieces):
    out = assemble([*pieces, *(member_swap(piece, 1) for piece in pieces)])
    return out.reshape(-1, out.shape[2])


def merge_kernel(own_ref, got_ref, near_ref, across_ref, left_ref, right_ref):
    half = own_ref.shape[2] // 2
    left, right = pl.ds(0, half), pl.ds(half, half)

    def total(lot, columns):
        return own_ref[lot, :, columns].astype(F32) + got_ref[lot, :, columns].astype(F32)

    for k, lot in enumerate((2, 3)):
        near_ref[k] = total(lot, left).astype(BF16)
    for k, lot in enumerate((1, 3)):
        across_ref[k] = total(lot, right).astype(BF16)
    for k, lot in enumerate((0, 1)):
        left_ref[k] = total(lot, left)
    for k, lot in enumerate((0, 2)):
        right_ref[k] = total(lot, right)


def merge(own, got):
    shape = (2, own.shape[1], own.shape[2] // 2)
    low, wide = jax.ShapeDtypeStruct(shape, BF16), jax.ShapeDtypeStruct(shape, F32)
    return pl.pallas_call(
        merge_kernel,
        out_shape=[low, low, wide, wide],
        compiler_params=pltpu.CompilerParams(vmem_limit_bytes=VMEM_LIMIT),
        cost_estimate=pl.CostEstimate(
            flops=own.size, transcendentals=0, bytes_accessed=7 * own.size
        ),
        name="merge",
    )(own, got)


def scatter_first(own, other, places):
    near, across, left, right = merge(own, member_swap(other, 1))
    near, across = near_swap(near, places), member_swap(across, 2)
    return left, near, right, across


def scatter_second(left, near, right, across, places):
    left_out = (left[1] + near[1].astype(F32)).astype(BF16)
    right_out = (right[1] + across[1].astype(F32)).astype(BF16)
    left_got, right_got = member_swap(left_out, 2), near_swap(right_out, places)
    left = left[0] + near[0].astype(F32) + left_got.astype(F32)
    right = right[0] + across[0].astype(F32) + right_got.astype(F32)
    return jnp.concatenate([left, right], axis=1)


def split_order(far):
    order = far_order(far) + [0]
    return order[: far // 2], order[far // 2 :]


def far_parts(term, places, cut=1):
    order = sum(split_order(places.far), [])
    slots = [(places.dp // 2 + r) % places.far * cut + k for r in order for k in range(cut)]
    return pick(term, jnp.stack(slots), [1] * len(slots))


def whole_parts(term, places):
    lots = split_order(places.far)
    slots = []
    for core in (1, 0):
        slots += [places.block(r, n, core + c) for c in (2, 0) for n in (1, 0) for r in lots[0]]
        slots += [places.block(r, n, core + c) for n in (1, 0) for c in (2, 0) for r in lots[1]]
    return pick(term, jnp.stack(slots), [4 * places.far] * 2)


def near_swap(value, places):
    return lax.ppermute(value, "dp", swap_pairs(places.size, 1))


def member_swap(value, bit):
    return lax.ppermute(value, "fsdp", swap_pairs(4, bit))


def added(own, got):
    return (own.astype(F32) + got.astype(F32)).astype(BF16)


def added_parts(own, got, cut):
    return added(own[:cut], got[:cut]), added(own[cut:], got[cut:])


def far_sends(lot, blocks, places):
    return [
        lax.ppermute(blocks[k], "dp", far_pairs(places.size, r)) if r else blocks[k]
        for k, r in enumerate(lot)
    ]


def total_of(parts):
    total = parts[0].astype(F32)
    for part in parts[1:]:
        total = total + part.astype(F32)
    return total


class Rounds:
    def __init__(self):
        self.results = ()

    def enter(self, *values):
        kept = lax.optimization_barrier((values, self.results))[0]
        self.results = ()
        return kept

    def leave(self, *values):
        self.results += values
        return list(values) if len(values) > 1 else values[0]


def sum_steps(value, axis, size, bit=1, end=None):
    while bit < (end or size):
        value = value + lax.ppermute(value, axis, swap_pairs(size, bit))
        bit *= 2
    return value


def local(
    tokens,
    cotangent,
    seq_lengths,
    deal_order,
    attn_gain,
    w_query,
    w_key,
    w_value,
    q_gain,
    k_gain,
    w_out,
    ffn_gain,
    w_gate,
    w_up,
    w_down,
):
    rows, width = tokens.shape
    dp_size = lax.axis_size("dp")
    shard = w_gate.shape[0]
    ff_rows = w_down.shape[0]
    member = lax.axis_index("fsdp")

    lengths = seq_lengths[0]
    slots = jnp.arange(lengths.shape[0], dtype=jnp.int32)
    starts = jnp.sum(jnp.where(slots[None, :] < slots[:, None], lengths[None, :], 0), axis=1)
    row_ids = member * rows + jnp.arange(rows, dtype=jnp.int32)
    begun = starts[None, :] <= row_ids[:, None]
    row_start = jnp.max(jnp.where(begun, starts[None, :], 0), axis=1)
    row_place = row_ids - row_start
    rel = jnp.broadcast_to((row_start - member * rows)[:, None], (rows, LANES))
    frequency = 10000.0 ** (-2.0 * jnp.arange(HD // 2, dtype=F32) / HD)
    angles = row_place.astype(F32)[:, None] * frequency[None, :]
    cosine, sine = jnp.cos(angles), jnp.sin(angles)
    cosine = jnp.concatenate([cosine] * 4, axis=1)
    sine = jnp.concatenate([-sine, sine, -sine, sine], axis=1)
    head_gains = jnp.concatenate([jnp.tile(q_gain, HEADS), jnp.tile(k_gain, KV_HEADS)])
    head_gains = jnp.broadcast_to(head_gains.astype(F32)[None, :], (8, head_gains.shape[0]))

    places = Places(dp_size)
    gain_columns = jnp.pad(
        jnp.stack([attn_gain, ffn_gain], axis=1), ((0, 0), (0, LANES - 2))
    )
    w_qkv = jnp.concatenate([w_query, w_key, w_value, gain_columns], axis=1)

    far = places.far
    ff_block = -(-ff_rows * far // LANES) * LANES // far
    ff_width = far * ff_block
    me = places.me.reshape(1)
    turned = places.member // 2 * 4 + places.dp % 2 * 2 + places.member % 2
    units = split_units(w_gate, w_up, turned.reshape(1), far, ff_rows, ff_block)
    sends = far_order(far)
    gather_far = functools.partial(
        lax.all_gather, axis_name="dp", axis=0, tiled=True, axis_index_groups=places.groups
    )

    rounds = Rounds()
    qkv_held = far_gather(w_qkv, places)
    qkv_mine = rounds.leave(jnp.stack([qkv_held[r] for r in [0] + sends]))
    units = rounds.leave(exchange_near(exchange_chips(units), places))

    qkv_mine, late_out, units, down_piece = rounds.enter(qkv_mine, w_out, units, w_down)
    out_held = far_gather(late_out, places)
    out_mine = rounds.leave(jnp.stack([out_held[r] for r in [0] + sends]))
    qkv_a, qkv_b = plane_first(qkv_mine, places)
    qkv_a, qkv_b = rounds.leave(qkv_a, qkv_b)
    down_piece = jnp.pad(down_piece, ((0, ff_block - ff_rows), (0, 0)))
    my_down = gather_far(down_piece)
    both_piece = rounds.leave(exchange_units(units, places))

    qkv_a, qkv_b, out_mine, both_piece = rounds.enter(qkv_a, qkv_b, out_mine, both_piece)
    qkv_a, qkv_b = rounds.leave(*plane_second(qkv_a, qkv_b, places))
    out_a, out_b = rounds.leave(*plane_first(out_mine, places))
    my_both = gather_far(both_piece.reshape(8 * shard, 2 * ff_width))

    qkv_a, qkv_b, out_a, out_b = rounds.enter(qkv_a, qkv_b, out_a, out_b)
    full_qkv = plane_last(qkv_a, qkv_b, sends, places).reshape(width, -1)
    out_a, out_b = plane_second(*gated((out_a, out_b), full_qkv), places)
    full_qkv = gated(full_qkv, my_down)

    gain_table = full_qkv[:, full_qkv.shape[1] - LANES :]
    pick = (
        lax.broadcasted_iota(jnp.int32, (8, LANES), 0)
        == lax.broadcasted_iota(jnp.int32, (8, LANES), 1)
    ).astype(BF16)
    gain_rows = right_transposed(pick, gain_table)
    attn_row, ffn_row = gain_rows[0:1], gain_rows[1:2]
    x = tokens.astype(F32)
    x_inverse = lax.rsqrt(jnp.mean(x * x, axis=-1, keepdims=True) + EPSILON)
    normed = (x * x_inverse * attn_row).astype(BF16)
    pre = product(normed, full_qkv)
    queries, kv = head_prep(pre, cosine, sine, head_gains)
    ahead_one = [(i, i + 1) for i in range(3)]
    ahead_two = [(i, i + 2) for i in range(2)]
    kv = gated(kv, (out_a, out_b))
    kv_one = lax.ppermute(kv, "fsdp", ahead_one)
    kv_two = lax.ppermute(kv, "fsdp", ahead_two)
    pieces = gather_first(gated(cotangent, kv_two), places)
    mixed = attend(queries, kv_two, kv_one, kv, rel)
    out_a, out_b, _ = gated((out_a, out_b, kv_one), kv_two)
    full_out = plane_last(out_a, out_b, sends, places).reshape(-1, width)
    pieces = gather_second(*gated(pieces, mixed), places)
    hidden = x + product(mixed, full_out)
    h_inverse = lax.rsqrt(jnp.mean(hidden * hidden, axis=-1, keepdims=True) + EPSILON)
    ffn_mine = (hidden * h_inverse * ffn_row).astype(BF16)

    ffn_pieces = gather_first(gated(ffn_mine, pieces), places)
    upstream = gather_last(*pieces)
    ffn_low = gather_last(*gather_second(*gated(ffn_pieces, upstream), places))
    tile = 2 * rows
    act_low, slopes = feed(ffn_low, my_both, tile)
    order = sum(split_order(far), [])

    def parts_of(left, right, cut=1):
        term = left_transposed(left, right).astype(BF16)
        return far_parts(term.reshape(far * cut, -1, term.shape[1]), places, cut)

    def far_sent(blocks, which, cut=1):
        return [
            lax.ppermute(blocks[k], "dp", far_pairs(dp_size, order[k // cut]))
            if order[k // cut]
            else blocks[k]
            for k in which
        ]

    first, second = range(far // 2), range(far // 2, far)
    sent = 2 * (far - 1)
    cut_a = sent // 2
    rounds = Rounds()

    *d_blocks, upstream, my_down, slopes = rounds.enter(
        *parts_of(act_low, upstream), upstream, my_down, slopes
    )
    d_first, d_second = far_sent(d_blocks, first), far_sent(d_blocks, second)
    rounds.leave(*d_first)
    grads, ffn_own, ffn_other = rounds.leave(
        *feed_back(upstream, my_down, slopes, my_both, rows, tile)
    )

    grads, ffn_own, ffn_other, act_low = rounds.enter(grads, ffn_own, ffn_other, act_low)
    grad_ffn = scatter_second(*scatter_first(ffn_own, ffn_other, places), places)
    grad_ffn = rounds.leave(grad_ffn)
    u_blocks = rounds.leave(*parts_of(ffn_low, grads, 2))
    out_own, out_other = rounds.leave(
        *(
            product(part, my_down).astype(BF16).reshape(4, rows, width)
            for part in (act_low[: 4 * rows], act_low[4 * rows :])
        )
    )
    rounds.leave(*d_second)

    *u_blocks, grad_ffn, out_own, out_other = rounds.enter(
        *u_blocks, grad_ffn, out_own, out_other
    )
    u_got = rounds.leave(*far_sent(u_blocks, range(cut_a), 2))
    out_steps = rounds.leave(*scatter_first(out_own, out_other, places))
    e = grad_ffn * ffn_row
    slope = jnp.mean(hidden * e, axis=-1, keepdims=True)
    grad_hidden = cotangent.astype(F32) + h_inverse * e - hidden * (h_inverse**3 * slope)
    ffn_gain_term = jnp.sum(grad_ffn * hidden * h_inverse, axis=0)
    grad_hidden_low = grad_hidden.astype(BF16)
    grad_mixed = right_transposed(grad_hidden_low, full_out).astype(BF16)
    gq, gkv_two, gkv_one, gkv = rounds.leave(
        *attend_back(queries, kv_two, kv_one, kv, rel, grad_mixed)
    )
    term_out = left_transposed(mixed, grad_hidden_low).astype(BF16)
    term_out = rounds.leave(term_out)
    down_grad = rounds.leave(total_of(d_first + d_second)[0, :ff_rows])

    u_blocks[sent - 2], gkv_one, gkv_two, gq, gkv, term_out, *out_steps = rounds.enter(
        u_blocks[sent - 2], gkv_one, gkv_two, gq, gkv, term_out, *out_steps
    )
    out_grad = lax.psum_scatter(term_out, BOTH, scatter_dimension=0, tiled=True).astype(F32)
    u_near = far_sent(u_blocks, [sent - 2], 2)
    rounds.leave(*u_near)
    got_one = lax.ppermute(gkv_one, "fsdp", [(b, a) for a, b in ahead_one])
    got_two = lax.ppermute(gkv_two, "fsdp", [(b, a) for a, b in ahead_two])
    output = rounds.leave((hidden + scatter_second(*out_steps, places)).astype(BF16))
    half = 2 * far
    quarter, eighth = half // 2, half // 4
    grad_pre, head_sums = head_back(gq, gkv, got_one, got_two, pre, cosine, sine, head_gains)
    term_qkv = left_transposed(normed, grad_pre).astype(BF16)
    q_other, q_own = rounds.leave(
        *whole_parts(term_qkv.reshape(4 * dp_size, shard, -1), places)
    )
    grad_pre = rounds.leave(grad_pre)

    u_blocks[cut_a], q_other, q_own, grad_pre = rounds.enter(
        u_blocks[cut_a], q_other, q_own, grad_pre
    )
    q_got = rounds.leave(member_swap(q_other, 1))
    middle = range(cut_a, sent - 2)
    u_middle = rounds.leave(far_sent(u_blocks, middle, 2))
    grad_normed = rounds.leave(right_transposed(grad_pre, full_qkv))

    a_out, q_a = added_parts(q_own[:half], q_got[:half], quarter)
    b_out, q_b = added_parts(q_own[half:], q_got[half:], quarter)
    u_blocks[sent - 1], a_out, b_out, grad_normed = rounds.enter(
        u_blocks[sent - 1], a_out, b_out, grad_normed
    )
    last = range(sent - 1, sent + 2)
    u_last = rounds.leave(far_sent(u_blocks, last, 2))
    a_got = rounds.leave(member_swap(a_out, 2))
    b_got = rounds.leave(near_swap(b_out, places))
    e = grad_normed * attn_row
    slope = jnp.mean(x * e, axis=-1, keepdims=True)
    input_grad = grad_hidden + x_inverse * e - x * (x_inverse**3 * slope)
    input_grad = rounds.leave(input_grad.astype(BF16))
    attn_gain_term = jnp.sum(grad_normed * x * x_inverse, axis=0)
    small = jnp.concatenate([attn_gain_term, ffn_gain_term, head_sums.reshape(-1)])
    small = rounds.leave(small.reshape(-1, LANES))

    u_got = dict(enumerate(u_got)) | {sent - 2: u_near[0]}
    u_got |= dict(zip(middle, u_middle)) | dict(zip(last, u_last))

    a_out, q_a = added_parts(q_a, a_got, eighth)
    b_out, q_b = added_parts(q_b, b_got, eighth)
    unit_sum = jnp.concatenate(
        [total_of([u_got[2 * r + k] for r in range(far)]) for k in range(2)], axis=1
    )
    unit_sum = unit_sum.astype(BF16).reshape(8, shard, 2 * ff_width)
    a_out, b_out, small, unit_sum = rounds.enter(a_out, b_out, small, unit_sum)
    a_got = rounds.leave(near_swap(a_out, places))
    b_got = rounds.leave(member_swap(b_out, 2))
    small = sum_steps(small, "fsdp", 4, 1, 2)
    small = rounds.leave(sum_steps(small, "dp", dp_size, 2))
    units = rounds.leave(return_core(unit_sum, places))

    q_a, q_b = added(q_a, a_got), added(q_b, b_got)
    q_a, q_b, small, units = rounds.enter(q_a, q_b, small, units)
    q_parts = far_sends(order[: far // 2], q_a, places) + far_sends(order[far // 2 :], q_b, places)
    unit_all = return_units(units, places)
    small = sum_steps(sum_steps(small, "fsdp", 4, 2), "dp", dp_size, 1, 2).reshape(-1)
    qkv_grad = total_of(q_parts)
    unit_all = gated(unit_all, out_grad)
    gate_grad, up_grad = join_units(unit_all, me, far, ff_rows, ff_block)

    mine = (lax.axis_index("dp") * 4 + member) * shard
    attn_gain_grad = lax.dynamic_slice(small, (mine,), (shard,))
    ffn_gain_grad = lax.dynamic_slice(small, (width + mine,), (shard,))
    head_total = small[2 * width : 2 * width + 2 * LANES].reshape(2, 2, HD).sum(axis=1)

    q_end = HEADS * HD
    k_end = q_end + KV_HEADS * HD
    v_end = k_end + KV_HEADS * HD
    return (
        output,
        input_grad.astype(BF16),
        attn_gain_grad,
        qkv_grad[:, :q_end],
        qkv_grad[:, q_end:k_end],
        qkv_grad[:, k_end:v_end],
        head_total[0],
        head_total[1],
        out_grad,
        ffn_gain_grad,
        gate_grad,
        up_grad,
        down_grad,
    )


def solution(mesh):
    rows = P(BOTH, None)
    vector = P(BOTH)
    in_specs = (
        rows,
        rows,
        P("dp", None),
        P("dp", None),
        vector,
        rows,
        rows,
        rows,
        P(),
        P(),
        rows,
        vector,
        rows,
        rows,
        rows,
    )
    out_specs = (rows, rows, vector, rows, rows, rows, P(), P(), rows, vector, rows, rows, rows)
    return jax.shard_map(local, mesh=mesh, in_specs=in_specs, out_specs=out_specs, check_vma=False)
```

```python
import functools
import math

import jax
import jax.numpy as jnp
from jax import lax
from jax.experimental import pallas as pl
from jax.experimental.pallas import tpu as pltpu
from jax.sharding import PartitionSpec as P

HEADS = 24
KV_HEADS = 6
HD = 64
EPSILON = 1e-06
MASKED = -1e30
LANES = 128
BOTH = ("dp", "fsdp")
F32 = jnp.float32
BF16 = jnp.bfloat16
VMEM_LIMIT = 48 * 1024 * 1024


def product(left, right):
    return jnp.dot(left, right, preferred_element_type=F32)


def right_transposed(left, right):
    return lax.dot_general(left, right, (((1,), (1,)), ((), ())), preferred_element_type=F32)


def left_transposed(left, right):
    return lax.dot_general(left, right, (((0,), (0,)), ((), ())), preferred_element_type=F32)


def half_sums(values):
    rows = lax.broadcasted_iota(jnp.int32, (LANES, LANES), 0) // HD
    cols = lax.broadcasted_iota(jnp.int32, (LANES, LANES), 1) // HD
    same = (rows == cols).astype(F32)
    return jnp.dot(values, same, precision=lax.Precision.HIGHEST, preferred_element_type=F32)


def swapped_halves(values):
    lane = lax.broadcasted_iota(jnp.int32, values.shape, 1) % HD
    return jnp.where(
        lane < HD // 2, pltpu.roll(values, LANES - HD // 2, 1), pltpu.roll(values, HD // 2, 1)
    )


def head_prep_kernel(pre_ref, cos_ref, sin_ref, gain_ref, q_ref, kv_ref):
    q_blocks = HEADS * HD // LANES
    k_blocks = KV_HEADS * HD // LANES
    cosine, sine = cos_ref[...], sin_ref[...]
    for block in range(q_blocks + k_blocks):
        at = pl.ds(block * LANES, LANES)
        u = pre_ref[:, at]
        n = u * lax.rsqrt(half_sums(u * u) / HD + EPSILON) * gain_ref[:1, at]
        turned = n * cosine + swapped_halves(n) * sine
        if block < q_blocks:
            q_ref[:, at] = (turned.astype(BF16).astype(F32) * (1.0 / math.sqrt(HD))).astype(BF16)
        else:
            kv_ref[0, :, pl.ds((block - q_blocks) * LANES, LANES)] = turned.astype(BF16)
    v_at = (q_blocks + k_blocks) * LANES
    kv_ref[1] = pre_ref[:, v_at : v_at + k_blocks * LANES].astype(BF16)


def head_prep(pre, cosine, sine, gains):
    rows = pre.shape[0]
    return pl.pallas_call(
        head_prep_kernel,
        out_shape=(
            jax.ShapeDtypeStruct((rows, HEADS * HD), BF16),
            jax.ShapeDtypeStruct((2, rows, KV_HEADS * HD), BF16),
        ),
        compiler_params=pltpu.CompilerParams(vmem_limit_bytes=VMEM_LIMIT),
        name="head_prep",
    )(pre, cosine, sine, gains)


def head_back_kernel(
    gq_ref, gkv_ref, one_ref, two_ref, pre_ref, cos_ref, sin_ref, gain_ref, out_ref, sums_ref
):
    q_blocks = HEADS * HD // LANES
    k_blocks = KV_HEADS * HD // LANES
    cosine, sine = cos_ref[...], sin_ref[...]
    sums_ref[...] = jnp.zeros_like(sums_ref)
    for block in range(q_blocks + k_blocks):
        at = pl.ds(block * LANES, LANES)
        if block < q_blocks:
            g = gq_ref[:, at]
        else:
            k_at = pl.ds((block - q_blocks) * LANES, LANES)
            g = gkv_ref[0, :, k_at] + one_ref[0, :, k_at].astype(F32) + two_ref[0, :, k_at].astype(F32)
        g = g * cosine - swapped_halves(g) * sine
        u = pre_ref[:, at]
        inverse = lax.rsqrt(half_sums(u * u) / HD + EPSILON)
        unit = u * inverse
        row = 0 if block < q_blocks else 1
        sums_ref[row : row + 1, :] += jnp.sum(unit * g, axis=0, keepdims=True)
        e = g * gain_ref[:1, at]
        out_ref[:, at] = (inverse * (e - unit * (half_sums(e * unit) / HD))).astype(BF16)
    v_at = (q_blocks + k_blocks) * LANES
    width = k_blocks * LANES
    out_ref[:, v_at : v_at + width] = (
        gkv_ref[1] + one_ref[1].astype(F32) + two_ref[1].astype(F32)
    ).astype(BF16)
    tail = out_ref.shape[1] - v_at - width
    out_ref[:, v_at + width :] = jnp.zeros((out_ref.shape[0], tail), BF16)


def head_back(gq, gkv, one, two, pre, cosine, sine, gains):
    rows, width = pre.shape
    return pl.pallas_call(
        head_back_kernel,
        out_shape=(
            jax.ShapeDtypeStruct((rows, width), BF16),
            jax.ShapeDtypeStruct((8, LANES), F32),
        ),
        compiler_params=pltpu.CompilerParams(vmem_limit_bytes=VMEM_LIMIT),
        name="head_back",
    )(gq, gkv, one, two, pre, cosine, sine, gains)


def stacked_heads(ref, pair, repeat):
    return jnp.concatenate(
        [ref[:, pl.ds((pair * repeat + h) * HD, HD)] for h in range(repeat)], axis=0
    )


def window_probs(q4, keys, rel, repeat):
    rows, span = rel.shape[0], keys.shape[0]
    scores = right_transposed(q4, keys).reshape(repeat, rows, span)
    key_at = lax.broadcasted_iota(jnp.int32, (rows, span), 1) - (span - rows)
    row_at = lax.broadcasted_iota(jnp.int32, (rows, span), 0)
    allowed = (key_at <= row_at) & (key_at >= rel)
    scores = jnp.where(allowed[None], scores, MASKED)
    top = jnp.max(scores, axis=-1, keepdims=True)
    raised = jnp.exp(scores - top)
    return raised * (1.0 / jnp.sum(raised, axis=-1, keepdims=True))


def attend_kernel(q_ref, two_ref, one_ref, kv_ref, rel_ref, out_ref):
    repeat = HEADS // KV_HEADS
    rows = q_ref.shape[0]
    rel = rel_ref[:, :1]
    keys = jnp.concatenate([two_ref[0], one_ref[0], kv_ref[0]], axis=0)
    vals = jnp.concatenate([two_ref[1], one_ref[1], kv_ref[1]], axis=0)
    for pair in range(2):
        part = slice(pair * HD, (pair + 1) * HD)
        q4 = stacked_heads(q_ref, pair, repeat)
        probs = window_probs(q4, keys[:, part], rel, repeat)
        low = probs.astype(BF16).reshape(repeat * rows, -1)
        mixed = product(low, vals[:, part])
        for h in range(repeat):
            out_ref[:, pl.ds((pair * repeat + h) * HD, HD)] = mixed[
                h * rows : (h + 1) * rows
            ].astype(BF16)


def attend_specs(rows):
    q_spec = pl.BlockSpec((rows, HEADS * HD // 3), lambda g: (0, g))
    kv_spec = pl.BlockSpec((2, rows, LANES), lambda g: (0, 0, g))
    rel_spec = pl.BlockSpec((rows, LANES), lambda g: (0, 0))
    return q_spec, kv_spec, rel_spec


def attend(q, two, one, kv, rel):
    rows = q.shape[0]
    q_spec, kv_spec, rel_spec = attend_specs(rows)
    return pl.pallas_call(
        attend_kernel,
        grid=(3,),
        in_specs=[q_spec, kv_spec, kv_spec, kv_spec, rel_spec],
        out_specs=q_spec,
        out_shape=jax.ShapeDtypeStruct((rows, HEADS * HD), BF16),
        compiler_params=pltpu.CompilerParams(vmem_limit_bytes=VMEM_LIMIT),
        name="attend",
    )(q, two, one, kv, rel)


def attend_back_kernel(
    q_ref, two_ref, one_ref, kv_ref, rel_ref, gm_ref, gq_ref, gtwo_ref, gone_ref, gkv_ref
):
    repeat = HEADS // KV_HEADS
    rows = q_ref.shape[0]
    rel = rel_ref[:, :1]
    keys = jnp.concatenate([two_ref[0], one_ref[0], kv_ref[0]], axis=0)
    vals = jnp.concatenate([two_ref[1], one_ref[1], kv_ref[1]], axis=0)
    key_grads, val_grads = [], []
    for pair in range(2):
        part = slice(pair * HD, (pair + 1) * HD)
        q4 = stacked_heads(q_ref, pair, repeat)
        gm4 = stacked_heads(gm_ref, pair, repeat)
        probs = window_probs(q4, keys[:, part], rel, repeat)
        grad_probs = right_transposed(gm4, vals[:, part]).reshape(probs.shape)
        weighted = jnp.sum(probs * grad_probs, axis=-1, keepdims=True)
        span = probs.shape[-1]
        gs = (probs * (grad_probs - weighted)).astype(BF16).reshape(repeat * rows, span)
        low = probs.astype(BF16).reshape(repeat * rows, span)
        gq = product(gs, keys[:, part]) * (1.0 / math.sqrt(HD))
        for h in range(repeat):
            gq_ref[:, pl.ds((pair * repeat + h) * HD, HD)] = gq[h * rows : (h + 1) * rows]
        key_grads.append(product(q4.T, gs).T)
        val_grads.append(product(gm4.T, low).T)
    for at, parts in ((0, key_grads), (1, val_grads)):
        both = jnp.concatenate(parts, axis=1)
        gtwo_ref[at] = both[:rows].astype(gtwo_ref.dtype)
        gone_ref[at] = both[rows : 2 * rows].astype(gone_ref.dtype)
        gkv_ref[at] = both[2 * rows :]


def attend_back(q, two, one, kv, rel, gm):
    rows = q.shape[0]
    q_spec, kv_spec, rel_spec = attend_specs(rows)
    return pl.pallas_call(
        attend_back_kernel,
        grid=(3,),
        in_specs=[q_spec, kv_spec, kv_spec, kv_spec, rel_spec, q_spec],
        out_specs=(q_spec, kv_spec, kv_spec, kv_spec),
        out_shape=(
            jax.ShapeDtypeStruct((rows, HEADS * HD), F32),
            jax.ShapeDtypeStruct((2, rows, KV_HEADS * HD), BF16),
            jax.ShapeDtypeStruct((2, rows, KV_HEADS * HD), BF16),
            jax.ShapeDtypeStruct((2, rows, KV_HEADS * HD), F32),
        ),
        compiler_params=pltpu.CompilerParams(vmem_limit_bytes=VMEM_LIMIT),
        name="attend_back",
    )(q, two, one, kv, rel, gm)


def feed_kernel(x_ref, both_ref, act_ref, slopes_ref):
    units = act_ref.shape[1]
    mixed = product(x_ref[...], both_ref[...])
    gate, up = mixed[:, :units], mixed[:, units:]
    sig = 1.0 / (1.0 + jnp.exp(-gate))
    silu = gate * sig
    act_ref[...] = (silu * up).astype(BF16)
    slopes_ref[:, :units] = (up * sig * (1.0 + gate * (1.0 - sig))).astype(BF16)
    slopes_ref[:, units:] = silu.astype(BF16)


def feed(x, both, tile):
    rows, width = x.shape
    units = both.shape[1] // 2
    return pl.pallas_call(
        feed_kernel,
        grid=(rows // tile,),
        in_specs=[
            pl.BlockSpec((tile, width), lambda i: (i, 0)),
            pl.BlockSpec((width, 2 * units), lambda i: (0, 0)),
        ],
        out_specs=[
            pl.BlockSpec((tile, units), lambda i: (i, 0)),
            pl.BlockSpec((tile, 2 * units), lambda i: (i, 0)),
        ],
        out_shape=[
            jax.ShapeDtypeStruct((rows, units), BF16),
            jax.ShapeDtypeStruct((rows, 2 * units), BF16),
        ],
        compiler_params=pltpu.CompilerParams(vmem_limit_bytes=VMEM_LIMIT),
        cost_estimate=pl.CostEstimate(
            flops=4 * rows * width * units,
            transcendentals=rows * units,
            bytes_accessed=2 * (rows * width + 2 * width * units + 3 * rows * units),
        ),
        name="feed",
    )(x, both)


def feed_back_kernel(x_ref, down_ref, slopes_ref, both_ref, grads_ref, own_ref, other_ref):
    step, steps = pl.program_id(0), pl.num_programs(0)
    lots = own_ref.shape[0]
    grad_act = right_transposed(x_ref[...], down_ref[...])
    both_act = jnp.concatenate([grad_act, grad_act], axis=1)
    grads = (both_act * slopes_ref[...].astype(F32)).astype(BF16)
    grads_ref[...] = grads
    total = right_transposed(grads, both_ref[...])
    total = total.reshape(lots, -1, total.shape[1])

    total = total.astype(BF16)

    @pl.when(step < steps // 2)
    def _():
        own_ref[...] = total

    @pl.when(step >= steps // 2)
    def _():
        other_ref[...] = total


def feed_back(upstream, down, slopes, both, lot, tile):
    rows, width = upstream.shape
    units = down.shape[0]
    steps = rows // tile
    lots = rows // lot
    per = tile // lot
    return pl.pallas_call(
        feed_back_kernel,
        grid=(steps,),
        in_specs=[
            pl.BlockSpec((tile, width), lambda i: (i, 0)),
            pl.BlockSpec((units, width), lambda i: (0, 0)),
            pl.BlockSpec((tile, 2 * units), lambda i: (i, 0)),
            pl.BlockSpec((width, 2 * units), lambda i: (0, 0)),
        ],
        out_specs=[
            pl.BlockSpec((tile, 2 * units), lambda i: (i, 0)),
            pl.BlockSpec((per, lot, width), lambda i: (jnp.minimum(i, steps // 2 - 1), 0, 0)),
            pl.BlockSpec((per, lot, width), lambda i: (jnp.maximum(i - steps // 2, 0), 0, 0)),
        ],
        out_shape=[
            jax.ShapeDtypeStruct((rows, 2 * units), BF16),
            jax.ShapeDtypeStruct((lots // 2, lot, width), BF16),
            jax.ShapeDtypeStruct((lots // 2, lot, width), BF16),
        ],
        compiler_params=pltpu.CompilerParams(vmem_limit_bytes=VMEM_LIMIT),
        cost_estimate=pl.CostEstimate(
            flops=6 * rows * width * units,
            transcendentals=0,
            bytes_accessed=2 * (3 * rows * width + 3 * width * units + 4 * rows * units),
        ),
        name="feed_back",
    )(upstream, down, slopes, both)


def lane_window(read, tiles, start):
    tile, shift = start // LANES, start % LANES
    first = read(min(max(tile, 0), tiles - 1))
    if shift == 0:
        return first
    second = read(min(max(tile + 1, 0), tiles - 1))
    lane = lax.broadcasted_iota(jnp.int32, first.shape, 1)
    return jnp.where(
        lane < LANES - shift,
        pltpu.roll(first, LANES - shift, 1),
        pltpu.roll(second, LANES - shift, 1),
    )


def lane_runs(target, runs, source_of):
    total = None
    for first, length, source in runs:
        low, high = max(first, target), min(first + length, target + LANES)
        if low >= high:
            continue
        window = source_of(source, target - first)
        lane = lax.broadcasted_iota(jnp.int32, window.shape, 1) + target
        kept = jnp.where((lane >= low) & (lane < high), window, 0.0)
        total = kept if total is None else total + kept
    return total


def split_kernel(far, unit, block, me_ref, gate_ref, up_ref, out_ref):
    units = far * block
    tiles = -(-gate_ref.shape[1] // LANES)
    for at, ref in ((0, gate_ref), (units, up_ref)):
        for part in range(8):
            runs = [(d * block, unit, (8 * d + part) * unit) for d in range(far)]

            def source_of(source, offset):
                read = lambda t: ref[:, t * LANES : (t + 1) * LANES].astype(F32)
                return lane_window(read, tiles, source + offset)

            for target in range(0, units, LANES):
                value = lane_runs(target, runs, source_of)
                to = pl.ds(at + target, LANES)
                turned = part // 2 % 2 * 4 + part // 4 * 2 + part % 2
                out_ref[turned ^ me_ref[0], :, to] = value.astype(BF16)


def split_units(gate, up, me, far, unit, block):
    return pl.pallas_call(
        functools.partial(split_kernel, far, unit, block),
        in_specs=[
            pl.BlockSpec(memory_space=pltpu.SMEM),
            pl.BlockSpec(memory_space=pltpu.VMEM),
            pl.BlockSpec(memory_space=pltpu.VMEM),
        ],
        out_shape=jax.ShapeDtypeStruct((8, gate.shape[0], 2 * far * block), BF16),
        compiler_params=pltpu.CompilerParams(vmem_limit_bytes=VMEM_LIMIT),
        name="split_units",
    )(me, gate, up)


def join_kernel(far, unit, block, me_ref, got_ref, gate_ref, up_ref):
    units = far * block
    tiles = got_ref.shape[2] // LANES
    runs = [
        ((8 * d + part) * unit, unit, (part, d * block)) for d in range(far) for part in range(8)
    ]
    for at, ref in ((0, gate_ref), (units, up_ref)):

        def source_of(source, offset):
            read = lambda t: got_ref[
                source[0] ^ me_ref[0], :, t * LANES : (t + 1) * LANES
            ].astype(F32)
            return lane_window(read, tiles, at + source[1] + offset)

        for target in range(0, ref.shape[1], LANES):
            ref[:, target : target + LANES] = lane_runs(target, runs, source_of)


def join_units(got, me, far, unit, block):
    out = jax.ShapeDtypeStruct((got.shape[1], 8 * far * unit), F32)
    return pl.pallas_call(
        functools.partial(join_kernel, far, unit, block),
        in_specs=[
            pl.BlockSpec(memory_space=pltpu.SMEM),
            pl.BlockSpec(memory_space=pltpu.VMEM),
        ],
        out_shape=[out, out],
        compiler_params=pltpu.CompilerParams(vmem_limit_bytes=VMEM_LIMIT),
        name="join_units",
    )(me, got)


def swap_pairs(size, bit):
    return [(i, i ^ bit) for i in range(size)]


def far_pairs(size, shift):
    far = size // 2
    return [(i, (i // 2 + shift) % far * 2 + i % 2) for i in range(size)]


def far_order(far):
    order = []
    for step in range(1, far // 2 + 1):
        order.append(step)
        if far - step != step:
            order.append(far - step)
    return order


def place_kernel(counts, slots, *refs):
    pieces, out, held, come, gone = refs[: len(counts)], *refs[len(counts) :]
    arrivals, departures = [], []
    for piece, count in zip(pieces, counts):
        for k in range(count):
            at = len(arrivals)
            arrivals.append(pltpu.make_async_copy(piece.at[k], held.at[at], come.at[at]))
            departures.append(pltpu.make_async_copy(held.at[at], out.at[slots[at]], gone.at[at]))
    for copy in arrivals:
        copy.start()
    for arrival, departure in zip(arrivals, departures):
        arrival.wait()
        departure.start()
    for copy in departures:
        copy.wait()


def place(pieces, slots):
    counts = [piece.shape[0] for piece in pieces]
    total = sum(counts)
    shape = (total,) + pieces[0].shape[1:]
    moved = 2 * math.prod(shape) * pieces[0].dtype.itemsize
    return pl.pallas_call(
        functools.partial(place_kernel, counts),
        in_specs=[pl.BlockSpec(memory_space=pltpu.SMEM)]
        + [pl.BlockSpec(memory_space=pl.ANY)] * len(pieces),
        out_specs=pl.BlockSpec(memory_space=pl.ANY),
        out_shape=jax.ShapeDtypeStruct(shape, pieces[0].dtype),
        scratch_shapes=[
            pltpu.VMEM(shape, pieces[0].dtype),
            pltpu.SemaphoreType.DMA((total,)),
            pltpu.SemaphoreType.DMA((total,)),
        ],
        compiler_params=pltpu.CompilerParams(vmem_limit_bytes=VMEM_LIMIT),
        cost_estimate=pl.CostEstimate(flops=0, transcendentals=0, bytes_accessed=moved),
        name="place",
    )(slots, *pieces)


def pick_kernel(counts, slots, source, *refs):
    outs, (held, come, gone) = refs[: len(counts)], refs[len(counts) :]
    arrivals, departures = [], []
    for out, count in zip(outs, counts):
        for k in range(count):
            at = len(arrivals)
            arrivals.append(pltpu.make_async_copy(source.at[slots[at]], held.at[at], come.at[at]))
            departures.append(pltpu.make_async_copy(held.at[at], out.at[k], gone.at[at]))
    for copy in arrivals:
        copy.start()
    for arrival, departure in zip(arrivals, departures):
        arrival.wait()
        departure.start()
    for copy in departures:
        copy.wait()


def pick(source, slots, counts):
    total = sum(counts)
    block = source.shape[1:]
    moved = 2 * total * math.prod(block) * source.dtype.itemsize
    return pl.pallas_call(
        functools.partial(pick_kernel, counts),
        in_specs=[pl.BlockSpec(memory_space=pltpu.SMEM), pl.BlockSpec(memory_space=pl.ANY)],
        out_specs=[pl.BlockSpec(memory_space=pl.ANY)] * len(counts),
        out_shape=[jax.ShapeDtypeStruct((n,) + block, source.dtype) for n in counts],
        scratch_shapes=[
            pltpu.VMEM((total,) + block, source.dtype),
            pltpu.SemaphoreType.DMA((total,)),
            pltpu.SemaphoreType.DMA((total,)),
        ],
        compiler_params=pltpu.CompilerParams(vmem_limit_bytes=VMEM_LIMIT),
        cost_estimate=pl.CostEstimate(flops=0, transcendentals=0, bytes_accessed=moved),
        name="pick",
    )(slots, source)


class Places:
    def __init__(self, dp_size):
        self.size, self.far = dp_size, dp_size // 2
        self.dp, self.member = lax.axis_index("dp"), lax.axis_index("fsdp")
        self.me = self.dp % 2 * 4 + self.member
        self.groups = [[2 * z + y for z in range(self.far)] for y in range(2)]

    def near_block(self, shift, near):
        return (self.dp // 2 + self.far + shift) % self.far * 2 + self.dp % 2 * (1 - near) + (
            1 - self.dp % 2
        ) * near

    def block(self, shift, near, member):
        return self.near_block(shift, near) * 4 + (self.member ^ member)


def far_gather(piece, places):
    held = {0: piece}
    for r in far_order(places.far):
        held[r] = lax.ppermute(piece, "dp", far_pairs(places.size, r))
    return held


def plane_first(mine, places):
    half = mine.shape[0] // 2
    first, second = mine[:half], mine[half:]
    near, across = near_swap(first, places), member_swap(second, 2)
    return jnp.concatenate([first, near]), jnp.concatenate([second, across])


def plane_second(first, second, places):
    across, near = member_swap(first, 2), near_swap(second, places)
    return jnp.concatenate([first, across]), jnp.concatenate([second, near])


def plane_last(first, second, sends, places):
    half = places.far // 2
    lots = [0, *sends][:half], [0, *sends][half:]
    slots = [
        places.block(-r, inner, 2 * outer + core)
        for core in (0, 1)
        for outer in (0, 1)
        for inner in (0, 1)
        for r in lots[0]
    ]
    later = [
        places.block(-r, outer, 2 * inner + core)
        for core in (0, 1)
        for outer in (0, 1)
        for inner in (0, 1)
        for r in lots[1]
    ]
    blocks = [first, member_swap(first, 1), second, member_swap(second, 1)]
    return place(blocks, jnp.stack(slots + later))


def gated(value, gate):
    return value if gate is None else lax.optimization_barrier((value, gate))[0]


def exchange_chips(parts):
    return jnp.stack([parts[:4], member_swap(parts[4:], 2)])


def exchange_near(parts, places):
    return jnp.stack([parts[:, :2], near_swap(parts[:, 2:], places)])


def exchange_units(parts, places):
    beside = member_swap(parts[:, :, 1], 1)
    own = parts[:, :, 0]
    blocks = [own.reshape(4, *own.shape[2:]), beside.reshape(4, *own.shape[2:])]
    slots = [
        places.me ^ (4 * near + 2 * chip + core)
        for core in (0, 1)
        for near in (0, 1)
        for chip in (0, 1)
    ]
    return place(blocks, jnp.stack(slots))


def return_core(blocks, places):
    slots = [
        places.me ^ (4 * near + 2 * chip + core)
        for core in (1, 0)
        for chip in (1, 0)
        for near in (1, 0)
    ]
    other, own = pick(blocks, jnp.stack(slots), [4, 4])
    return jnp.stack([own, member_swap(other, 1)])


def return_units(held, places):
    across = member_swap(held[:, :2], 2)
    held = jnp.stack([held[:, 2:], across])
    near = near_swap(held[:, :, 0], places)
    held = jnp.stack([held[:, :, 1], near])
    return held.reshape(8, *held.shape[3:])


def assemble_kernel(*refs):
    pieces, (out, held, come, gone) = refs[:-4], refs[-4:]
    half = out.shape[2] // 2
    arrivals, departures = [], []
    for k, piece in enumerate(pieces):
        core, at = k // 5, k % 5
        columns = pl.ds(0, 2 * half) if at < 3 else pl.ds((at - 3) * half, half)
        spot = (core * 4 + min(at, 3), slice(None), columns)
        arrivals.append(pltpu.make_async_copy(piece, held.at[spot], come.at[k]))
        departures.append(pltpu.make_async_copy(held.at[spot], out.at[spot], gone.at[k]))
    for copy in arrivals:
        copy.start()
    for arrival, departure in zip(arrivals, departures):
        arrival.wait()
        departure.start()
    for copy in departures:
        copy.wait()


def assemble(pieces):
    rows, width = pieces[0].shape
    shape = (8, rows, width)
    return pl.pallas_call(
        assemble_kernel,
        in_specs=[pl.BlockSpec(memory_space=pl.ANY)] * len(pieces),
        out_specs=pl.BlockSpec(memory_space=pl.ANY),
        out_shape=jax.ShapeDtypeStruct(shape, BF16),
        scratch_shapes=[
            pltpu.VMEM(shape, BF16),
            pltpu.SemaphoreType.DMA((len(pieces),)),
            pltpu.SemaphoreType.DMA((len(pieces),)),
        ],
        compiler_params=pltpu.CompilerParams(vmem_limit_bytes=VMEM_LIMIT),
        cost_estimate=pl.CostEstimate(
            flops=0, transcendentals=0, bytes_accessed=4 * math.prod(shape)
        ),
        name="assemble",
    )(*pieces)


def gather_first(rows, places):
    return rows, member_swap(rows, 2), near_swap(rows, places)


def gather_second(rows, across, near, places):
    half = rows.shape[1] // 2
    left = near_swap(across[:, :half], places)
    right = member_swap(near[:, half:], 2)
    return rows, across, near, left, right


def gather_last(*pieces):
    out = assemble([*pieces, *(member_swap(piece, 1) for piece in pieces)])
    return out.reshape(-1, out.shape[2])


def merge_kernel(own_ref, got_ref, near_ref, across_ref, left_ref, right_ref):
    half = own_ref.shape[2] // 2
    left, right = pl.ds(0, half), pl.ds(half, half)

    def total(lot, columns):
        return own_ref[lot, :, columns].astype(F32) + got_ref[lot, :, columns].astype(F32)

    for k, lot in enumerate((2, 3)):
        near_ref[k] = total(lot, left).astype(BF16)
    for k, lot in enumerate((1, 3)):
        across_ref[k] = total(lot, right).astype(BF16)
    for k, lot in enumerate((0, 1)):
        left_ref[k] = total(lot, left)
    for k, lot in enumerate((0, 2)):
        right_ref[k] = total(lot, right)


def merge(own, got):
    shape = (2, own.shape[1], own.shape[2] // 2)
    low, wide = jax.ShapeDtypeStruct(shape, BF16), jax.ShapeDtypeStruct(shape, F32)
    return pl.pallas_call(
        merge_kernel,
        out_shape=[low, low, wide, wide],
        compiler_params=pltpu.CompilerParams(vmem_limit_bytes=VMEM_LIMIT),
        cost_estimate=pl.CostEstimate(
            flops=own.size, transcendentals=0, bytes_accessed=7 * own.size
        ),
        name="merge",
    )(own, got)


def scatter_first(own, other, places):
    near, across, left, right = merge(own, member_swap(other, 1))
    near, across = near_swap(near, places), member_swap(across, 2)
    return left, near, right, across


def scatter_second(left, near, right, across, places):
    left_out = (left[1] + near[1].astype(F32)).astype(BF16)
    right_out = (right[1] + across[1].astype(F32)).astype(BF16)
    left_got, right_got = member_swap(left_out, 2), near_swap(right_out, places)
    left = left[0] + near[0].astype(F32) + left_got.astype(F32)
    right = right[0] + across[0].astype(F32) + right_got.astype(F32)
    return jnp.concatenate([left, right], axis=1)


def split_order(far):
    order = far_order(far) + [0]
    return order[: far // 2], order[far // 2 :]


def far_parts(term, places, cut=1):
    order = sum(split_order(places.far), [])
    slots = [(places.dp // 2 + r) % places.far * cut + k for r in order for k in range(cut)]
    return pick(term, jnp.stack(slots), [1] * len(slots))


def whole_parts(term, places):
    lots = split_order(places.far)
    slots = []
    for core in (1, 0):
        slots += [places.block(r, n, core + c) for c in (2, 0) for n in (1, 0) for r in lots[0]]
        slots += [places.block(r, n, core + c) for n in (1, 0) for c in (2, 0) for r in lots[1]]
    return pick(term, jnp.stack(slots), [4 * places.far] * 2)


def near_swap(value, places):
    return lax.ppermute(value, "dp", swap_pairs(places.size, 1))


def member_swap(value, bit):
    return lax.ppermute(value, "fsdp", swap_pairs(4, bit))


def added(own, got):
    return (own.astype(F32) + got.astype(F32)).astype(BF16)


def added_parts(own, got, cut):
    return added(own[:cut], got[:cut]), added(own[cut:], got[cut:])


def far_sends(lot, blocks, places):
    return [
        lax.ppermute(blocks[k], "dp", far_pairs(places.size, r)) if r else blocks[k]
        for k, r in enumerate(lot)
    ]


def total_of(parts):
    total = parts[0].astype(F32)
    for part in parts[1:]:
        total = total + part.astype(F32)
    return total


class Rounds:
    def __init__(self):
        self.results = ()

    def enter(self, *values):
        kept = lax.optimization_barrier((values, self.results))[0]
        self.results = ()
        return kept

    def leave(self, *values):
        self.results += values
        return list(values) if len(values) > 1 else values[0]


def sum_steps(value, axis, size, bit=1, end=None):
    while bit < (end or size):
        value = value + lax.ppermute(value, axis, swap_pairs(size, bit))
        bit *= 2
    return value


def local(
    tokens,
    cotangent,
    seq_lengths,
    deal_order,
    attn_gain,
    w_query,
    w_key,
    w_value,
    q_gain,
    k_gain,
    w_out,
    ffn_gain,
    w_gate,
    w_up,
    w_down,
):
    rows, width = tokens.shape
    dp_size = lax.axis_size("dp")
    shard = w_gate.shape[0]
    ff_rows = w_down.shape[0]
    member = lax.axis_index("fsdp")

    lengths = seq_lengths[0]
    slots = jnp.arange(lengths.shape[0], dtype=jnp.int32)
    starts = jnp.sum(jnp.where(slots[None, :] < slots[:, None], lengths[None, :], 0), axis=1)
    row_ids = member * rows + jnp.arange(rows, dtype=jnp.int32)
    begun = starts[None, :] <= row_ids[:, None]
    row_start = jnp.max(jnp.where(begun, starts[None, :], 0), axis=1)
    row_place = row_ids - row_start
    rel = jnp.broadcast_to((row_start - member * rows)[:, None], (rows, LANES))
    frequency = 10000.0 ** (-2.0 * jnp.arange(HD // 2, dtype=F32) / HD)
    angles = row_place.astype(F32)[:, None] * frequency[None, :]
    cosine, sine = jnp.cos(angles), jnp.sin(angles)
    cosine = jnp.concatenate([cosine] * 4, axis=1)
    sine = jnp.concatenate([-sine, sine, -sine, sine], axis=1)
    head_gains = jnp.concatenate([jnp.tile(q_gain, HEADS), jnp.tile(k_gain, KV_HEADS)])
    head_gains = jnp.broadcast_to(head_gains.astype(F32)[None, :], (8, head_gains.shape[0]))

    places = Places(dp_size)
    gain_columns = jnp.pad(
        jnp.stack([attn_gain, ffn_gain], axis=1), ((0, 0), (0, LANES - 2))
    )
    w_qkv = jnp.concatenate([w_query, w_key, w_value, gain_columns], axis=1)

    far = places.far
    ff_block = -(-ff_rows * far // LANES) * LANES // far
    ff_width = far * ff_block
    me = places.me.reshape(1)
    turned = places.member // 2 * 4 + places.dp % 2 * 2 + places.member % 2
    units = split_units(w_gate, w_up, turned.reshape(1), far, ff_rows, ff_block)
    sends = far_order(far)
    gather_far = functools.partial(
        lax.all_gather, axis_name="dp", axis=0, tiled=True, axis_index_groups=places.groups
    )

    rounds = Rounds()
    qkv_held = far_gather(w_qkv, places)
    qkv_mine = rounds.leave(jnp.stack([qkv_held[r] for r in [0] + sends]))
    units = rounds.leave(exchange_near(exchange_chips(units), places))

    qkv_mine, units, down_piece = rounds.enter(qkv_mine, units, w_down)
    qkv_a, qkv_b = plane_first(qkv_mine, places)
    qkv_a, qkv_b = rounds.leave(qkv_a, qkv_b)
    down_piece = jnp.pad(down_piece, ((0, ff_block - ff_rows), (0, 0)))
    my_down = gather_far(down_piece)
    both_piece = rounds.leave(exchange_units(units, places))

    qkv_a, qkv_b, late_out, both_piece = rounds.enter(qkv_a, qkv_b, w_out, both_piece)
    out_held = far_gather(late_out, places)
    out_mine = rounds.leave(jnp.stack([out_held[r] for r in [0] + sends]))
    qkv_a, qkv_b = rounds.leave(*plane_second(qkv_a, qkv_b, places))
    my_both = gather_far(both_piece.reshape(8 * shard, 2 * ff_width))

    qkv_a, qkv_b, out_mine = rounds.enter(qkv_a, qkv_b, out_mine)
    full_qkv = plane_last(qkv_a, qkv_b, sends, places).reshape(width, -1)
    out_first = plane_first(gated(out_mine, full_qkv), places)

    gain_table = full_qkv[:, full_qkv.shape[1] - LANES :]
    pick = (
        lax.broadcasted_iota(jnp.int32, (8, LANES), 0)
        == lax.broadcasted_iota(jnp.int32, (8, LANES), 1)
    ).astype(BF16)
    gain_rows = right_transposed(pick, gain_table)
    attn_row, ffn_row = gain_rows[0:1], gain_rows[1:2]
    x = tokens.astype(F32)
    x_inverse = lax.rsqrt(jnp.mean(x * x, axis=-1, keepdims=True) + EPSILON)
    normed = (x * x_inverse * attn_row).astype(BF16)
    pre = product(normed, full_qkv)
    queries, kv = head_prep(pre, cosine, sine, head_gains)
    ahead_one = [(i, i + 1) for i in range(3)]
    ahead_two = [(i, i + 2) for i in range(2)]
    kv = gated(kv, my_down)
    kv_one = lax.ppermute(kv, "fsdp", ahead_one)
    kv_two = lax.ppermute(kv, "fsdp", ahead_two)
    out_a, out_b = plane_second(*gated(out_first, (kv_one, kv_two)), places)
    mixed = attend(queries, kv_two, kv_one, kv, rel)
    pieces = gather_first(gated(cotangent, (out_a, out_b, mixed)), places)
    full_out = plane_last(out_a, out_b, sends, places).reshape(-1, width)
    pieces = gather_second(*gated(pieces, full_out), places)
    hidden = x + product(mixed, full_out)
    h_inverse = lax.rsqrt(jnp.mean(hidden * hidden, axis=-1, keepdims=True) + EPSILON)
    ffn_mine = (hidden * h_inverse * ffn_row).astype(BF16)

    ffn_pieces = gather_first(gated(ffn_mine, pieces), places)
    upstream = gather_last(*pieces)
    ffn_low = gather_last(*gather_second(*gated(ffn_pieces, upstream), places))
    tile = 2 * rows
    act_low, slopes = feed(ffn_low, my_both, tile)
    order = sum(split_order(far), [])

    def parts_of(left, right, cut=1):
        term = left_transposed(left, right).astype(BF16)
        return far_parts(term.reshape(far * cut, -1, term.shape[1]), places, cut)

    def far_sent(blocks, which, cut=1):
        return [
            lax.ppermute(blocks[k], "dp", far_pairs(dp_size, order[k // cut]))
            if order[k // cut]
            else blocks[k]
            for k in which
        ]

    first, second = range(far // 2), range(far // 2, far)
    sent = 2 * (far - 1)
    cut_a = sent // 2
    rounds = Rounds()

    *d_blocks, upstream, my_down, slopes = rounds.enter(
        *parts_of(act_low, upstream), upstream, my_down, slopes
    )
    d_first, d_second = far_sent(d_blocks, first), far_sent(d_blocks, second)
    rounds.leave(*d_first)
    grads, ffn_own, ffn_other = rounds.leave(
        *feed_back(upstream, my_down, slopes, my_both, rows, tile)
    )

    grads, ffn_own, ffn_other, act_low = rounds.enter(grads, ffn_own, ffn_other, act_low)
    grad_ffn = scatter_second(*scatter_first(ffn_own, ffn_other, places), places)
    grad_ffn = rounds.leave(grad_ffn)
    u_blocks = rounds.leave(*parts_of(ffn_low, grads, 2))
    out_own, out_other = rounds.leave(
        *(
            product(part, my_down).astype(BF16).reshape(4, rows, width)
            for part in (act_low[: 4 * rows], act_low[4 * rows :])
        )
    )
    rounds.leave(*d_second)

    *u_blocks, grad_ffn, out_own, out_other = rounds.enter(
        *u_blocks, grad_ffn, out_own, out_other
    )
    u_got = rounds.leave(*far_sent(u_blocks, range(cut_a), 2))
    out_steps = rounds.leave(*scatter_first(out_own, out_other, places))
    e = grad_ffn * ffn_row
    slope = jnp.mean(hidden * e, axis=-1, keepdims=True)
    grad_hidden = cotangent.astype(F32) + h_inverse * e - hidden * (h_inverse**3 * slope)
    ffn_gain_term = jnp.sum(grad_ffn * hidden * h_inverse, axis=0)
    grad_hidden_low = grad_hidden.astype(BF16)
    grad_mixed = right_transposed(grad_hidden_low, full_out).astype(BF16)
    gq, gkv_two, gkv_one, gkv = rounds.leave(
        *attend_back(queries, kv_two, kv_one, kv, rel, grad_mixed)
    )
    grad_hidden_low = rounds.leave(grad_hidden_low)
    down_grad = rounds.leave(total_of(d_first + d_second)[0, :ff_rows])

    u_blocks[sent - 2], gkv_one, gkv_two, gq, gkv, grad_hidden_low, *out_steps = rounds.enter(
        u_blocks[sent - 2], gkv_one, gkv_two, gq, gkv, grad_hidden_low, *out_steps
    )
    term_out = left_transposed(mixed, grad_hidden_low).astype(BF16)
    gq, term_out = lax.optimization_barrier((gq, term_out))
    out_grad = lax.psum_scatter(term_out, BOTH, scatter_dimension=0, tiled=True).astype(F32)
    u_near = far_sent(u_blocks, [sent - 2], 2)
    rounds.leave(*u_near)
    got_one = lax.ppermute(gkv_one, "fsdp", [(b, a) for a, b in ahead_one])
    got_two = lax.ppermute(gkv_two, "fsdp", [(b, a) for a, b in ahead_two])
    output = rounds.leave((hidden + scatter_second(*out_steps, places)).astype(BF16))
    half = 2 * far
    quarter, eighth = half // 2, half // 4
    grad_pre, head_sums = head_back(gq, gkv, got_one, got_two, pre, cosine, sine, head_gains)
    term_qkv = left_transposed(normed, grad_pre).astype(BF16)
    q_other, q_own = rounds.leave(
        *whole_parts(term_qkv.reshape(4 * dp_size, shard, -1), places)
    )
    grad_pre = rounds.leave(grad_pre)

    u_blocks[cut_a], q_other, q_own, grad_pre = rounds.enter(
        u_blocks[cut_a], q_other, q_own, grad_pre
    )
    q_got = rounds.leave(member_swap(q_other, 1))
    middle = range(cut_a, sent - 2)
    u_middle = rounds.leave(far_sent(u_blocks, middle, 2))
    grad_normed = rounds.leave(right_transposed(grad_pre, full_qkv))

    a_out, q_a = added_parts(q_own[:half], q_got[:half], quarter)
    b_out, q_b = added_parts(q_own[half:], q_got[half:], quarter)
    u_blocks[sent - 1], a_out, b_out, grad_normed = rounds.enter(
        u_blocks[sent - 1], a_out, b_out, grad_normed
    )
    last = range(sent - 1, sent + 2)
    u_last = rounds.leave(far_sent(u_blocks, last, 2))
    a_got = rounds.leave(member_swap(a_out, 2))
    b_got = rounds.leave(near_swap(b_out, places))
    e = grad_normed * attn_row
    slope = jnp.mean(x * e, axis=-1, keepdims=True)
    input_grad = grad_hidden + x_inverse * e - x * (x_inverse**3 * slope)
    input_grad = rounds.leave(input_grad.astype(BF16))
    attn_gain_term = jnp.sum(grad_normed * x * x_inverse, axis=0)
    small = jnp.concatenate([attn_gain_term, ffn_gain_term, head_sums.reshape(-1)])
    small = rounds.leave(small.reshape(-1, LANES))

    u_got = dict(enumerate(u_got)) | {sent - 2: u_near[0]}
    u_got |= dict(zip(middle, u_middle)) | dict(zip(last, u_last))

    a_out, q_a = added_parts(q_a, a_got, eighth)
    b_out, q_b = added_parts(q_b, b_got, eighth)
    unit_sum = jnp.concatenate(
        [total_of([u_got[2 * r + k] for r in range(far)]) for k in range(2)], axis=1
    )
    unit_sum = unit_sum.astype(BF16).reshape(8, shard, 2 * ff_width)
    a_out, b_out, small, unit_sum = rounds.enter(a_out, b_out, small, unit_sum)
    a_got = rounds.leave(near_swap(a_out, places))
    b_got = rounds.leave(member_swap(b_out, 2))
    small = sum_steps(small, "fsdp", 4, 1, 2)
    small = rounds.leave(sum_steps(small, "dp", dp_size, 2))
    units = rounds.leave(return_core(unit_sum, places))

    q_a, q_b = added(q_a, a_got), added(q_b, b_got)
    q_a, q_b, small, units = rounds.enter(q_a, q_b, small, units)
    q_parts = far_sends(order[: far // 2], q_a, places) + far_sends(order[far // 2 :], q_b, places)
    unit_all = return_units(units, places)
    small = sum_steps(sum_steps(small, "fsdp", 4, 2), "dp", dp_size, 1, 2).reshape(-1)
    qkv_grad = total_of(q_parts)
    unit_all = gated(unit_all, out_grad)
    gate_grad, up_grad = join_units(unit_all, me, far, ff_rows, ff_block)

    mine = (lax.axis_index("dp") * 4 + member) * shard
    attn_gain_grad = lax.dynamic_slice(small, (mine,), (shard,))
    ffn_gain_grad = lax.dynamic_slice(small, (width + mine,), (shard,))
    head_total = small[2 * width : 2 * width + 2 * LANES].reshape(2, 2, HD).sum(axis=1)

    q_end = HEADS * HD
    k_end = q_end + KV_HEADS * HD
    v_end = k_end + KV_HEADS * HD
    return (
        output,
        input_grad.astype(BF16),
        attn_gain_grad,
        qkv_grad[:, :q_end],
        qkv_grad[:, q_end:k_end],
        qkv_grad[:, k_end:v_end],
        head_total[0],
        head_total[1],
        out_grad,
        ffn_gain_grad,
        gate_grad,
        up_grad,
        down_grad,
    )


def solution(mesh):
    rows = P(BOTH, None)
    vector = P(BOTH)
    in_specs = (
        rows,
        rows,
        P("dp", None),
        P("dp", None),
        vector,
        rows,
        rows,
        rows,
        P(),
        P(),
        rows,
        vector,
        rows,
        rows,
        rows,
    )
    out_specs = (rows, rows, vector, rows, rows, rows, P(), P(), rows, vector, rows, rows, rows)
    return jax.shard_map(local, mesh=mesh, in_specs=in_specs, out_specs=out_specs, check_vma=False)
```

```python
import functools
import math

import jax
import jax.numpy as jnp
from jax import lax
from jax.experimental import pallas as pl
from jax.experimental.pallas import tpu as pltpu
from jax.sharding import PartitionSpec as P

HEADS = 24
KV_HEADS = 6
HD = 64
EPSILON = 1e-06
MASKED = -1e30
LANES = 128
BOTH = ("dp", "fsdp")
F32 = jnp.float32
BF16 = jnp.bfloat16
VMEM_LIMIT = 48 * 1024 * 1024


def product(left, right):
    return jnp.dot(left, right, preferred_element_type=F32)


def right_transposed(left, right):
    return lax.dot_general(left, right, (((1,), (1,)), ((), ())), preferred_element_type=F32)


def left_transposed(left, right):
    return lax.dot_general(left, right, (((0,), (0,)), ((), ())), preferred_element_type=F32)


def half_sums(values):
    rows = lax.broadcasted_iota(jnp.int32, (LANES, LANES), 0) // HD
    cols = lax.broadcasted_iota(jnp.int32, (LANES, LANES), 1) // HD
    same = (rows == cols).astype(F32)
    return jnp.dot(values, same, precision=lax.Precision.HIGHEST, preferred_element_type=F32)


def swapped_halves(values):
    lane = lax.broadcasted_iota(jnp.int32, values.shape, 1) % HD
    return jnp.where(
        lane < HD // 2, pltpu.roll(values, LANES - HD // 2, 1), pltpu.roll(values, HD // 2, 1)
    )


def head_prep_kernel(pre_ref, cos_ref, sin_ref, gain_ref, q_ref, kv_ref):
    q_blocks = HEADS * HD // LANES
    k_blocks = KV_HEADS * HD // LANES
    cosine, sine = cos_ref[...], sin_ref[...]
    for block in range(q_blocks + k_blocks):
        at = pl.ds(block * LANES, LANES)
        u = pre_ref[:, at]
        n = u * lax.rsqrt(half_sums(u * u) / HD + EPSILON) * gain_ref[:1, at]
        turned = n * cosine + swapped_halves(n) * sine
        if block < q_blocks:
            q_ref[:, at] = (turned.astype(BF16).astype(F32) * (1.0 / math.sqrt(HD))).astype(BF16)
        else:
            kv_ref[0, :, pl.ds((block - q_blocks) * LANES, LANES)] = turned.astype(BF16)
    v_at = (q_blocks + k_blocks) * LANES
    kv_ref[1] = pre_ref[:, v_at : v_at + k_blocks * LANES].astype(BF16)


def head_prep(pre, cosine, sine, gains):
    rows = pre.shape[0]
    return pl.pallas_call(
        head_prep_kernel,
        out_shape=(
            jax.ShapeDtypeStruct((rows, HEADS * HD), BF16),
            jax.ShapeDtypeStruct((2, rows, KV_HEADS * HD), BF16),
        ),
        compiler_params=pltpu.CompilerParams(vmem_limit_bytes=VMEM_LIMIT),
        name="head_prep",
    )(pre, cosine, sine, gains)


def head_back_kernel(
    gq_ref, gkv_ref, one_ref, two_ref, pre_ref, cos_ref, sin_ref, gain_ref, out_ref, sums_ref
):
    q_blocks = HEADS * HD // LANES
    k_blocks = KV_HEADS * HD // LANES
    cosine, sine = cos_ref[...], sin_ref[...]
    sums_ref[...] = jnp.zeros_like(sums_ref)
    for block in range(q_blocks + k_blocks):
        at = pl.ds(block * LANES, LANES)
        if block < q_blocks:
            g = gq_ref[:, at]
        else:
            k_at = pl.ds((block - q_blocks) * LANES, LANES)
            g = gkv_ref[0, :, k_at] + one_ref[0, :, k_at].astype(F32) + two_ref[0, :, k_at].astype(F32)
        g = g * cosine - swapped_halves(g) * sine
        u = pre_ref[:, at]
        inverse = lax.rsqrt(half_sums(u * u) / HD + EPSILON)
        unit = u * inverse
        row = 0 if block < q_blocks else 1
        sums_ref[row : row + 1, :] += jnp.sum(unit * g, axis=0, keepdims=True)
        e = g * gain_ref[:1, at]
        out_ref[:, at] = (inverse * (e - unit * (half_sums(e * unit) / HD))).astype(BF16)
    v_at = (q_blocks + k_blocks) * LANES
    width = k_blocks * LANES
    out_ref[:, v_at : v_at + width] = (
        gkv_ref[1] + one_ref[1].astype(F32) + two_ref[1].astype(F32)
    ).astype(BF16)
    tail = out_ref.shape[1] - v_at - width
    out_ref[:, v_at + width :] = jnp.zeros((out_ref.shape[0], tail), BF16)


def head_back(gq, gkv, one, two, pre, cosine, sine, gains):
    rows, width = pre.shape
    return pl.pallas_call(
        head_back_kernel,
        out_shape=(
            jax.ShapeDtypeStruct((rows, width), BF16),
            jax.ShapeDtypeStruct((8, LANES), F32),
        ),
        compiler_params=pltpu.CompilerParams(vmem_limit_bytes=VMEM_LIMIT),
        name="head_back",
    )(gq, gkv, one, two, pre, cosine, sine, gains)


def stacked_heads(ref, pair, repeat):
    return jnp.concatenate(
        [ref[:, pl.ds((pair * repeat + h) * HD, HD)] for h in range(repeat)], axis=0
    )


def window_probs(q4, keys, rel, repeat):
    rows, span = rel.shape[0], keys.shape[0]
    scores = right_transposed(q4, keys).reshape(repeat, rows, span)
    key_at = lax.broadcasted_iota(jnp.int32, (rows, span), 1) - (span - rows)
    row_at = lax.broadcasted_iota(jnp.int32, (rows, span), 0)
    allowed = (key_at <= row_at) & (key_at >= rel)
    scores = jnp.where(allowed[None], scores, MASKED)
    top = jnp.max(scores, axis=-1, keepdims=True)
    raised = jnp.exp(scores - top)
    return raised * (1.0 / jnp.sum(raised, axis=-1, keepdims=True))


def attend_kernel(q_ref, two_ref, one_ref, kv_ref, rel_ref, out_ref):
    repeat = HEADS // KV_HEADS
    rows = q_ref.shape[0]
    rel = rel_ref[:, :1]
    keys = jnp.concatenate([two_ref[0], one_ref[0], kv_ref[0]], axis=0)
    vals = jnp.concatenate([two_ref[1], one_ref[1], kv_ref[1]], axis=0)
    for pair in range(2):
        part = slice(pair * HD, (pair + 1) * HD)
        q4 = stacked_heads(q_ref, pair, repeat)
        probs = window_probs(q4, keys[:, part], rel, repeat)
        low = probs.astype(BF16).reshape(repeat * rows, -1)
        mixed = product(low, vals[:, part])
        for h in range(repeat):
            out_ref[:, pl.ds((pair * repeat + h) * HD, HD)] = mixed[
                h * rows : (h + 1) * rows
            ].astype(BF16)


def attend_specs(rows):
    q_spec = pl.BlockSpec((rows, HEADS * HD // 3), lambda g: (0, g))
    kv_spec = pl.BlockSpec((2, rows, LANES), lambda g: (0, 0, g))
    rel_spec = pl.BlockSpec((rows, LANES), lambda g: (0, 0))
    return q_spec, kv_spec, rel_spec


def attend(q, two, one, kv, rel):
    rows = q.shape[0]
    q_spec, kv_spec, rel_spec = attend_specs(rows)
    return pl.pallas_call(
        attend_kernel,
        grid=(3,),
        in_specs=[q_spec, kv_spec, kv_spec, kv_spec, rel_spec],
        out_specs=q_spec,
        out_shape=jax.ShapeDtypeStruct((rows, HEADS * HD), BF16),
        compiler_params=pltpu.CompilerParams(vmem_limit_bytes=VMEM_LIMIT),
        name="attend",
    )(q, two, one, kv, rel)


def attend_back_kernel(
    q_ref, two_ref, one_ref, kv_ref, rel_ref, gm_ref, gq_ref, gtwo_ref, gone_ref, gkv_ref
):
    repeat = HEADS // KV_HEADS
    rows = q_ref.shape[0]
    rel = rel_ref[:, :1]
    keys = jnp.concatenate([two_ref[0], one_ref[0], kv_ref[0]], axis=0)
    vals = jnp.concatenate([two_ref[1], one_ref[1], kv_ref[1]], axis=0)
    key_grads, val_grads = [], []
    for pair in range(2):
        part = slice(pair * HD, (pair + 1) * HD)
        q4 = stacked_heads(q_ref, pair, repeat)
        gm4 = stacked_heads(gm_ref, pair, repeat)
        probs = window_probs(q4, keys[:, part], rel, repeat)
        grad_probs = right_transposed(gm4, vals[:, part]).reshape(probs.shape)
        weighted = jnp.sum(probs * grad_probs, axis=-1, keepdims=True)
        span = probs.shape[-1]
        gs = (probs * (grad_probs - weighted)).astype(BF16).reshape(repeat * rows, span)
        low = probs.astype(BF16).reshape(repeat * rows, span)
        gq = product(gs, keys[:, part]) * (1.0 / math.sqrt(HD))
        for h in range(repeat):
            gq_ref[:, pl.ds((pair * repeat + h) * HD, HD)] = gq[h * rows : (h + 1) * rows]
        key_grads.append(product(q4.T, gs).T)
        val_grads.append(product(gm4.T, low).T)
    for at, parts in ((0, key_grads), (1, val_grads)):
        both = jnp.concatenate(parts, axis=1)
        gtwo_ref[at] = both[:rows].astype(gtwo_ref.dtype)
        gone_ref[at] = both[rows : 2 * rows].astype(gone_ref.dtype)
        gkv_ref[at] = both[2 * rows :]


def attend_back(q, two, one, kv, rel, gm):
    rows = q.shape[0]
    q_spec, kv_spec, rel_spec = attend_specs(rows)
    return pl.pallas_call(
        attend_back_kernel,
        grid=(3,),
        in_specs=[q_spec, kv_spec, kv_spec, kv_spec, rel_spec, q_spec],
        out_specs=(q_spec, kv_spec, kv_spec, kv_spec),
        out_shape=(
            jax.ShapeDtypeStruct((rows, HEADS * HD), F32),
            jax.ShapeDtypeStruct((2, rows, KV_HEADS * HD), BF16),
            jax.ShapeDtypeStruct((2, rows, KV_HEADS * HD), BF16),
            jax.ShapeDtypeStruct((2, rows, KV_HEADS * HD), F32),
        ),
        compiler_params=pltpu.CompilerParams(vmem_limit_bytes=VMEM_LIMIT),
        name="attend_back",
    )(q, two, one, kv, rel, gm)


def feed_kernel(x_ref, both_ref, act_ref, slopes_ref):
    units = act_ref.shape[1]
    mixed = product(x_ref[...], both_ref[...])
    gate, up = mixed[:, :units], mixed[:, units:]
    sig = 1.0 / (1.0 + jnp.exp(-gate))
    silu = gate * sig
    act_ref[...] = (silu * up).astype(BF16)
    slopes_ref[:, :units] = (up * sig * (1.0 + gate * (1.0 - sig))).astype(BF16)
    slopes_ref[:, units:] = silu.astype(BF16)


def feed(x, both, tile):
    rows, width = x.shape
    units = both.shape[1] // 2
    return pl.pallas_call(
        feed_kernel,
        grid=(rows // tile,),
        in_specs=[
            pl.BlockSpec((tile, width), lambda i: (i, 0)),
            pl.BlockSpec((width, 2 * units), lambda i: (0, 0)),
        ],
        out_specs=[
            pl.BlockSpec((tile, units), lambda i: (i, 0)),
            pl.BlockSpec((tile, 2 * units), lambda i: (i, 0)),
        ],
        out_shape=[
            jax.ShapeDtypeStruct((rows, units), BF16),
            jax.ShapeDtypeStruct((rows, 2 * units), BF16),
        ],
        compiler_params=pltpu.CompilerParams(vmem_limit_bytes=VMEM_LIMIT),
        cost_estimate=pl.CostEstimate(
            flops=4 * rows * width * units,
            transcendentals=rows * units,
            bytes_accessed=2 * (rows * width + 2 * width * units + 3 * rows * units),
        ),
        name="feed",
    )(x, both)


def feed_back_kernel(x_ref, down_ref, slopes_ref, both_ref, grads_ref, own_ref, other_ref):
    step, steps = pl.program_id(0), pl.num_programs(0)
    lots = own_ref.shape[0]
    grad_act = right_transposed(x_ref[...], down_ref[...])
    both_act = jnp.concatenate([grad_act, grad_act], axis=1)
    grads = (both_act * slopes_ref[...].astype(F32)).astype(BF16)
    grads_ref[...] = grads
    total = right_transposed(grads, both_ref[...])
    total = total.reshape(lots, -1, total.shape[1])

    total = total.astype(BF16)

    @pl.when(step < steps // 2)
    def _():
        own_ref[...] = total

    @pl.when(step >= steps // 2)
    def _():
        other_ref[...] = total


def feed_back(upstream, down, slopes, both, lot, tile):
    rows, width = upstream.shape
    units = down.shape[0]
    steps = rows // tile
    lots = rows // lot
    per = tile // lot
    return pl.pallas_call(
        feed_back_kernel,
        grid=(steps,),
        in_specs=[
            pl.BlockSpec((tile, width), lambda i: (i, 0)),
            pl.BlockSpec((units, width), lambda i: (0, 0)),
            pl.BlockSpec((tile, 2 * units), lambda i: (i, 0)),
            pl.BlockSpec((width, 2 * units), lambda i: (0, 0)),
        ],
        out_specs=[
            pl.BlockSpec((tile, 2 * units), lambda i: (i, 0)),
            pl.BlockSpec((per, lot, width), lambda i: (jnp.minimum(i, steps // 2 - 1), 0, 0)),
            pl.BlockSpec((per, lot, width), lambda i: (jnp.maximum(i - steps // 2, 0), 0, 0)),
        ],
        out_shape=[
            jax.ShapeDtypeStruct((rows, 2 * units), BF16),
            jax.ShapeDtypeStruct((lots // 2, lot, width), BF16),
            jax.ShapeDtypeStruct((lots // 2, lot, width), BF16),
        ],
        compiler_params=pltpu.CompilerParams(vmem_limit_bytes=VMEM_LIMIT),
        cost_estimate=pl.CostEstimate(
            flops=6 * rows * width * units,
            transcendentals=0,
            bytes_accessed=2 * (3 * rows * width + 3 * width * units + 4 * rows * units),
        ),
        name="feed_back",
    )(upstream, down, slopes, both)


def lane_window(read, tiles, start):
    tile, shift = start // LANES, start % LANES
    first = read(min(max(tile, 0), tiles - 1))
    if shift == 0:
        return first
    second = read(min(max(tile + 1, 0), tiles - 1))
    lane = lax.broadcasted_iota(jnp.int32, first.shape, 1)
    return jnp.where(
        lane < LANES - shift,
        pltpu.roll(first, LANES - shift, 1),
        pltpu.roll(second, LANES - shift, 1),
    )


def lane_runs(target, runs, source_of):
    total = None
    for first, length, source in runs:
        low, high = max(first, target), min(first + length, target + LANES)
        if low >= high:
            continue
        window = source_of(source, target - first)
        lane = lax.broadcasted_iota(jnp.int32, window.shape, 1) + target
        kept = jnp.where((lane >= low) & (lane < high), window, 0.0)
        total = kept if total is None else total + kept
    return total


def split_kernel(far, unit, block, me_ref, gate_ref, up_ref, out_ref):
    units = far * block
    tiles = -(-gate_ref.shape[1] // LANES)
    for at, ref in ((0, gate_ref), (units, up_ref)):
        for part in range(8):
            runs = [(d * block, unit, (8 * d + part) * unit) for d in range(far)]

            def source_of(source, offset):
                read = lambda t: ref[:, t * LANES : (t + 1) * LANES].astype(F32)
                return lane_window(read, tiles, source + offset)

            for target in range(0, units, LANES):
                value = lane_runs(target, runs, source_of)
                to = pl.ds(at + target, LANES)
                turned = part // 2 % 2 * 4 + part // 4 * 2 + part % 2
                out_ref[turned ^ me_ref[0], :, to] = value.astype(BF16)


def split_units(gate, up, me, far, unit, block):
    return pl.pallas_call(
        functools.partial(split_kernel, far, unit, block),
        in_specs=[
            pl.BlockSpec(memory_space=pltpu.SMEM),
            pl.BlockSpec(memory_space=pltpu.VMEM),
            pl.BlockSpec(memory_space=pltpu.VMEM),
        ],
        out_shape=jax.ShapeDtypeStruct((8, gate.shape[0], 2 * far * block), BF16),
        compiler_params=pltpu.CompilerParams(vmem_limit_bytes=VMEM_LIMIT),
        name="split_units",
    )(me, gate, up)


def join_kernel(far, unit, block, me_ref, got_ref, gate_ref, up_ref):
    units = far * block
    tiles = got_ref.shape[2] // LANES
    runs = [
        ((8 * d + part) * unit, unit, (part, d * block)) for d in range(far) for part in range(8)
    ]
    for at, ref in ((0, gate_ref), (units, up_ref)):

        def source_of(source, offset):
            read = lambda t: got_ref[
                source[0] ^ me_ref[0], :, t * LANES : (t + 1) * LANES
            ].astype(F32)
            return lane_window(read, tiles, at + source[1] + offset)

        for target in range(0, ref.shape[1], LANES):
            ref[:, target : target + LANES] = lane_runs(target, runs, source_of)


def join_units(got, me, far, unit, block):
    out = jax.ShapeDtypeStruct((got.shape[1], 8 * far * unit), F32)
    return pl.pallas_call(
        functools.partial(join_kernel, far, unit, block),
        in_specs=[
            pl.BlockSpec(memory_space=pltpu.SMEM),
            pl.BlockSpec(memory_space=pltpu.VMEM),
        ],
        out_shape=[out, out],
        compiler_params=pltpu.CompilerParams(vmem_limit_bytes=VMEM_LIMIT),
        name="join_units",
    )(me, got)


def swap_pairs(size, bit):
    return [(i, i ^ bit) for i in range(size)]


def far_pairs(size, shift):
    far = size // 2
    return [(i, (i // 2 + shift) % far * 2 + i % 2) for i in range(size)]


def far_order(far):
    order = []
    for step in range(1, far // 2 + 1):
        order.append(step)
        if far - step != step:
            order.append(far - step)
    return order


def place_kernel(counts, slots, *refs):
    pieces, out, held, come, gone = refs[: len(counts)], *refs[len(counts) :]
    arrivals, departures = [], []
    for piece, count in zip(pieces, counts):
        for k in range(count):
            at = len(arrivals)
            arrivals.append(pltpu.make_async_copy(piece.at[k], held.at[at], come.at[at]))
            departures.append(pltpu.make_async_copy(held.at[at], out.at[slots[at]], gone.at[at]))
    for copy in arrivals:
        copy.start()
    for arrival, departure in zip(arrivals, departures):
        arrival.wait()
        departure.start()
    for copy in departures:
        copy.wait()


def place(pieces, slots):
    counts = [piece.shape[0] for piece in pieces]
    total = sum(counts)
    shape = (total,) + pieces[0].shape[1:]
    moved = 2 * math.prod(shape) * pieces[0].dtype.itemsize
    return pl.pallas_call(
        functools.partial(place_kernel, counts),
        in_specs=[pl.BlockSpec(memory_space=pltpu.SMEM)]
        + [pl.BlockSpec(memory_space=pl.ANY)] * len(pieces),
        out_specs=pl.BlockSpec(memory_space=pl.ANY),
        out_shape=jax.ShapeDtypeStruct(shape, pieces[0].dtype),
        scratch_shapes=[
            pltpu.VMEM(shape, pieces[0].dtype),
            pltpu.SemaphoreType.DMA((total,)),
            pltpu.SemaphoreType.DMA((total,)),
        ],
        compiler_params=pltpu.CompilerParams(vmem_limit_bytes=VMEM_LIMIT),
        cost_estimate=pl.CostEstimate(flops=0, transcendentals=0, bytes_accessed=moved),
        name="place",
    )(slots, *pieces)


def pick_kernel(counts, slots, source, *refs):
    outs, (held, come, gone) = refs[: len(counts)], refs[len(counts) :]
    arrivals, departures = [], []
    for out, count in zip(outs, counts):
        for k in range(count):
            at = len(arrivals)
            arrivals.append(pltpu.make_async_copy(source.at[slots[at]], held.at[at], come.at[at]))
            departures.append(pltpu.make_async_copy(held.at[at], out.at[k], gone.at[at]))
    for copy in arrivals:
        copy.start()
    for arrival, departure in zip(arrivals, departures):
        arrival.wait()
        departure.start()
    for copy in departures:
        copy.wait()


def pick(source, slots, counts):
    total = sum(counts)
    block = source.shape[1:]
    moved = 2 * total * math.prod(block) * source.dtype.itemsize
    return pl.pallas_call(
        functools.partial(pick_kernel, counts),
        in_specs=[pl.BlockSpec(memory_space=pltpu.SMEM), pl.BlockSpec(memory_space=pl.ANY)],
        out_specs=[pl.BlockSpec(memory_space=pl.ANY)] * len(counts),
        out_shape=[jax.ShapeDtypeStruct((n,) + block, source.dtype) for n in counts],
        scratch_shapes=[
            pltpu.VMEM((total,) + block, source.dtype),
            pltpu.SemaphoreType.DMA((total,)),
            pltpu.SemaphoreType.DMA((total,)),
        ],
        compiler_params=pltpu.CompilerParams(vmem_limit_bytes=VMEM_LIMIT),
        cost_estimate=pl.CostEstimate(flops=0, transcendentals=0, bytes_accessed=moved),
        name="pick",
    )(slots, source)


class Places:
    def __init__(self, dp_size):
        self.size, self.far = dp_size, dp_size // 2
        self.dp, self.member = lax.axis_index("dp"), lax.axis_index("fsdp")
        self.me = self.dp % 2 * 4 + self.member
        self.groups = [[2 * z + y for z in range(self.far)] for y in range(2)]

    def near_block(self, shift, near):
        return (self.dp // 2 + self.far + shift) % self.far * 2 + self.dp % 2 * (1 - near) + (
            1 - self.dp % 2
        ) * near

    def block(self, shift, near, member):
        return self.near_block(shift, near) * 4 + (self.member ^ member)


def far_gather(piece, places):
    held = {0: piece}
    for r in far_order(places.far):
        held[r] = lax.ppermute(piece, "dp", far_pairs(places.size, r))
    return held


def plane_first(mine, places):
    half = mine.shape[0] // 2
    first, second = mine[:half], mine[half:]
    near, across = near_swap(first, places), member_swap(second, 2)
    return jnp.concatenate([first, near]), jnp.concatenate([second, across])


def plane_second(first, second, places):
    across, near = member_swap(first, 2), near_swap(second, places)
    return jnp.concatenate([first, across]), jnp.concatenate([second, near])


def plane_last(first, second, sends, places):
    half = places.far // 2
    lots = [0, *sends][:half], [0, *sends][half:]
    slots = [
        places.block(-r, inner, 2 * outer + core)
        for core in (0, 1)
        for outer in (0, 1)
        for inner in (0, 1)
        for r in lots[0]
    ]
    later = [
        places.block(-r, outer, 2 * inner + core)
        for core in (0, 1)
        for outer in (0, 1)
        for inner in (0, 1)
        for r in lots[1]
    ]
    blocks = [first, member_swap(first, 1), second, member_swap(second, 1)]
    return place(blocks, jnp.stack(slots + later))


def gated(value, gate):
    return value if gate is None else lax.optimization_barrier((value, gate))[0]


def exchange_chips(parts):
    return jnp.stack([parts[:4], member_swap(parts[4:], 2)])


def exchange_near(parts, places):
    return jnp.stack([parts[:, :2], near_swap(parts[:, 2:], places)])


def exchange_units(parts, places):
    beside = member_swap(parts[:, :, 1], 1)
    own = parts[:, :, 0]
    blocks = [own.reshape(4, *own.shape[2:]), beside.reshape(4, *own.shape[2:])]
    slots = [
        places.me ^ (4 * near + 2 * chip + core)
        for core in (0, 1)
        for near in (0, 1)
        for chip in (0, 1)
    ]
    return place(blocks, jnp.stack(slots))


def return_core(blocks, places):
    slots = [
        places.me ^ (4 * near + 2 * chip + core)
        for core in (1, 0)
        for chip in (1, 0)
        for near in (1, 0)
    ]
    other, own = pick(blocks, jnp.stack(slots), [4, 4])
    return jnp.stack([own, member_swap(other, 1)])


def return_units(held, places):
    across = member_swap(held[:, :2], 2)
    held = jnp.stack([held[:, 2:], across])
    near = near_swap(held[:, :, 0], places)
    held = jnp.stack([held[:, :, 1], near])
    return held.reshape(8, *held.shape[3:])


def assemble_kernel(*refs):
    pieces, (out, held, come, gone) = refs[:-4], refs[-4:]
    half = out.shape[2] // 2
    arrivals, departures = [], []
    for k, piece in enumerate(pieces):
        core, at = k // 5, k % 5
        columns = pl.ds(0, 2 * half) if at < 3 else pl.ds((at - 3) * half, half)
        spot = (core * 4 + min(at, 3), slice(None), columns)
        arrivals.append(pltpu.make_async_copy(piece, held.at[spot], come.at[k]))
        departures.append(pltpu.make_async_copy(held.at[spot], out.at[spot], gone.at[k]))
    for copy in arrivals:
        copy.start()
    for arrival, departure in zip(arrivals, departures):
        arrival.wait()
        departure.start()
    for copy in departures:
        copy.wait()


def assemble(pieces):
    rows, width = pieces[0].shape
    shape = (8, rows, width)
    return pl.pallas_call(
        assemble_kernel,
        in_specs=[pl.BlockSpec(memory_space=pl.ANY)] * len(pieces),
        out_specs=pl.BlockSpec(memory_space=pl.ANY),
        out_shape=jax.ShapeDtypeStruct(shape, BF16),
        scratch_shapes=[
            pltpu.VMEM(shape, BF16),
            pltpu.SemaphoreType.DMA((len(pieces),)),
            pltpu.SemaphoreType.DMA((len(pieces),)),
        ],
        compiler_params=pltpu.CompilerParams(vmem_limit_bytes=VMEM_LIMIT),
        cost_estimate=pl.CostEstimate(
            flops=0, transcendentals=0, bytes_accessed=4 * math.prod(shape)
        ),
        name="assemble",
    )(*pieces)


def gather_first(rows, places):
    return rows, member_swap(rows, 2), near_swap(rows, places)


def gather_second(rows, across, near, places):
    half = rows.shape[1] // 2
    left = near_swap(across[:, :half], places)
    right = member_swap(near[:, half:], 2)
    return rows, across, near, left, right


def gather_last(*pieces):
    out = assemble([*pieces, *(member_swap(piece, 1) for piece in pieces)])
    return out.reshape(-1, out.shape[2])


def merge_kernel(own_ref, got_ref, near_ref, across_ref, left_ref, right_ref):
    half = own_ref.shape[2] // 2
    left, right = pl.ds(0, half), pl.ds(half, half)

    def total(lot, columns):
        return own_ref[lot, :, columns].astype(F32) + got_ref[lot, :, columns].astype(F32)

    for k, lot in enumerate((2, 3)):
        near_ref[k] = total(lot, left).astype(BF16)
    for k, lot in enumerate((1, 3)):
        across_ref[k] = total(lot, right).astype(BF16)
    for k, lot in enumerate((0, 1)):
        left_ref[k] = total(lot, left)
    for k, lot in enumerate((0, 2)):
        right_ref[k] = total(lot, right)


def merge(own, got):
    shape = (2, own.shape[1], own.shape[2] // 2)
    low, wide = jax.ShapeDtypeStruct(shape, BF16), jax.ShapeDtypeStruct(shape, F32)
    return pl.pallas_call(
        merge_kernel,
        out_shape=[low, low, wide, wide],
        compiler_params=pltpu.CompilerParams(vmem_limit_bytes=VMEM_LIMIT),
        cost_estimate=pl.CostEstimate(
            flops=own.size, transcendentals=0, bytes_accessed=7 * own.size
        ),
        name="merge",
    )(own, got)


def scatter_first(own, other, places):
    near, across, left, right = merge(own, member_swap(other, 1))
    near, across = near_swap(near, places), member_swap(across, 2)
    return left, near, right, across


def scatter_second(left, near, right, across, places):
    left_out = (left[1] + near[1].astype(F32)).astype(BF16)
    right_out = (right[1] + across[1].astype(F32)).astype(BF16)
    left_got, right_got = member_swap(left_out, 2), near_swap(right_out, places)
    left = left[0] + near[0].astype(F32) + left_got.astype(F32)
    right = right[0] + across[0].astype(F32) + right_got.astype(F32)
    return jnp.concatenate([left, right], axis=1)


def split_order(far):
    order = far_order(far) + [0]
    return order[: far // 2], order[far // 2 :]


def far_parts(term, places, cut=1):
    order = sum(split_order(places.far), [])
    slots = [(places.dp // 2 + r) % places.far * cut + k for r in order for k in range(cut)]
    return pick(term, jnp.stack(slots), [1] * len(slots))


def whole_parts(term, places):
    lots = split_order(places.far)
    slots = []
    for core in (1, 0):
        slots += [places.block(r, n, core + c) for c in (2, 0) for n in (1, 0) for r in lots[0]]
        slots += [places.block(r, n, core + c) for n in (1, 0) for c in (2, 0) for r in lots[1]]
    return pick(term, jnp.stack(slots), [4 * places.far] * 2)


def near_swap(value, places):
    return lax.ppermute(value, "dp", swap_pairs(places.size, 1))


def member_swap(value, bit):
    return lax.ppermute(value, "fsdp", swap_pairs(4, bit))


def added(own, got):
    return (own.astype(F32) + got.astype(F32)).astype(BF16)


def added_parts(own, got, cut):
    return added(own[:cut], got[:cut]), added(own[cut:], got[cut:])


def far_sends(lot, blocks, places):
    return [
        lax.ppermute(blocks[k], "dp", far_pairs(places.size, r)) if r else blocks[k]
        for k, r in enumerate(lot)
    ]


def total_of(parts):
    total = parts[0].astype(F32)
    for part in parts[1:]:
        total = total + part.astype(F32)
    return total


class Rounds:
    def __init__(self):
        self.results = ()

    def enter(self, *values):
        kept = lax.optimization_barrier((values, self.results))[0]
        self.results = ()
        return kept

    def leave(self, *values):
        self.results += values
        return list(values) if len(values) > 1 else values[0]


def sum_steps(value, axis, size, bit=1, end=None):
    while bit < (end or size):
        value = value + lax.ppermute(value, axis, swap_pairs(size, bit))
        bit *= 2
    return value


def local(
    tokens,
    cotangent,
    seq_lengths,
    deal_order,
    attn_gain,
    w_query,
    w_key,
    w_value,
    q_gain,
    k_gain,
    w_out,
    ffn_gain,
    w_gate,
    w_up,
    w_down,
):
    rows, width = tokens.shape
    dp_size = lax.axis_size("dp")
    shard = w_gate.shape[0]
    ff_rows = w_down.shape[0]
    member = lax.axis_index("fsdp")

    lengths = seq_lengths[0]
    slots = jnp.arange(lengths.shape[0], dtype=jnp.int32)
    starts = jnp.sum(jnp.where(slots[None, :] < slots[:, None], lengths[None, :], 0), axis=1)
    row_ids = member * rows + jnp.arange(rows, dtype=jnp.int32)
    begun = starts[None, :] <= row_ids[:, None]
    row_start = jnp.max(jnp.where(begun, starts[None, :], 0), axis=1)
    row_place = row_ids - row_start
    rel = jnp.broadcast_to((row_start - member * rows)[:, None], (rows, LANES))
    frequency = 10000.0 ** (-2.0 * jnp.arange(HD // 2, dtype=F32) / HD)
    angles = row_place.astype(F32)[:, None] * frequency[None, :]
    cosine, sine = jnp.cos(angles), jnp.sin(angles)
    cosine = jnp.concatenate([cosine] * 4, axis=1)
    sine = jnp.concatenate([-sine, sine, -sine, sine], axis=1)
    head_gains = jnp.concatenate([jnp.tile(q_gain, HEADS), jnp.tile(k_gain, KV_HEADS)])
    head_gains = jnp.broadcast_to(head_gains.astype(F32)[None, :], (8, head_gains.shape[0]))

    places = Places(dp_size)
    gain_columns = jnp.pad(
        jnp.stack([attn_gain, ffn_gain], axis=1), ((0, 0), (0, LANES - 2))
    )
    w_qkv = jnp.concatenate([w_query, w_key, w_value, gain_columns], axis=1)

    far = places.far
    ff_block = -(-ff_rows * far // LANES) * LANES // far
    ff_width = far * ff_block
    me = places.me.reshape(1)
    turned = places.member // 2 * 4 + places.dp % 2 * 2 + places.member % 2
    units = split_units(w_gate, w_up, turned.reshape(1), far, ff_rows, ff_block)
    sends = far_order(far)
    gather_far = functools.partial(
        lax.all_gather, axis_name="dp", axis=0, tiled=True, axis_index_groups=places.groups
    )

    rounds = Rounds()
    qkv_held = far_gather(w_qkv, places)
    qkv_mine = rounds.leave(jnp.stack([qkv_held[r] for r in [0] + sends]))
    units = rounds.leave(exchange_near(exchange_chips(units), places))

    qkv_mine, late_out, units, down_piece = rounds.enter(qkv_mine, w_out, units, w_down)
    out_held = far_gather(late_out, places)
    out_mine = rounds.leave(jnp.stack([out_held[r] for r in [0] + sends]))
    qkv_a, qkv_b = plane_first(qkv_mine, places)
    qkv_a, qkv_b = rounds.leave(qkv_a, qkv_b)
    down_piece = jnp.pad(down_piece, ((0, ff_block - ff_rows), (0, 0)))
    my_down = gather_far(down_piece)
    both_piece = rounds.leave(exchange_units(units, places))

    qkv_a, qkv_b, out_mine, both_piece = rounds.enter(qkv_a, qkv_b, out_mine, both_piece)
    qkv_a, qkv_b = rounds.leave(*plane_second(qkv_a, qkv_b, places))
    out_a, out_b = rounds.leave(*plane_first(out_mine, places))
    my_both = gather_far(both_piece.reshape(8 * shard, 2 * ff_width))

    qkv_a, qkv_b, out_a, out_b = rounds.enter(qkv_a, qkv_b, out_a, out_b)
    full_qkv = plane_last(qkv_a, qkv_b, sends, places).reshape(width, -1)
    out_a, out_b = plane_second(*gated((out_a, out_b), full_qkv), places)
    full_qkv = gated(full_qkv, my_down)

    gain_table = full_qkv[:, full_qkv.shape[1] - LANES :]
    pick = (
        lax.broadcasted_iota(jnp.int32, (8, LANES), 0)
        == lax.broadcasted_iota(jnp.int32, (8, LANES), 1)
    ).astype(BF16)
    gain_rows = right_transposed(pick, gain_table)
    attn_row, ffn_row = gain_rows[0:1], gain_rows[1:2]
    x = tokens.astype(F32)
    x_inverse = lax.rsqrt(jnp.mean(x * x, axis=-1, keepdims=True) + EPSILON)
    normed = (x * x_inverse * attn_row).astype(BF16)
    pre = product(normed, full_qkv)
    queries, kv = head_prep(pre, cosine, sine, head_gains)
    ahead_one = [(i, i + 1) for i in range(3)]
    ahead_two = [(i, i + 2) for i in range(2)]
    kv = gated(kv, (out_a, out_b))
    kv_one = lax.ppermute(kv, "fsdp", ahead_one)
    kv_two = lax.ppermute(kv, "fsdp", ahead_two)
    pieces = gather_first(gated(cotangent, kv_two), places)
    mixed = attend(queries, kv_two, kv_one, kv, rel)
    out_a, out_b, _ = gated((out_a, out_b, kv_one), kv_two)
    full_out = plane_last(out_a, out_b, sends, places).reshape(-1, width)
    pieces = gather_second(*gated(pieces, full_out), places)
    hidden = x + product(mixed, full_out)
    h_inverse = lax.rsqrt(jnp.mean(hidden * hidden, axis=-1, keepdims=True) + EPSILON)
    ffn_mine = (hidden * h_inverse * ffn_row).astype(BF16)

    ffn_pieces = gather_first(gated(ffn_mine, pieces), places)
    upstream = gather_last(*pieces)
    ffn_low = gather_last(*gather_second(*gated(ffn_pieces, upstream), places))
    tile = 2 * rows
    act_low, slopes = feed(ffn_low, my_both, tile)
    order = sum(split_order(far), [])

    def parts_of(left, right, cut=1):
        term = left_transposed(left, right).astype(BF16)
        return far_parts(term.reshape(far * cut, -1, term.shape[1]), places, cut)

    def far_sent(blocks, which, cut=1):
        return [
            lax.ppermute(blocks[k], "dp", far_pairs(dp_size, order[k // cut]))
            if order[k // cut]
            else blocks[k]
            for k in which
        ]

    first, second = range(far // 2), range(far // 2, far)
    sent = 2 * (far - 1)
    cut_a = sent // 2
    rounds = Rounds()

    *d_blocks, upstream, my_down, slopes = rounds.enter(
        *parts_of(act_low, upstream), upstream, my_down, slopes
    )
    d_first, d_second = far_sent(d_blocks, first), far_sent(d_blocks, second)
    rounds.leave(*d_first)
    grads, ffn_own, ffn_other = rounds.leave(
        *feed_back(upstream, my_down, slopes, my_both, rows, tile)
    )

    grads, ffn_own, ffn_other, act_low = rounds.enter(grads, ffn_own, ffn_other, act_low)
    grad_ffn = scatter_second(*scatter_first(ffn_own, ffn_other, places), places)
    grad_ffn = rounds.leave(grad_ffn)
    u_blocks = rounds.leave(*parts_of(ffn_low, grads, 2))
    out_own, out_other = rounds.leave(
        *(
            product(part, my_down).astype(BF16).reshape(4, rows, width)
            for part in (act_low[: 4 * rows], act_low[4 * rows :])
        )
    )
    rounds.leave(*d_second)

    *u_blocks, grad_ffn, out_own, out_other = rounds.enter(
        *u_blocks, grad_ffn, out_own, out_other
    )
    u_got = rounds.leave(*far_sent(u_blocks, range(cut_a), 2))
    out_steps = rounds.leave(*scatter_first(out_own, out_other, places))
    e = grad_ffn * ffn_row
    slope = jnp.mean(hidden * e, axis=-1, keepdims=True)
    grad_hidden = cotangent.astype(F32) + h_inverse * e - hidden * (h_inverse**3 * slope)
    ffn_gain_term = jnp.sum(grad_ffn * hidden * h_inverse, axis=0)
    grad_hidden_low = grad_hidden.astype(BF16)
    grad_mixed = right_transposed(grad_hidden_low, full_out).astype(BF16)
    gq, gkv_two, gkv_one, gkv = rounds.leave(
        *attend_back(queries, kv_two, kv_one, kv, rel, grad_mixed)
    )
    term_out = left_transposed(mixed, grad_hidden_low).astype(BF16)
    term_out = rounds.leave(term_out)
    down_grad = rounds.leave(total_of(d_first + d_second)[0, :ff_rows])

    u_blocks[sent - 2], gkv_one, gkv_two, gq, gkv, term_out, *out_steps = rounds.enter(
        u_blocks[sent - 2], gkv_one, gkv_two, gq, gkv, term_out, *out_steps
    )
    out_grad = lax.psum_scatter(term_out, BOTH, scatter_dimension=0, tiled=True).astype(F32)
    u_near = far_sent(u_blocks, [sent - 2], 2)
    rounds.leave(*u_near)
    got_one = lax.ppermute(gkv_one, "fsdp", [(b, a) for a, b in ahead_one])
    got_two = lax.ppermute(gkv_two, "fsdp", [(b, a) for a, b in ahead_two])
    output = rounds.leave((hidden + scatter_second(*out_steps, places)).astype(BF16))
    half = 2 * far
    quarter, eighth = half // 2, half // 4
    grad_pre, head_sums = head_back(gq, gkv, got_one, got_two, pre, cosine, sine, head_gains)
    term_qkv = left_transposed(normed, grad_pre).astype(BF16)
    q_other, q_own = rounds.leave(
        *whole_parts(term_qkv.reshape(4 * dp_size, shard, -1), places)
    )
    grad_pre = rounds.leave(grad_pre)

    u_blocks[cut_a], q_other, q_own, grad_pre = rounds.enter(
        u_blocks[cut_a], q_other, q_own, grad_pre
    )
    q_got = rounds.leave(member_swap(q_other, 1))
    middle = range(cut_a, sent - 2)
    u_middle = rounds.leave(far_sent(u_blocks, middle, 2))
    grad_normed = rounds.leave(right_transposed(grad_pre, full_qkv))

    a_out, q_a = added_parts(q_own[:half], q_got[:half], quarter)
    b_out, q_b = added_parts(q_own[half:], q_got[half:], quarter)
    u_blocks[sent - 1], a_out, b_out, grad_normed = rounds.enter(
        u_blocks[sent - 1], a_out, b_out, grad_normed
    )
    last = range(sent - 1, sent + 2)
    u_last = rounds.leave(far_sent(u_blocks, last, 2))
    a_got = rounds.leave(member_swap(a_out, 2))
    b_got = rounds.leave(near_swap(b_out, places))
    e = grad_normed * attn_row
    slope = jnp.mean(x * e, axis=-1, keepdims=True)
    input_grad = grad_hidden + x_inverse * e - x * (x_inverse**3 * slope)
    input_grad = rounds.leave(input_grad.astype(BF16))
    attn_gain_term = jnp.sum(grad_normed * x * x_inverse, axis=0)
    small = jnp.concatenate([attn_gain_term, ffn_gain_term, head_sums.reshape(-1)])
    small = rounds.leave(small.reshape(-1, LANES))

    u_got = dict(enumerate(u_got)) | {sent - 2: u_near[0]}
    u_got |= dict(zip(middle, u_middle)) | dict(zip(last, u_last))

    a_out, q_a = added_parts(q_a, a_got, eighth)
    b_out, q_b = added_parts(q_b, b_got, eighth)
    unit_sum = jnp.concatenate(
        [total_of([u_got[2 * r + k] for r in range(far)]) for k in range(2)], axis=1
    )
    unit_sum = unit_sum.astype(BF16).reshape(8, shard, 2 * ff_width)
    a_out, b_out, small, unit_sum = rounds.enter(a_out, b_out, small, unit_sum)
    a_got = rounds.leave(near_swap(a_out, places))
    b_got = rounds.leave(member_swap(b_out, 2))
    small = sum_steps(small, "fsdp", 4, 1, 2)
    small = rounds.leave(sum_steps(small, "dp", dp_size, 2))
    units = rounds.leave(return_core(unit_sum, places))

    q_a, q_b = added(q_a, a_got), added(q_b, b_got)
    q_a, q_b, small, units = rounds.enter(q_a, q_b, small, units)
    q_parts = far_sends(order[: far // 2], q_a, places) + far_sends(order[far // 2 :], q_b, places)
    unit_all = return_units(units, places)
    small = sum_steps(sum_steps(small, "fsdp", 4, 2), "dp", dp_size, 1, 2).reshape(-1)
    qkv_grad = total_of(q_parts)
    unit_all = gated(unit_all, out_grad)
    gate_grad, up_grad = join_units(unit_all, me, far, ff_rows, ff_block)

    mine = (lax.axis_index("dp") * 4 + member) * shard
    attn_gain_grad = lax.dynamic_slice(small, (mine,), (shard,))
    ffn_gain_grad = lax.dynamic_slice(small, (width + mine,), (shard,))
    head_total = small[2 * width : 2 * width + 2 * LANES].reshape(2, 2, HD).sum(axis=1)

    q_end = HEADS * HD
    k_end = q_end + KV_HEADS * HD
    v_end = k_end + KV_HEADS * HD
    return (
        output,
        input_grad.astype(BF16),
        attn_gain_grad,
        qkv_grad[:, :q_end],
        qkv_grad[:, q_end:k_end],
        qkv_grad[:, k_end:v_end],
        head_total[0],
        head_total[1],
        out_grad,
        ffn_gain_grad,
        gate_grad,
        up_grad,
        down_grad,
    )


def solution(mesh):
    rows = P(BOTH, None)
    vector = P(BOTH)
    in_specs = (
        rows,
        rows,
        P("dp", None),
        P("dp", None),
        vector,
        rows,
        rows,
        rows,
        P(),
        P(),
        rows,
        vector,
        rows,
        rows,
        rows,
    )
    out_specs = (rows, rows, vector, rows, rows, rows, P(), P(), rows, vector, rows, rows, rows)
    return jax.shard_map(local, mesh=mesh, in_specs=in_specs, out_specs=out_specs, check_vma=False)
```
